32 devices in a mesh: lat: 4 (over z), lon: 8 (over y, x, core).
Axes of the slice: x: 2, y: 2, z: 4, core: 2. Of those that a mesh axis runs over, the one named last changes fastest.
Arguments:
- fields: float32 [5, 960, 2880], P(None, 'lat', 'lon'), may hold values from -6 to 6
- east_courant: float32 [960, 2880], P('lat', 'lon'), may hold values from -0.4 to 0.4
- north_courant: float32 [960, 2880], P('lat', 'lon'), may hold values from -0.4 to 0.4
- cutoff: int32 [960], replicated, may hold values from 1 to 1439
- damping: float32 [960], replicated, may hold values from 0.05 to 0.5
- ship_rows: int32 [4, 4, 60], replicated, may hold values from -1 to 239, as said below
Outputs:
- updated: float32 [5, 960, 2880], P(None, 'lat', 'lon')
The draws below stay inside these ranges and needn't reach their ends.
Inputs may be any that keep to these rules, and one draw needn't show every extreme that they name: ship_rows[s, d, j] is a row of band s (0 to 239) whose filter is computed by band d, or -1 for an empty slot; no row is listed twice; every row within 240 rows of either pole is listed, no row farther than 360 from both poles is listed, and rows between are listed or not, so that bands 0 and 3 are covered whole; a band's listed rows fill the slots of its destinations in full except the last destination it uses, so band 0 fills 60 slots to some band.
All inputs are finite; a program needn't handle non-finite values.
Results may differ from the reference program's by a relative error of at most 0.0003.
Values sent between devices are 32-bit elements; how exact they have to be, the bound alone decides.
A program may use at most 256 MiB of HBM per device.

```python
import math
import jax
import jax.numpy as jnp

CHANNELS = 5
NLON = 2880
ROWS_DEV = 240
BANDS = 4
NLAT = 960
CAP = 60


def draw_ship_rows(key, part):
    key = jax.random.fold_in(key, 7919)
    key_zone, key_order, key_dest = jax.random.split(key, 3)
    lat_count = ROWS_DEV * BANDS
    lower_bound = ROWS_DEV
    upper_bound = max(lat_count // 4, ROWS_DEV + ROWS_DEV // 2)
    global_rows = jnp.arange(BANDS, dtype=jnp.int32)[:, None] * ROWS_DEV + jnp.arange(ROWS_DEV, dtype=jnp.int32)[None, :]
    pole_distance = jnp.minimum(global_rows, lat_count - 1 - global_rows)
    coin = jax.random.randint(key_zone, (BANDS, ROWS_DEV), 0, 2).astype(jnp.int32)
    listed = jnp.where(pole_distance < lower_bound, 1, jnp.where(pole_distance < upper_bound, coin, 0)).astype(jnp.int32)
    scores = jax.vmap(lambda subkey: jax.random.permutation(subkey, ROWS_DEV))(jax.random.split(key_order, BANDS)).astype(jnp.int32)
    sort_keys = (1 - listed) * ROWS_DEV + scores
    ordering = jnp.argsort(sort_keys, axis=1, stable=True).astype(jnp.int32)
    listed_count = jnp.sum(listed, axis=1)
    destinations = jax.vmap(lambda subkey: jax.random.permutation(subkey, BANDS))(jax.random.split(key_dest, BANDS)).astype(jnp.int32)
    positions = jnp.arange(ROWS_DEV, dtype=jnp.int32)
    target_band = destinations[:, positions // CAP]
    target_slot = jnp.broadcast_to(positions % CAP, (BANDS, ROWS_DEV))
    entries = jnp.where(positions[None, :] < listed_count[:, None], ordering, -1).astype(jnp.int32)
    source_band = jnp.broadcast_to(jnp.arange(BANDS, dtype=jnp.int32)[:, None], (BANDS, ROWS_DEV))
    empty_lists = jnp.full((BANDS, BANDS, CAP), -1, jnp.int32)
    return empty_lists.at[source_band, target_band, target_slot].set(entries)


def place_ends(drawn, rng, low, top_value):
    extent = drawn.shape
    index_at = [jax.random.randint(jax.random.fold_in(rng, axis), (), 0, extent[axis]) for axis in range(len(extent))]
    drawn = drawn.at[tuple(index_at)].set(low)
    longest = extent.index(max(extent))
    index_at[longest] = (index_at[longest] + 1) % extent[longest]
    return drawn.at[tuple(index_at)].set(top_value)


def levels(stream_key, dims, pieces, low, largest):
    def one(axis_at, parts):
        draws = jax.random.uniform(jax.random.fold_in(jax.random.fold_in(stream_key, 6), axis_at), (parts,), jnp.float32, low / len(pieces), largest / len(pieces))
        return jnp.repeat(jnp.exp(draws), dims[axis_at] // parts).reshape((-1,) + (1,) * (len(dims) - axis_at - 1))

    factor_of = one(*pieces[0])
    for cut in pieces[1:]:
        factor_of = factor_of * one(*cut)
    return factor_of


def gaussian(own_key, extent, deviation, limit, cuts=(), kind=jnp.bfloat16):
    array = deviation * jax.random.normal(own_key, extent, jnp.float32)
    if cuts:
        array = array * levels(own_key, extent, cuts, -0.22, 0.18)
    return jnp.clip(array, -limit, limit).astype(kind)


def setup_inputs(seed: int = 0) -> dict:
    keys = jax.random.split(jax.random.key(seed), 7)
    return {
        "fields": gaussian(keys[0], (CHANNELS, NLAT, NLON), 1.0, 6.0, ((1, 4), (2, 8)), jnp.float32),
        "east_courant": jnp.clip(jax.random.uniform(keys[1], (NLAT, NLON), jnp.float32, -0.4, 0.4) * levels(keys[1], (NLAT, NLON), ((0, 4), (1, 8)), -0.4, 0.0), -0.4, 0.4),
        "north_courant": jnp.clip(jax.random.uniform(keys[2], (NLAT, NLON), jnp.float32, -0.4, 0.4) * levels(keys[2], (NLAT, NLON), ((0, 4), (1, 8)), -0.4, 0.0), -0.4, 0.4),
        "cutoff": place_ends(jax.random.randint(keys[3], (NLAT,), 1, NLON // 2), jax.random.fold_in(keys[3], 1), 1, (NLON // 2) - 1).astype(jnp.int32),
        "damping": jnp.clip(jnp.exp(jax.random.uniform(keys[4], (NLAT,), jnp.float32, math.log(0.05), math.log(0.5))), 0.05, 0.5),
        "ship_rows": draw_ship_rows(jax.random.fold_in(keys[6], 71), 0),
    }


def reference(fields, east_courant, north_courant, cutoff, damping, ship_rows):
    lat_count = fields.shape[1]
    lon_count = fields.shape[2]
    east_cells = jnp.roll(fields, -1, axis=2)
    west_cells = jnp.roll(fields, 1, axis=2)
    west_courant = jnp.roll(east_courant, 1, axis=1)
    east_flux = east_courant * jnp.where(east_courant > 0, fields, east_cells)
    west_flux = west_courant * jnp.where(west_courant > 0, west_cells, fields)
    zero_row = jnp.zeros_like(fields[:, :1, :])
    north_cells = jnp.concatenate([fields[:, 1:, :], zero_row], axis=1)
    south_cells = jnp.concatenate([zero_row, fields[:, :-1, :]], axis=1)
    south_courant = jnp.concatenate([jnp.zeros_like(north_courant[:1]), north_courant[:-1]], axis=0)
    global_rows = jnp.arange(lat_count, dtype=jnp.int32)
    latitudes = global_rows.astype(jnp.float32)
    face_n = jnp.sin((latitudes + 1.0) * (math.pi / lat_count))
    face_s = jnp.sin(latitudes * (math.pi / lat_count))
    centre = jnp.sin((latitudes + 0.5) * (math.pi / lat_count))
    north_mask = (global_rows < lat_count - 1).astype(jnp.float32)
    south_mask = (global_rows > 0).astype(jnp.float32)
    north_flux = north_courant * jnp.where(north_courant > 0, fields, north_cells) * (face_n * north_mask)[:, None]
    south_flux = south_courant * jnp.where(south_courant > 0, south_cells, fields) * (face_s * south_mask)[:, None]
    advected = fields - (east_flux - west_flux) - (north_flux - south_flux) / centre[:, None]

    sources = jnp.arange(BANDS, dtype=jnp.int32)[:, None, None]
    listed_rows = sources * ROWS_DEV + ship_rows
    placement = jnp.where(ship_rows >= 0, listed_rows, NLAT).reshape(-1).astype(jnp.int32)
    marked = jnp.zeros((NLAT,), jnp.int32).at[placement].set(1, mode="drop")

    spectrum = jnp.fft.rfft(advected, axis=2)
    wavenumbers = jnp.arange(lon_count // 2 + 1, dtype=jnp.int32)
    response = jnp.where(wavenumbers[None, :] <= cutoff[:, None], jnp.ones_like(damping)[:, None], damping[:, None])
    filtered = jnp.fft.irfft(spectrum * response[None, :, :], n=lon_count, axis=2).astype(jnp.float32)
    return jnp.where(marked[None, :, None] > 0, filtered, advected)
```

```python
import functools
import math

import jax
import jax.numpy as jnp
import numpy as np
from jax import lax
from jax.experimental import pallas as pl
from jax.experimental.pallas import tpu as pltpu
from jax.sharding import PartitionSpec as P

MESH = pl.DeviceIdType.MESH
BF16 = jnp.bfloat16
F32 = jnp.float32
BLOCK = 16
SIN = (3.14159265357, -5.1677127773, 2.55016398193, -0.59926406421, 0.0821440508123,
       -0.00736648693826, 0.000461586773619, -1.89446619668e-05)
COS = (0.999999999886, -4.93480218586, 4.05871181724, -1.33526028616, 0.235320825531,
       -0.0257858087643, 0.00190432895602, -8.86909350679e-05)


def ceil_to(value, unit):
    return -(-value // unit) * unit


def elliptic_dn(fraction, complement):
    a, b = [1.0], [math.sqrt(complement)]
    c = [math.sqrt(1.0 - complement)]
    for _ in range(12):
        x, y = a[-1], b[-1]
        a.append((x + y) / 2)
        b.append(math.sqrt(x * y))
        c.append((x - y) / 2)
    phi = 2.0 ** 12 * fraction * math.pi / 2
    for i in range(12, 0, -1):
        phi = (phi + math.asin(max(-1.0, min(1.0, c[i] * math.sin(phi) / a[i])))) / 2
    return math.sqrt(1.0 - (1.0 - complement) * math.sin(phi) ** 2)


def zolotarev(a, b, c, d, unit):
    gamma = (c - a) * (d - b) / ((c - b) * (d - a))
    count = ceil_to(math.ceil(math.log(16 * gamma) * math.log(4 * 2.0 ** 24) / math.pi ** 2), unit)
    alpha = 2 * gamma - 1 + 2 * math.sqrt(gamma * gamma - gamma)

    def moebius(z):
        q = (z + alp) * -2.0 / ((z - 1.0) * (alp - 1.0)) * (b - a) / (b - c)
        return (a - q * c) / (1.0 - q)

    alp = alpha
    values = [alp * elliptic_dn((i + 0.5) / count, 1.0 / alp ** 2) for i in range(count)]
    return [moebius(-v) for v in values], [moebius(v) for v in values]


def factor(total, length, low, high, pole, unit):
    step = math.pi / total
    ref = pole - total / 2

    def turn(n):
        return (n - ref + total / 2) % total - total / 2

    def tangent(n):
        return math.tan(step * turn(n))

    here, there = (tangent(0), tangent(length - 1)), (tangent(low), tangent(high))
    if here[0] < there[0]:
        y, x = zolotarev(*here, *there, unit)
    else:
        x, y = zolotarev(*there, *here, unit)
    cell = np.array([tangent(m) for m in range(length)])
    cosine = np.array([math.cos(step * turn(m)) for m in range(length)])
    rows, nodes = [], []
    for k in range(len(y)):
        angle = math.atan(y[k])
        value = math.cos(angle) / cosine
        for j in range(len(y)):
            if j != k:
                value = value * ((cell - y[j]) / (y[k] - y[j]))
            value = value * ((x[j] - y[k]) / (x[j] - cell))
        rows.append(value)
        nodes.append(angle / step - turn(0))
    return np.stack(rows, axis=1), np.array(nodes)


def split3(matrix):
    hi = matrix.astype(np.float32).astype(BF16)
    lo = (matrix - hi.astype(np.float64)).astype(np.float32).astype(BF16)
    return np.concatenate([hi, hi, lo], axis=0)


def tables(segments, length, width):
    total = segments * length
    cells = np.arange(length, dtype=np.float64)

    def kernel(target, source):
        return 1.0 / (total * np.sin(np.pi / total * (target[None, :] - source[:, None])))

    right, right_nodes = factor(total, length, length, 2 * length - 1, total / 2 + length, 8)
    left, left_nodes = factor(total, length, total - length, total - 1, total / 2, 8)
    far, far_nodes = factor(total, length, 2 * length, total - length - 1, 1.5 * length - 0.5, 8)
    near_count, far_count = right.shape[1], far.shape[1]
    assert left.shape[1] == near_count
    charges = 2 * near_count + far_count
    forward = np.zeros((width, width + ceil_to(charges, 128)))
    with np.errstate(divide="ignore"):
        own = kernel(cells, cells)
    np.fill_diagonal(own, 0.0)
    forward[:length, :length] = own
    forward[:length, width : width + charges] = np.concatenate([right, left, far], axis=1)
    arriving = [kernel(cells + length, right_nodes), kernel(cells + (segments - 1) * length, left_nodes)]
    arriving += [kernel(cells + delta * length, far_nodes) for delta in range(2, segments - 1)]
    arriving = np.concatenate(arriving, axis=0)
    inward = np.zeros((ceil_to(arriving.shape[0], 128), width))
    inward[: arriving.shape[0], :length] = arriving
    return split3(forward), split3(inward), near_count, far_count


def series(terms, square):
    value = jnp.full_like(square, terms[-1])
    for term in terms[-2::-1]:
        value = value * square + term
    return value


def pad_lanes(value, width):
    rows, length = value.shape
    if width == length:
        return value
    return jnp.concatenate([value, jnp.zeros((rows, width - length), value.dtype)], axis=1)


def halves(value):
    hi = value.astype(BF16)
    return hi, (value - hi.astype(F32)).astype(BF16)


def step_kernel(
    segments, bands, chunk, near, far,
    fields_hbm, east_hbm, north_hbm, cutoff_hbm, damping_hbm, ship_hbm, forward_hbm, inward_hbm, out_hbm,
    cells, east, north, cutoff, damping, ship, forward, inward, facts, mix, sines, edge_out, edge_in,
    advected, spread, near_part, charges, arrived, result,
    load_sem, small_sem, halo_send, halo_recv, send_sem, recv_sem, store_sem,
):
    channels, rows_dev, length = fields_hbm.shape
    width = advected.shape[2]
    total = segments * length
    lat_count = rows_dev * bands
    chunks = rows_dev // chunk
    lines = channels * chunk
    slots = 2 * near + (segments - 3) * far
    me, band = lax.axis_index("lon"), lax.axis_index("lat")
    right, left = lax.rem(me + 1, segments), lax.rem(me + segments - 1, segments)
    peers = [lax.rem(me + p, segments) for p in range(1, segments)]
    small = [
        pltpu.make_async_copy(cutoff_hbm, cutoff, small_sem.at[0]),
        pltpu.make_async_copy(damping_hbm, damping, small_sem.at[1]),
        pltpu.make_async_copy(ship_hbm, ship, small_sem.at[2]),
        pltpu.make_async_copy(forward_hbm, forward, small_sem.at[3]),
        pltpu.make_async_copy(inward_hbm, inward, small_sem.at[4]),
    ]
    body = pl.ds(8, rows_dev)
    loads = [
        pltpu.make_async_copy(fields_hbm, cells.at[:, body], load_sem.at[0]),
        pltpu.make_async_copy(east_hbm, east, load_sem.at[1]),
        pltpu.make_async_copy(north_hbm, north.at[body], load_sem.at[2]),
    ]
    for load in small[:3] + loads + small[3:]:
        load.start()
    barrier = pltpu.get_barrier_semaphore()
    for peer in peers:
        pl.semaphore_signal(barrier, inc=1, device_id={"lon": peer}, device_id_type=MESH)

    @pl.when(band > 0)
    def _():
        pl.semaphore_signal(barrier, inc=1, device_id={"lat": band - 1}, device_id_type=MESH)

    @pl.when(band < bands - 1)
    def _():
        pl.semaphore_signal(barrier, inc=1, device_id={"lat": band + 1}, device_id_type=MESH)

    @pl.when(band == 0)
    def _():
        cells[:, 0:8, :] = jnp.zeros((channels, 8, length), F32)
        north[0:8, :] = jnp.zeros((8, length), F32)

    @pl.when(band == bands - 1)
    def _():
        cells[:, rows_dev + 8 : rows_dev + 16, :] = jnp.zeros((channels, 8, length), F32)

    def sine(k):
        z = jnp.minimum(k, lat_count - k) * (1.0 / lat_count)
        return z * series(SIN, z * z)

    for r in range(0, rows_dev, 8):
        row = (band * rows_dev + r + lax.broadcasted_iota(jnp.int32, (8, 128), 0)).astype(F32)
        inverse = 1.0 / sine(row + 0.5)
        facts[0, r : r + 8, :] = jnp.where(row < lat_count - 1, sine(row + 1.0), 0.0) * inverse
        facts[1, r : r + 8, :] = jnp.where(row > 0, sine(row), 0.0) * inverse

    for load in small[:3]:
        load.wait()
    repeat = width // 128

    def wide(value):
        return jnp.concatenate([value] * repeat, axis=1)

    column = lax.broadcasted_iota(jnp.int32, (BLOCK, width), 1)
    place = (me * length + column).astype(F32)
    every = lax.broadcasted_iota(jnp.int32, (BLOCK, lat_count), 1)
    local = lax.broadcasted_iota(jnp.int32, (BLOCK, lat_count), 0)
    slot_row = lax.broadcasted_iota(jnp.int32, (BLOCK, ship.shape[2]), 0)
    for r in range(0, rows_dev, BLOCK):
        here = slice(r, r + BLOCK)
        hit = every == local + (band * rows_dev + r)
        cut = jnp.sum(jnp.where(hit, cutoff[...].astype(F32), 0.0), axis=1, keepdims=True)
        damp = jnp.sum(jnp.where(hit, damping[...], 0.0), axis=1, keepdims=True)
        listed = jnp.zeros((BLOCK, ship.shape[2]), F32)
        for d in range(bands):
            listed = listed + jnp.where(ship[band, d : d + 1, :] == slot_row + r, 1.0, 0.0)
        polar = jnp.sum(listed, axis=1, keepdims=True) > 0.0
        waves = 2.0 * cut + 1.0
        mix[0, here, :] = jnp.broadcast_to(
            jnp.where(polar, damp + (1.0 - damp) * (waves * (1.0 / total)), 1.0), (BLOCK, 128)
        )
        mix[1, here, :] = jnp.broadcast_to(jnp.where(polar, 1.0 - damp, 0.0), (BLOCK, 128))
        turns = waves * place
        part = turns - jnp.floor(turns * (0.5 / total) + 0.5) * (2.0 * total)
        z = part * (1.0 / total)
        square = z * z
        sines[0, here, :] = z * series(SIN, square)
        sines[1, here, :] = series(COS, square)

    for load in loads:
        load.wait()
    blocks = rows_dev // BLOCK
    lane = lax.broadcasted_iota(jnp.int32, (BLOCK, edge_out.shape[2]), 1)
    eastern, western = jnp.zeros(lane.shape, F32), jnp.zeros(lane.shape, F32)
    for b in range(blocks):
        for c in range(channels):
            rows = slice(8 + b * BLOCK, 8 + (b + 1) * BLOCK)
            eastern = jnp.where(lane == 8 * b + c, cells[c, rows, length - 1 : length], eastern)
            western = jnp.where(lane == 8 * b + c, cells[c, rows, 0:1], western)
        eastern = jnp.where(lane == 8 * b + channels, east[b * BLOCK : (b + 1) * BLOCK, length - 1 : length], eastern)
    edge_out[0] = eastern
    edge_out[1] = western
    beside = jnp.where(band > 0, 1, 0) + jnp.where(band < bands - 1, 1, 0)
    pl.semaphore_wait(barrier, segments - 1 + beside)

    def halo(source, target, slot, device):
        return pltpu.make_async_remote_copy(
            src_ref=source, dst_ref=target, send_sem=halo_send.at[slot],
            recv_sem=halo_recv.at[slot], device_id=device, device_id_type=MESH,
        )

    first, last = pl.ds(0, 8), pl.ds(rows_dev - 8, 8)
    above = pl.ds(rows_dev + 8, 8)
    up = {"lat": jnp.minimum(band + 1, bands - 1)}
    down = {"lat": jnp.maximum(band - 1, 0)}
    northward = [
        halo(fields_hbm.at[:, last], cells.at[:, pl.ds(0, 8)], 0, up),
        halo(north_hbm.at[last], north.at[pl.ds(0, 8)], 1, up),
    ]
    southward = halo(fields_hbm.at[:, first], cells.at[:, above], 2, down)
    sideways = [
        halo(edge_out.at[0], edge_in.at[0], 3, {"lon": right}),
        halo(edge_out.at[1], edge_in.at[1], 4, {"lon": left}),
    ]
    for copy in sideways:
        copy.start()

    @pl.when(band < bands - 1)
    def _():
        for copy in northward:
            copy.start()

    @pl.when(band > 0)
    def _():
        southward.start()

    for copy in sideways:
        copy.wait()

    @pl.when(band < bands - 1)
    def _():
        for copy in northward:
            copy.wait_send()
        southward.wait_recv()

    @pl.when(band > 0)
    def _():
        southward.wait_send()
        for copy in northward:
            copy.wait_recv()

    for load in small[3:]:
        load.wait()

    def advect(k):
        for r in range(k * chunk, (k + 1) * chunk, BLOCK):
            here = slice(r, r + BLOCK)
            lane0 = 8 * (r // BLOCK)
            ce = pad_lanes(east[here, :], width)
            cw = pltpu.roll(ce, 1, 1)
            cw = jnp.where(column == 0, edge_in[0, :, lane0 + channels : lane0 + channels + 1], cw)
            cw = jnp.where(column < length, cw, 0.0)
            cn = pad_lanes(north[8 + r : 8 + r + BLOCK, :], width) * wide(facts[0, here, :])
            cs = pad_lanes(north[7 + r : 7 + r + BLOCK, :], width) * wide(facts[1, here, :])
            at_east, at_west = jnp.minimum(ce, 0.0), jnp.maximum(cw, 0.0)
            at_north, at_south = jnp.minimum(cn, 0.0), jnp.maximum(cs, 0.0)
            at_home = 1.0 - (ce - at_east) + (cw - at_west) - (cn - at_north) + (cs - at_south)
            sin, cos = sines[0, here, :], sines[1, here, :]
            for c in range(channels):
                field = pad_lanes(cells[c, 8 + r : 8 + r + BLOCK, :], width)
                upper = pad_lanes(cells[c, 9 + r : 9 + r + BLOCK, :], width)
                lower = pad_lanes(cells[c, 7 + r : 7 + r + BLOCK, :], width)
                ahead = jnp.where(
                    column == length - 1, edge_in[1, :, lane0 + c : lane0 + c + 1], pltpu.roll(field, width - 1, 1)
                )
                behind = jnp.where(column == 0, edge_in[0, :, lane0 + c : lane0 + c + 1], pltpu.roll(field, 1, 1))
                value = at_home * field - at_east * ahead + at_west * behind - at_north * upper + at_south * lower
                advected[c, here, :] = value
                line = c * chunk + r - k * chunk
                for q, wave in enumerate((sin, cos)):
                    hi, lo = halves(value * wave)
                    spread[k % 2, q * lines + line : q * lines + line + BLOCK, 0:width] = hi
                    spread[k % 2, q * lines + line : q * lines + line + BLOCK, width : 2 * width] = lo

    outward = []

    def exchange(k):
        for p, peer in enumerate(peers):
            delta = p + 1
            if delta == 1:
                source, target, count = 0, 0, near
            elif delta == segments - 1:
                source, target, count = near, near, near
            else:
                source, target, count = 2 * near, 2 * near + (delta - 2) * far, far
            copy = pltpu.make_async_remote_copy(
                src_ref=charges.at[k, :, pl.ds(source, count)],
                dst_ref=arrived.at[k, :, pl.ds(target, count)],
                send_sem=send_sem.at[k, p],
                recv_sem=recv_sem.at[k, p],
                device_id={"lon": peer},
                device_id_type=MESH,
            )
            copy.start()
            outward.append(copy)

    for k in range(chunks):
        advect(k)
        product = jnp.dot(
            spread[k % 2], forward[0 : 2 * width, :], preferred_element_type=F32
        ) + jnp.dot(spread[k % 2, :, 0:width], forward[2 * width : 3 * width, :], preferred_element_type=F32)
        for q in range(2):
            moments = product[q * lines : (q + 1) * lines, width:]
            charges[k, q] = moments.T[0 : 2 * near + far, :]
        exchange(k)
        near_part[k] = product[:, 0:width]

    slot = lax.broadcasted_iota(jnp.int32, (slots, lines), 0)
    ahead_of = jnp.where(
        slot < near, jnp.where(me >= 1, 1, 0),
        jnp.where(
            slot < 2 * near, jnp.where(me >= segments - 1, 1, 0),
            jnp.where(slot < 2 * near + (me - 1) * far, 1, 0),
        ),
    )
    sign = jnp.where(ahead_of > 0, 1.0, -1.0)
    deep = inward.shape[0] // 3
    stores = []
    for k in range(chunks):
        for p in range(segments - 1):
            outward[k * (segments - 1) + p].wait_recv()
        sums = []
        for q in range(2):
            hi, lo = halves(pad_lanes((arrived[k, q] * sign).T, deep))
            sums.append(
                jnp.dot(jnp.concatenate([hi, lo], axis=1), inward[0 : 2 * deep, :], preferred_element_type=F32)
                + jnp.dot(hi, inward[2 * deep : 3 * deep, :], preferred_element_type=F32)
            )
        for r in range(k * chunk, (k + 1) * chunk, BLOCK):
            here = slice(r, r + BLOCK)
            keep, share = wide(mix[0, here, :]), wide(mix[1, here, :])
            sin, cos = sines[0, here, :] * share, sines[1, here, :] * share
            for c in range(channels):
                line = c * chunk + r - k * chunk
                u = near_part[k, line : line + BLOCK, :] + sums[0][line : line + BLOCK, :]
                v = near_part[k, lines + line : lines + line + BLOCK, :] + sums[1][line : line + BLOCK, :]
                value = keep * advected[c, here, :] + (sin * v - cos * u)
                result[c, here, :] = value[:, 0:length]
        rows = pl.ds(k * chunk, chunk)
        store = pltpu.make_async_copy(result.at[:, rows], out_hbm.at[:, rows], store_sem.at[k])
        store.start()
        stores.append(store)
    for store in stores:
        store.wait()
    for copy in outward:
        copy.wait_send()


def per_device(fields, east_courant, north_courant, cutoff, damping, ship_rows):
    channels, rows_dev, length = fields.shape
    segments, bands = lax.axis_size("lon"), lax.axis_size("lat")
    width = ceil_to(length, 128)
    chunk = max(c for c in range(BLOCK, 49, BLOCK) if rows_dev % c == 0)
    chunks = rows_dev // chunk
    lines = channels * chunk
    forward, inward, near, far = tables(segments, length, width)
    slots = 2 * near + (segments - 3) * far
    edge = pltpu.VMEM((2, BLOCK, ceil_to(8 * (rows_dev // BLOCK), 128)), F32)
    semaphores = pltpu.SemaphoreType.DMA((chunks, segments - 1))
    whole = pl.BlockSpec(memory_space=pl.ANY)
    return pl.pallas_call(
        functools.partial(step_kernel, segments, bands, chunk, near, far),
        out_shape=jax.ShapeDtypeStruct(fields.shape, F32),
        in_specs=[whole] * 8,
        out_specs=whole,
        scratch_shapes=[
            pltpu.VMEM((channels, rows_dev + 16, length), F32),
            pltpu.VMEM((rows_dev, length), F32),
            pltpu.VMEM((rows_dev + 16, length), F32),
            pltpu.VMEM((1, cutoff.shape[0]), jnp.int32),
            pltpu.VMEM((1, damping.shape[0]), F32),
            pltpu.VMEM(ship_rows.shape, jnp.int32),
            pltpu.VMEM(forward.shape, BF16),
            pltpu.VMEM(inward.shape, BF16),
            pltpu.VMEM((2, rows_dev, 128), F32),
            pltpu.VMEM((2, rows_dev, 128), F32),
            pltpu.VMEM((2, rows_dev, width), F32),
            edge, edge,
            pltpu.VMEM((channels, rows_dev, width), F32),
            pltpu.VMEM((2, 2 * lines, 2 * width), BF16),
            pltpu.VMEM((chunks, 2 * lines, width), F32),
            pltpu.VMEM((chunks, 2, 2 * near + far, lines), F32),
            pltpu.VMEM((chunks, 2, slots, lines), F32),
            pltpu.VMEM((channels, rows_dev, length), F32),
            pltpu.SemaphoreType.DMA((3,)),
            pltpu.SemaphoreType.DMA((5,)),
            pltpu.SemaphoreType.DMA((5,)),
            pltpu.SemaphoreType.DMA((5,)),
            semaphores, semaphores,
            pltpu.SemaphoreType.DMA((chunks,)),
        ],
        compiler_params=pltpu.CompilerParams(
            collective_id=0, has_side_effects=True, vmem_limit_bytes=36 * 1024 * 1024
        ),
    )(
        fields, east_courant, north_courant, cutoff[None, :], damping[None, :], ship_rows,
        jnp.asarray(forward), jnp.asarray(inward),
    )


def solution(mesh):
    placed = (P(None, "lat", "lon"), P("lat", "lon"), P("lat", "lon"), P(), P(), P())
    return jax.shard_map(
        per_device, mesh=mesh, in_specs=placed, out_specs=P(None, "lat", "lon"), check_vma=False
    )
```

```python
import functools
import math

import jax
import jax.numpy as jnp
import numpy as np
from jax import lax
from jax.experimental import pallas as pl
from jax.experimental.pallas import tpu as pltpu
from jax.sharding import PartitionSpec as P

MESH = pl.DeviceIdType.MESH
BF16 = jnp.bfloat16
F32 = jnp.float32
BLOCK = 16
SIN = (3.14159265357, -5.1677127773, 2.55016398193, -0.59926406421, 0.0821440508123,
       -0.00736648693826, 0.000461586773619, -1.89446619668e-05)
COS = (0.999999999886, -4.93480218586, 4.05871181724, -1.33526028616, 0.235320825531,
       -0.0257858087643, 0.00190432895602, -8.86909350679e-05)


def ceil_to(value, unit):
    return -(-value // unit) * unit


def elliptic_dn(fraction, complement):
    a, b = [1.0], [math.sqrt(complement)]
    c = [math.sqrt(1.0 - complement)]
    for _ in range(12):
        x, y = a[-1], b[-1]
        a.append((x + y) / 2)
        b.append(math.sqrt(x * y))
        c.append((x - y) / 2)
    phi = 2.0 ** 12 * fraction * math.pi / 2
    for i in range(12, 0, -1):
        phi = (phi + math.asin(max(-1.0, min(1.0, c[i] * math.sin(phi) / a[i])))) / 2
    return math.sqrt(1.0 - (1.0 - complement) * math.sin(phi) ** 2)


def zolotarev(a, b, c, d, unit):
    gamma = (c - a) * (d - b) / ((c - b) * (d - a))
    count = ceil_to(math.ceil(math.log(16 * gamma) * math.log(4 * 2.0 ** 24) / math.pi ** 2), unit)
    alpha = 2 * gamma - 1 + 2 * math.sqrt(gamma * gamma - gamma)

    def moebius(z):
        q = (z + alp) * -2.0 / ((z - 1.0) * (alp - 1.0)) * (b - a) / (b - c)
        return (a - q * c) / (1.0 - q)

    alp = alpha
    values = [alp * elliptic_dn((i + 0.5) / count, 1.0 / alp ** 2) for i in range(count)]
    return [moebius(-v) for v in values], [moebius(v) for v in values]


def factor(total, length, low, high, pole, unit):
    step = math.pi / total
    ref = pole - total / 2

    def turn(n):
        return (n - ref + total / 2) % total - total / 2

    def tangent(n):
        return math.tan(step * turn(n))

    here, there = (tangent(0), tangent(length - 1)), (tangent(low), tangent(high))
    if here[0] < there[0]:
        y, x = zolotarev(*here, *there, unit)
    else:
        x, y = zolotarev(*there, *here, unit)
    cell = np.array([tangent(m) for m in range(length)])
    cosine = np.array([math.cos(step * turn(m)) for m in range(length)])
    rows, nodes = [], []
    for k in range(len(y)):
        angle = math.atan(y[k])
        value = math.cos(angle) / cosine
        for j in range(len(y)):
            if j != k:
                value = value * ((cell - y[j]) / (y[k] - y[j]))
            value = value * ((x[j] - y[k]) / (x[j] - cell))
        rows.append(value)
        nodes.append(angle / step - turn(0))
    return np.stack(rows, axis=1), np.array(nodes)


def split3(matrix):
    hi = matrix.astype(np.float32).astype(BF16)
    lo = (matrix - hi.astype(np.float64)).astype(np.float32).astype(BF16)
    return np.concatenate([hi, hi, lo], axis=0)


def tables(segments, length, width):
    total = segments * length
    cells = np.arange(length, dtype=np.float64)

    def kernel(target, source):
        return 1.0 / (total * np.sin(np.pi / total * (target[None, :] - source[:, None])))

    right, right_nodes = factor(total, length, length, 2 * length - 1, total / 2 + length, 8)
    left, left_nodes = factor(total, length, total - length, total - 1, total / 2, 8)
    far, far_nodes = factor(total, length, 2 * length, total - length - 1, 1.5 * length - 0.5, 8)
    near_count, far_count = right.shape[1], far.shape[1]
    assert left.shape[1] == near_count
    charges = 2 * near_count + far_count
    forward = np.zeros((width, width + ceil_to(charges, 128)))
    with np.errstate(divide="ignore"):
        own = kernel(cells, cells)
    np.fill_diagonal(own, 0.0)
    forward[:length, :length] = own
    forward[:length, width : width + charges] = np.concatenate([right, left, far], axis=1)
    arriving = [kernel(cells + length, right_nodes), kernel(cells + (segments - 1) * length, left_nodes)]
    arriving += [kernel(cells + delta * length, far_nodes) for delta in range(2, segments - 1)]
    arriving = np.concatenate(arriving, axis=0)
    inward = np.zeros((ceil_to(arriving.shape[0], 128), width))
    inward[: arriving.shape[0], :length] = arriving
    return split3(forward), split3(inward), near_count, far_count


def series(terms, square):
    value = jnp.full_like(square, terms[-1])
    for term in terms[-2::-1]:
        value = value * square + term
    return value


def pad_lanes(value, width):
    rows, length = value.shape
    if width == length:
        return value
    return jnp.concatenate([value, jnp.zeros((rows, width - length), value.dtype)], axis=1)


def halves(value):
    hi = value.astype(BF16)
    return hi, (value - hi.astype(F32)).astype(BF16)


def step_kernel(
    segments, bands, chunk, near, far,
    fields_hbm, east_hbm, north_hbm, cutoff_hbm, damping_hbm, ship_hbm, forward_hbm, inward_hbm, result,
    cells, east, north, cutoff, damping, ship, forward, inward, facts, mix, sines, edge_out, edge_in,
    advected, spread, near_part, charges, arrived,
    load_sem, small_sem, halo_send, halo_recv, send_sem, recv_sem,
):
    channels, rows_dev, length = fields_hbm.shape
    width = advected.shape[2]
    total = segments * length
    lat_count = rows_dev * bands
    chunks = rows_dev // chunk
    lines = channels * chunk
    slots = 2 * near + (segments - 3) * far
    me, band = lax.axis_index("lon"), lax.axis_index("lat")
    right, left = lax.rem(me + 1, segments), lax.rem(me + segments - 1, segments)
    peers = [lax.rem(me + p, segments) for p in range(1, segments)]
    small = [
        pltpu.make_async_copy(cutoff_hbm, cutoff, small_sem.at[0]),
        pltpu.make_async_copy(damping_hbm, damping, small_sem.at[1]),
        pltpu.make_async_copy(ship_hbm, ship, small_sem.at[2]),
        pltpu.make_async_copy(forward_hbm, forward, small_sem.at[3]),
        pltpu.make_async_copy(inward_hbm, inward, small_sem.at[4]),
    ]
    body = pl.ds(8, rows_dev)
    loads = [
        pltpu.make_async_copy(fields_hbm, cells.at[:, body], load_sem.at[0]),
        pltpu.make_async_copy(east_hbm, east, load_sem.at[1]),
        pltpu.make_async_copy(north_hbm, north.at[body], load_sem.at[2]),
    ]
    for load in small[:3] + loads + small[3:]:
        load.start()
    barrier = pltpu.get_barrier_semaphore()
    for peer in peers:
        pl.semaphore_signal(barrier, inc=1, device_id={"lon": peer}, device_id_type=MESH)

    @pl.when(band > 0)
    def _():
        pl.semaphore_signal(barrier, inc=1, device_id={"lat": band - 1}, device_id_type=MESH)

    @pl.when(band < bands - 1)
    def _():
        pl.semaphore_signal(barrier, inc=1, device_id={"lat": band + 1}, device_id_type=MESH)

    @pl.when(band == 0)
    def _():
        cells[:, 0:8, :] = jnp.zeros((channels, 8, length), F32)
        north[0:8, :] = jnp.zeros((8, length), F32)

    @pl.when(band == bands - 1)
    def _():
        cells[:, rows_dev + 8 : rows_dev + 16, :] = jnp.zeros((channels, 8, length), F32)

    def sine(k):
        z = jnp.minimum(k, lat_count - k) * (1.0 / lat_count)
        return z * series(SIN, z * z)

    for r in range(0, rows_dev, 8):
        row = (band * rows_dev + r + lax.broadcasted_iota(jnp.int32, (8, 128), 0)).astype(F32)
        inverse = 1.0 / sine(row + 0.5)
        facts[0, r : r + 8, :] = jnp.where(row < lat_count - 1, sine(row + 1.0), 0.0) * inverse
        facts[1, r : r + 8, :] = jnp.where(row > 0, sine(row), 0.0) * inverse

    for load in small[:3]:
        load.wait()
    repeat = width // 128

    def wide(value):
        return jnp.concatenate([value] * repeat, axis=1)

    column = lax.broadcasted_iota(jnp.int32, (BLOCK, width), 1)
    place = (me * length + column).astype(F32)
    every = lax.broadcasted_iota(jnp.int32, (BLOCK, lat_count), 1)
    local = lax.broadcasted_iota(jnp.int32, (BLOCK, lat_count), 0)
    slot_row = lax.broadcasted_iota(jnp.int32, (BLOCK, ship.shape[2]), 0)
    for r in range(0, rows_dev, BLOCK):
        here = slice(r, r + BLOCK)
        hit = every == local + (band * rows_dev + r)
        cut = jnp.sum(jnp.where(hit, cutoff[...].astype(F32), 0.0), axis=1, keepdims=True)
        damp = jnp.sum(jnp.where(hit, damping[...], 0.0), axis=1, keepdims=True)
        listed = jnp.zeros((BLOCK, ship.shape[2]), F32)
        for d in range(bands):
            listed = listed + jnp.where(ship[band, d : d + 1, :] == slot_row + r, 1.0, 0.0)
        polar = jnp.sum(listed, axis=1, keepdims=True) > 0.0
        waves = 2.0 * cut + 1.0
        mix[0, here, :] = jnp.broadcast_to(
            jnp.where(polar, damp + (1.0 - damp) * (waves * (1.0 / total)), 1.0), (BLOCK, 128)
        )
        mix[1, here, :] = jnp.broadcast_to(jnp.where(polar, 1.0 - damp, 0.0), (BLOCK, 128))
        turns = waves * place
        part = turns - jnp.floor(turns * (0.5 / total) + 0.5) * (2.0 * total)
        z = part * (1.0 / total)
        square = z * z
        sines[0, here, :] = z * series(SIN, square)
        sines[1, here, :] = series(COS, square)

    for load in loads:
        load.wait()
    blocks = rows_dev // BLOCK
    lane = lax.broadcasted_iota(jnp.int32, (BLOCK, edge_out.shape[2]), 1)
    eastern, western = jnp.zeros(lane.shape, F32), jnp.zeros(lane.shape, F32)
    for b in range(blocks):
        for c in range(channels):
            rows = slice(8 + b * BLOCK, 8 + (b + 1) * BLOCK)
            eastern = jnp.where(lane == 8 * b + c, cells[c, rows, length - 1 : length], eastern)
            western = jnp.where(lane == 8 * b + c, cells[c, rows, 0:1], western)
        eastern = jnp.where(lane == 8 * b + channels, east[b * BLOCK : (b + 1) * BLOCK, length - 1 : length], eastern)
    edge_out[0] = eastern
    edge_out[1] = western
    beside = jnp.where(band > 0, 1, 0) + jnp.where(band < bands - 1, 1, 0)
    pl.semaphore_wait(barrier, segments - 1 + beside)

    def halo(source, target, slot, device):
        return pltpu.make_async_remote_copy(
            src_ref=source, dst_ref=target, send_sem=halo_send.at[slot],
            recv_sem=halo_recv.at[slot], device_id=device, device_id_type=MESH,
        )

    first, last = pl.ds(0, 8), pl.ds(rows_dev - 8, 8)
    above = pl.ds(rows_dev + 8, 8)
    up = {"lat": jnp.minimum(band + 1, bands - 1)}
    down = {"lat": jnp.maximum(band - 1, 0)}
    northward = [
        halo(fields_hbm.at[:, last], cells.at[:, pl.ds(0, 8)], 0, up),
        halo(north_hbm.at[last], north.at[pl.ds(0, 8)], 1, up),
    ]
    southward = halo(fields_hbm.at[:, first], cells.at[:, above], 2, down)
    sideways = [
        halo(edge_out.at[0], edge_in.at[0], 3, {"lon": right}),
        halo(edge_out.at[1], edge_in.at[1], 4, {"lon": left}),
    ]
    for copy in sideways:
        copy.start()

    @pl.when(band < bands - 1)
    def _():
        for copy in northward:
            copy.start()

    @pl.when(band > 0)
    def _():
        southward.start()

    for copy in sideways:
        copy.wait()

    @pl.when(band < bands - 1)
    def _():
        for copy in northward:
            copy.wait_send()
        southward.wait_recv()

    @pl.when(band > 0)
    def _():
        southward.wait_send()
        for copy in northward:
            copy.wait_recv()

    for load in small[3:]:
        load.wait()

    def advect(k):
        for r in range(k * chunk, (k + 1) * chunk, BLOCK):
            here = slice(r, r + BLOCK)
            lane0 = 8 * (r // BLOCK)
            ce = pad_lanes(east[here, :], width)
            cw = pltpu.roll(ce, 1, 1)
            cw = jnp.where(column == 0, edge_in[0, :, lane0 + channels : lane0 + channels + 1], cw)
            cw = jnp.where(column < length, cw, 0.0)
            cn = pad_lanes(north[8 + r : 8 + r + BLOCK, :], width) * wide(facts[0, here, :])
            cs = pad_lanes(north[7 + r : 7 + r + BLOCK, :], width) * wide(facts[1, here, :])
            at_east, at_west = jnp.minimum(ce, 0.0), jnp.maximum(cw, 0.0)
            at_north, at_south = jnp.minimum(cn, 0.0), jnp.maximum(cs, 0.0)
            at_home = 1.0 - (ce - at_east) + (cw - at_west) - (cn - at_north) + (cs - at_south)
            sin, cos = sines[0, here, :], sines[1, here, :]
            for c in range(channels):
                field = pad_lanes(cells[c, 8 + r : 8 + r + BLOCK, :], width)
                upper = pad_lanes(cells[c, 9 + r : 9 + r + BLOCK, :], width)
                lower = pad_lanes(cells[c, 7 + r : 7 + r + BLOCK, :], width)
                ahead = jnp.where(
                    column == length - 1, edge_in[1, :, lane0 + c : lane0 + c + 1], pltpu.roll(field, width - 1, 1)
                )
                behind = jnp.where(column == 0, edge_in[0, :, lane0 + c : lane0 + c + 1], pltpu.roll(field, 1, 1))
                value = at_home * field - at_east * ahead + at_west * behind - at_north * upper + at_south * lower
                advected[c, here, :] = value
                line = c * chunk + r - k * chunk
                for q, wave in enumerate((sin, cos)):
                    hi, lo = halves(value * wave)
                    spread[k % 2, q * lines + line : q * lines + line + BLOCK, 0:width] = hi
                    spread[k % 2, q * lines + line : q * lines + line + BLOCK, width : 2 * width] = lo

    outward = []

    def exchange(k):
        for p, peer in enumerate(peers):
            delta = p + 1
            if delta == 1:
                source, target, count = 0, 0, near
            elif delta == segments - 1:
                source, target, count = near, near, near
            else:
                source, target, count = 2 * near, 2 * near + (delta - 2) * far, far
            copy = pltpu.make_async_remote_copy(
                src_ref=charges.at[k, :, pl.ds(source, count)],
                dst_ref=arrived.at[k, :, pl.ds(target, count)],
                send_sem=send_sem.at[k, p],
                recv_sem=recv_sem.at[k, p],
                device_id={"lon": peer},
                device_id_type=MESH,
            )
            copy.start()
            outward.append(copy)

    for k in range(chunks):
        advect(k)
        product = jnp.dot(
            spread[k % 2], forward[0 : 2 * width, :], preferred_element_type=F32
        ) + jnp.dot(spread[k % 2, :, 0:width], forward[2 * width : 3 * width, :], preferred_element_type=F32)
        for q in range(2):
            moments = product[q * lines : (q + 1) * lines, width:]
            charges[k, q] = moments.T[0 : 2 * near + far, :]
        exchange(k)
        near_part[k] = product[:, 0:width]

    slot = lax.broadcasted_iota(jnp.int32, (slots, lines), 0)
    ahead_of = jnp.where(
        slot < near, jnp.where(me >= 1, 1, 0),
        jnp.where(
            slot < 2 * near, jnp.where(me >= segments - 1, 1, 0),
            jnp.where(slot < 2 * near + (me - 1) * far, 1, 0),
        ),
    )
    sign = jnp.where(ahead_of > 0, 1.0, -1.0)
    deep = inward.shape[0] // 3
    for k in range(chunks):
        for p in range(segments - 1):
            outward[k * (segments - 1) + p].wait_recv()
        sums = []
        for q in range(2):
            hi, lo = halves(pad_lanes((arrived[k, q] * sign).T, deep))
            sums.append(
                jnp.dot(jnp.concatenate([hi, lo], axis=1), inward[0 : 2 * deep, :], preferred_element_type=F32)
                + jnp.dot(hi, inward[2 * deep : 3 * deep, :], preferred_element_type=F32)
            )
        for r in range(k * chunk, (k + 1) * chunk, BLOCK):
            here = slice(r, r + BLOCK)
            keep, share = wide(mix[0, here, :]), wide(mix[1, here, :])
            sin, cos = sines[0, here, :] * share, sines[1, here, :] * share
            for c in range(channels):
                line = c * chunk + r - k * chunk
                u = near_part[k, line : line + BLOCK, :] + sums[0][line : line + BLOCK, :]
                v = near_part[k, lines + line : lines + line + BLOCK, :] + sums[1][line : line + BLOCK, :]
                value = keep * advected[c, here, :] + (sin * v - cos * u)
                result[c, here, :] = value[:, 0:length]
    for copy in outward:
        copy.wait_send()


def per_device(fields, east_courant, north_courant, cutoff, damping, ship_rows):
    channels, rows_dev, length = fields.shape
    segments, bands = lax.axis_size("lon"), lax.axis_size("lat")
    width = ceil_to(length, 128)
    chunk = max(c for c in range(BLOCK, 49, BLOCK) if rows_dev % c == 0)
    chunks = rows_dev // chunk
    lines = channels * chunk
    forward, inward, near, far = tables(segments, length, width)
    slots = 2 * near + (segments - 3) * far
    edge = pltpu.VMEM((2, BLOCK, ceil_to(8 * (rows_dev // BLOCK), 128)), F32)
    semaphores = pltpu.SemaphoreType.DMA((chunks, segments - 1))
    whole = pl.BlockSpec(memory_space=pl.ANY)
    return pl.pallas_call(
        functools.partial(step_kernel, segments, bands, chunk, near, far),
        out_shape=pltpu.VMEM(fields.shape, F32),
        in_specs=[whole] * 8,
        out_specs=pl.BlockSpec(memory_space=pltpu.VMEM),
        scratch_shapes=[
            pltpu.VMEM((channels, rows_dev + 16, length), F32),
            pltpu.VMEM((rows_dev, length), F32),
            pltpu.VMEM((rows_dev + 16, length), F32),
            pltpu.VMEM((1, cutoff.shape[0]), jnp.int32),
            pltpu.VMEM((1, damping.shape[0]), F32),
            pltpu.VMEM(ship_rows.shape, jnp.int32),
            pltpu.VMEM(forward.shape, BF16),
            pltpu.VMEM(inward.shape, BF16),
            pltpu.VMEM((2, rows_dev, 128), F32),
            pltpu.VMEM((2, rows_dev, 128), F32),
            pltpu.VMEM((2, rows_dev, width), F32),
            edge, edge,
            pltpu.VMEM((channels, rows_dev, width), F32),
            pltpu.VMEM((2, 2 * lines, 2 * width), BF16),
            pltpu.VMEM((chunks, 2 * lines, width), F32),
            pltpu.VMEM((chunks, 2, 2 * near + far, lines), F32),
            pltpu.VMEM((chunks, 2, slots, lines), F32),
            pltpu.SemaphoreType.DMA((3,)),
            pltpu.SemaphoreType.DMA((5,)),
            pltpu.SemaphoreType.DMA((5,)),
            pltpu.SemaphoreType.DMA((5,)),
            semaphores, semaphores,
        ],
        compiler_params=pltpu.CompilerParams(
            collective_id=0, has_side_effects=True, vmem_limit_bytes=36 * 1024 * 1024
        ),
    )(
        *(
            pltpu.with_memory_space_constraint(value, pltpu.HBM)
            for value in (
                fields, east_courant, north_courant, cutoff[None, :], damping[None, :], ship_rows,
                jnp.asarray(forward), jnp.asarray(inward),
            )
        )
    )


def solution(mesh):
    placed = (P(None, "lat", "lon"), P("lat", "lon"), P("lat", "lon"), P(), P(), P())
    return jax.shard_map(
        per_device, mesh=mesh, in_specs=placed, out_specs=P(None, "lat", "lon"), check_vma=False
    )
```

```python
import functools
import math

import jax
import jax.numpy as jnp
import numpy as np
from jax import lax
from jax.experimental import pallas as pl
from jax.experimental.pallas import tpu as pltpu
from jax.sharding import PartitionSpec as P

MESH = pl.DeviceIdType.MESH
BF16 = jnp.bfloat16
F32 = jnp.float32
BLOCK = 16
SIN = (3.14159265357, -5.1677127773, 2.55016398193, -0.59926406421, 0.0821440508123,
       -0.00736648693826, 0.000461586773619, -1.89446619668e-05)
COS = (0.999999999886, -4.93480218586, 4.05871181724, -1.33526028616, 0.235320825531,
       -0.0257858087643, 0.00190432895602, -8.86909350679e-05)


def ceil_to(value, unit):
    return -(-value // unit) * unit


def elliptic_dn(fraction, complement):
    a, b = [1.0], [math.sqrt(complement)]
    c = [math.sqrt(1.0 - complement)]
    for _ in range(12):
        x, y = a[-1], b[-1]
        a.append((x + y) / 2)
        b.append(math.sqrt(x * y))
        c.append((x - y) / 2)
    phi = 2.0 ** 12 * fraction * math.pi / 2
    for i in range(12, 0, -1):
        phi = (phi + math.asin(max(-1.0, min(1.0, c[i] * math.sin(phi) / a[i])))) / 2
    return math.sqrt(1.0 - (1.0 - complement) * math.sin(phi) ** 2)


def zolotarev(a, b, c, d, count):
    gamma = (c - a) * (d - b) / ((c - b) * (d - a))
    alpha = 2 * gamma - 1 + 2 * math.sqrt(gamma * gamma - gamma)

    def moebius(z):
        q = (z + alpha) * -2.0 / ((z - 1.0) * (alpha - 1.0)) * (b - a) / (b - c)
        return (a - q * c) / (1.0 - q)

    values = [alpha * elliptic_dn((i + 0.5) / count, 1.0 / alpha ** 2) for i in range(count)]
    return [moebius(-v) for v in values], [moebius(v) for v in values]


def cosecant(total, target, source):
    away = target[None, :] - source[:, None]
    with np.errstate(divide="ignore"):
        return np.where(away == 0, 0.0, 1.0 / (total * np.sin(np.pi / total * away)))


def factor(total, length, low, high, pole):
    step = math.pi / total
    ref = pole - total / 2

    def turn(n):
        return (n - ref + total / 2) % total - total / 2

    def tangent(n):
        return math.tan(step * turn(n))

    here, there = (tangent(0), tangent(length - 1)), (tangent(low), tangent(high))
    cell = np.array([tangent(m) for m in range(length)])
    cosine = np.array([math.cos(step * turn(m)) for m in range(length)])
    source, target = np.arange(length, dtype=np.float64), np.arange(low, high + 1, dtype=np.float64)
    exact = cosecant(total, target, source)
    for count in range(8, 64, 8):
        if here[0] < there[0]:
            y, x = zolotarev(*here, *there, count)
        else:
            x, y = zolotarev(*there, *here, count)
        rows, nodes = [], []
        for k in range(count):
            angle = math.atan(y[k])
            value = math.cos(angle) / cosine
            for j in range(count):
                if j != k:
                    value = value * ((cell - y[j]) / (y[k] - y[j]))
                value = value * ((x[j] - y[k]) / (x[j] - cell))
            rows.append(value)
            nodes.append(angle / step - turn(0))
        charge, nodes = np.stack(rows, axis=1), np.array(nodes)
        if np.abs(charge @ cosecant(total, target, nodes) / exact - 1.0).max() < 2.0 ** -24:
            break
    return charge, nodes


def split3(matrix):
    hi = matrix.astype(np.float32).astype(BF16)
    lo = (matrix - hi.astype(np.float64)).astype(np.float32).astype(BF16)
    return np.concatenate([hi, hi, lo], axis=0)


def layout(segments, near, far):
    start = {1: 0, segments - 1: near}
    for delta in range(2, segments - 1):
        start[delta] = 2 * near + (delta - 2) * far
    ends = 2 * near + (segments - 3) * far
    return start, ends, ends + 2 * segments


def tables(segments, length, width):
    total = segments * length
    cells = np.arange(length, dtype=np.float64)
    right, right_nodes = factor(total, length, length, 2 * length - 1, total / 2 + length)
    left, left_nodes = factor(total, length, total - length, total - 1, total / 2)
    others, far_nodes = factor(total, length, 2 * length, total - length - 1, 1.5 * length - 0.5)
    near, far = right.shape[1], others.shape[1]
    assert left.shape[1] == near
    start, ends, rows = layout(segments, near, far)
    forward = np.zeros((width, width + ceil_to(2 * near + far, 128)))
    forward[:length, :length] = cosecant(total, cells, cells)
    for at, block in ((0, right), (near, left), (2 * near, others)):
        forward[:length, width + at : width + at + block.shape[1]] = block
    inward = np.zeros((ceil_to(rows, 128), width))
    for delta in range(segments):
        target = cells + delta * length
        if delta > 0:
            nodes = {1: right_nodes, segments - 1: left_nodes}.get(delta, far_nodes)
            inward[start[delta] : start[delta] + nodes.size, :length] = cosecant(total, target, nodes)
        inward[ends + delta, :length] = cosecant(total, target, np.array([length - 1.0]))[0]
        inward[ends + segments + delta, :length] = cosecant(total, target, np.array([0.0]))[0]
    return split3(forward), split3(inward), near, far


def series(terms, square):
    value = jnp.full_like(square, terms[-1])
    for term in terms[-2::-1]:
        value = value * square + term
    return value


def pad_lanes(value, width):
    rows, length = value.shape
    if width == length:
        return value
    return jnp.concatenate([value, jnp.zeros((rows, width - length), value.dtype)], axis=1)


def halves(value):
    hi = value.astype(BF16)
    return hi, (value - hi.astype(F32)).astype(BF16)


def step_kernel(
    segments, bands, chunk, near, far,
    fields_hbm, east_hbm, north_hbm, cutoff_hbm, damping_hbm, ship_hbm, forward_hbm, inward_hbm, result,
    cells, east, north, cutoff, damping, ship, forward, inward, facts, mix, sines, edge_pack, edge_out, edge_in,
    faces, face_columns, advected, spread, near_part, charges, arrived,
    load_sem, small_sem, halo_send, halo_recv, face_send, face_recv, send_sem, recv_sem,
):
    channels, rows_dev, length = fields_hbm.shape
    width = advected.shape[2]
    total = segments * length
    lat_count = rows_dev * bands
    chunks = rows_dev // chunk
    lines = channels * chunk
    start, ends, slots = layout(segments, near, far)
    me, band = lax.axis_index("lon"), lax.axis_index("lat")
    right, left = lax.rem(me + 1, segments), lax.rem(me + segments - 1, segments)
    peers = [lax.rem(me + p, segments) for p in range(1, segments)]
    small = [
        pltpu.make_async_copy(cutoff_hbm, cutoff, small_sem.at[0]),
        pltpu.make_async_copy(damping_hbm, damping, small_sem.at[1]),
        pltpu.make_async_copy(ship_hbm, ship, small_sem.at[2]),
        pltpu.make_async_copy(forward_hbm, forward, small_sem.at[3]),
        pltpu.make_async_copy(inward_hbm, inward, small_sem.at[4]),
    ]
    body = pl.ds(8, rows_dev)
    loads = [
        pltpu.make_async_copy(fields_hbm, cells.at[:, body], load_sem.at[0]),
        pltpu.make_async_copy(east_hbm, east, load_sem.at[1]),
        pltpu.make_async_copy(north_hbm, north.at[body], load_sem.at[2]),
    ]
    barrier = pltpu.get_barrier_semaphore()
    for peer in peers:
        pl.semaphore_signal(barrier, inc=1, device_id={"lon": peer}, device_id_type=MESH)

    @pl.when(band > 0)
    def _():
        pl.semaphore_signal(barrier, inc=1, device_id={"lat": band - 1}, device_id_type=MESH)

    @pl.when(band < bands - 1)
    def _():
        pl.semaphore_signal(barrier, inc=1, device_id={"lat": band + 1}, device_id_type=MESH)

    for load in small[:3] + loads + small[3:]:
        load.start()

    @pl.when(band == 0)
    def _():
        cells[:, 0:8, :] = jnp.zeros((channels, 8, length), F32)
        north[0:8, :] = jnp.zeros((8, length), F32)

    @pl.when(band == bands - 1)
    def _():
        cells[:, rows_dev + 8 : rows_dev + 16, :] = jnp.zeros((channels, 8, length), F32)

    def sine(k):
        z = jnp.minimum(k, lat_count - k) * (1.0 / lat_count)
        return z * series(SIN, z * z)

    def waves_at(turns):
        part = turns - jnp.floor(turns * (0.5 / total) + 0.5) * (2.0 * total)
        z = part * (1.0 / total)
        square = z * z
        return z * series(SIN, square), series(COS, square)

    for r in range(0, rows_dev, 8):
        row = (band * rows_dev + r + lax.broadcasted_iota(jnp.int32, (8, 128), 0)).astype(F32)
        inverse = 1.0 / sine(row + 0.5)
        facts[0, r : r + 8, :] = jnp.where(row < lat_count - 1, sine(row + 1.0), 0.0) * inverse
        facts[1, r : r + 8, :] = jnp.where(row > 0, sine(row), 0.0) * inverse

    for load in small[:3]:
        load.wait()
    repeat = width // 128

    def wide(value):
        return jnp.concatenate([value] * repeat, axis=1)

    column = lax.broadcasted_iota(jnp.int32, (BLOCK, width), 1)
    place = (me * length + column).astype(F32)
    every = lax.broadcasted_iota(jnp.int32, (BLOCK, lat_count), 1)
    local = lax.broadcasted_iota(jnp.int32, (BLOCK, lat_count), 0)
    slot_row = lax.broadcasted_iota(jnp.int32, (BLOCK, ship.shape[2]), 0)
    for r in range(0, rows_dev, BLOCK):
        here = slice(r, r + BLOCK)
        hit = every == local + (band * rows_dev + r)
        cut = jnp.sum(jnp.where(hit, cutoff[...].astype(F32), 0.0), axis=1, keepdims=True)
        damp = jnp.sum(jnp.where(hit, damping[...], 0.0), axis=1, keepdims=True)
        listed = jnp.zeros((BLOCK, ship.shape[2]), F32)
        for d in range(bands):
            listed = listed + jnp.where(ship[band, d : d + 1, :] == slot_row + r, 1.0, 0.0)
        polar = jnp.sum(listed, axis=1, keepdims=True) > 0.0
        waves = 2.0 * cut + 1.0
        mix[0, here, :] = jnp.broadcast_to(
            jnp.where(polar, damp + (1.0 - damp) * (waves * (1.0 / total)), 1.0), (BLOCK, 128)
        )
        mix[1, here, :] = jnp.broadcast_to(jnp.where(polar, 1.0 - damp, 0.0), (BLOCK, 128))
        mix[2, here, :] = jnp.broadcast_to(waves, (BLOCK, 128))
        sines[0, here, :], sines[1, here, :] = waves_at(waves * place)

    beside = jnp.where(band > 0, 1, 0) + jnp.where(band < bands - 1, 1, 0)
    pl.semaphore_wait(barrier, segments - 1 + beside)

    def halo(source, target, slot, device):
        return pltpu.make_async_remote_copy(
            src_ref=source, dst_ref=target, send_sem=halo_send.at[slot],
            recv_sem=halo_recv.at[slot], device_id=device, device_id_type=MESH,
        )

    up = {"lat": jnp.minimum(band + 1, bands - 1)}
    down = {"lat": jnp.maximum(band - 1, 0)}
    first, last = pl.ds(0, 1), pl.ds(rows_dev - 1, 1)
    northward = [
        halo(fields_hbm.at[:, last], cells.at[:, pl.ds(7, 1)], 0, up),
        halo(north_hbm.at[last], north.at[pl.ds(7, 1)], 1, up),
    ]
    southward = halo(fields_hbm.at[:, first], cells.at[:, pl.ds(rows_dev + 8, 1)], 2, down)

    @pl.when(band < bands - 1)
    def _():
        for copy in northward:
            copy.start()

    @pl.when(band > 0)
    def _():
        southward.start()

    for load in loads:
        load.wait()
    lane = lax.broadcasted_iota(jnp.int32, (BLOCK, 128), 1)
    for r in range(0, rows_dev, BLOCK):
        packed = jnp.zeros((BLOCK, 128), F32)
        for c in range(channels):
            packed = jnp.where(lane == c, cells[c, 8 + r : 8 + r + BLOCK, 0:1], packed)
            packed = jnp.where(lane == 8 + c, cells[c, 8 + r : 8 + r + BLOCK, length - 1 : length], packed)
        edge_pack[r : r + BLOCK, :] = jnp.where(
            lane == 8 + channels, east[r : r + BLOCK, length - 1 : length], packed
        )
    edge_out[...] = edge_pack[...].T[0:16, :]
    sideways = [
        halo(edge_out.at[pl.ds(8, 8)], edge_in.at[pl.ds(8, 8)], 3, {"lon": right}),
        halo(edge_out.at[pl.ds(0, 8)], edge_in.at[pl.ds(0, 8)], 4, {"lon": left}),
    ]
    for copy in sideways:
        copy.start()
    for load in small[3:]:
        load.wait()

    def advect(k):
        for r in range(k * chunk, (k + 1) * chunk, BLOCK):
            here = slice(r, r + BLOCK)
            ce = jnp.where(column == length - 1, 0.0, pad_lanes(east[here, :], width))
            cw = pltpu.roll(ce, 1, 1)
            cn = pad_lanes(north[8 + r : 8 + r + BLOCK, :], width) * wide(facts[0, here, :])
            cs = pad_lanes(north[7 + r : 7 + r + BLOCK, :], width) * wide(facts[1, here, :])
            at_east, at_west = jnp.minimum(ce, 0.0), jnp.maximum(cw, 0.0)
            at_north, at_south = jnp.minimum(cn, 0.0), jnp.maximum(cs, 0.0)
            at_home = 1.0 - (ce - at_east) + (cw - at_west) - (cn - at_north) + (cs - at_south)
            sin, cos = sines[0, here, :], sines[1, here, :]
            for c in range(channels):
                field = pad_lanes(cells[c, 8 + r : 8 + r + BLOCK, :], width)
                upper = pad_lanes(cells[c, 9 + r : 9 + r + BLOCK, :], width)
                lower = pad_lanes(cells[c, 7 + r : 7 + r + BLOCK, :], width)
                ahead, behind = pltpu.roll(field, width - 1, 1), pltpu.roll(field, 1, 1)
                value = at_home * field - at_east * ahead + at_west * behind - at_north * upper + at_south * lower
                advected[c, here, :] = value
                line = c * chunk + r - k * chunk
                for q, wave in enumerate((sin, cos)):
                    hi, lo = halves(value * wave)
                    spread[k % 2, q * lines + line : q * lines + line + BLOCK, 0:width] = hi
                    spread[k % 2, q * lines + line : q * lines + line + BLOCK, width : 2 * width] = lo

    outward = {}

    def exchange(k):
        for p, peer in enumerate(peers):
            delta = p + 1
            count = near if delta in (1, segments - 1) else far
            source = {1: 0, segments - 1: near}.get(delta, 2 * near)
            copy = pltpu.make_async_remote_copy(
                src_ref=charges.at[k, :, pl.ds(source, count)],
                dst_ref=arrived.at[k, :, pl.ds(start[delta], count)],
                send_sem=send_sem.at[k, p],
                recv_sem=recv_sem.at[k, p],
                device_id={"lon": peer},
                device_id_type=MESH,
            )
            copy.start()
            outward[k, p] = copy

    def leave(k):
        advect(k)
        product = jnp.dot(
            spread[k % 2], forward[0 : 2 * width, :], preferred_element_type=F32
        ) + jnp.dot(spread[k % 2, :, 0:width], forward[2 * width : 3 * width, :], preferred_element_type=F32)
        for q in range(2):
            moments = product[q * lines : (q + 1) * lines, width:]
            charges[k, q] = moments.T[0 : 2 * near + far, :]
        exchange(k)
        near_part[k] = product[:, 0:width]

    for k in range(1, chunks - 1):
        leave(k)

    for copy in sideways:
        copy.wait()
    courant, courant_left = edge_out[8 + channels : 9 + channels, :], edge_in[8 + channels : 9 + channels, :]
    eastern = courant * jnp.where(courant > 0, edge_out[8:16, :], edge_in[0:8, :])
    western = courant_left * jnp.where(courant_left > 0, edge_in[8:16, :], edge_out[0:8, :])
    faces[0] = eastern
    around = []
    for p, peer in enumerate(peers):
        copy = pltpu.make_async_remote_copy(
            src_ref=faces.at[0], dst_ref=faces.at[p + 1], send_sem=face_send.at[p], recv_sem=face_recv.at[p],
            device_id={"lon": peer}, device_id_type=MESH,
        )
        copy.start()
        around.append(copy)
    face_columns[:, 0:16] = jnp.concatenate([western, eastern], axis=0).T

    @pl.when(band < bands - 1)
    def _():
        for copy in northward:
            copy.wait_send()
        southward.wait_recv()

    @pl.when(band > 0)
    def _():
        southward.wait_send()
        for copy in northward:
            copy.wait_recv()

    for k in (0, chunks - 1):
        leave(k)

    delta = lax.broadcasted_iota(jnp.int32, (2 * segments, rows_dev), 0)
    owner = me - jnp.where(delta < segments, delta, delta - segments)
    owner = jnp.where(owner < 0, owner + segments, owner) * length + jnp.where(delta < segments, length - 1, 0)
    end_waves = waves_at(mix[2].T[0 : 2 * segments, :] * owner.astype(F32))
    for copy in around:
        copy.wait_recv()
    end_charges = []
    for c in range(channels):
        face = faces[:, c, :]
        face = jnp.concatenate([-face, face[1:segments], face[0:1]], axis=0)
        end_charges.append([face * wave for wave in end_waves])

    slot = lax.broadcasted_iota(jnp.int32, (slots, lines), 0)
    bound = jnp.where(slot < ends, 2 * near + (me - 1) * far, ends + me + 1)
    bound = jnp.where(slot < ends + segments, bound, ends + segments + me + 1)
    bound = jnp.where(slot < 2 * near, jnp.where(me >= segments - 1, 2 * near, 0), bound)
    bound = jnp.where(slot < near, jnp.where(me >= 1, near, 0), bound)
    sign = jnp.where(slot < bound, 1.0, -1.0)
    deep = inward.shape[0] // 3
    for k in list(range(1, chunks - 1)) + [0, chunks - 1]:
        for p in range(segments - 1):
            outward[k, p].wait_recv()
        sums = []
        for q in range(2):
            ended = jnp.concatenate([e[q][:, k * chunk : (k + 1) * chunk] for e in end_charges], axis=1)
            gathered = jnp.concatenate([arrived[k, q], ended], axis=0)
            hi, lo = halves(pad_lanes((gathered * sign).T, deep))
            sums.append(
                jnp.dot(jnp.concatenate([hi, lo], axis=1), inward[0 : 2 * deep, :], preferred_element_type=F32)
                + jnp.dot(hi, inward[2 * deep : 3 * deep, :], preferred_element_type=F32)
            )
        for r in range(k * chunk, (k + 1) * chunk, BLOCK):
            here = slice(r, r + BLOCK)
            keep, share = wide(mix[0, here, :]), wide(mix[1, here, :])
            sin, cos = sines[0, here, :] * share, sines[1, here, :] * share
            for c in range(channels):
                line = c * chunk + r - k * chunk
                u = near_part[k, line : line + BLOCK, :] + sums[0][line : line + BLOCK, :]
                v = near_part[k, lines + line : lines + line + BLOCK, :] + sums[1][line : line + BLOCK, :]
                value = advected[c, here, :]
                value = jnp.where(column == 0, value + face_columns[here, c : c + 1], value)
                value = jnp.where(column == length - 1, value - face_columns[here, 8 + c : 9 + c], value)
                value = keep * value + (sin * v - cos * u)
                result[c, here, :] = value[:, 0:length]
    for copy in list(outward.values()) + around:
        copy.wait_send()


def per_device(fields, east_courant, north_courant, cutoff, damping, ship_rows):
    channels, rows_dev, length = fields.shape
    segments, bands = lax.axis_size("lon"), lax.axis_size("lat")
    width = ceil_to(length, 128)
    chunk = max(c for c in range(BLOCK, 49, BLOCK) if rows_dev % c == 0)
    chunks = rows_dev // chunk
    lines = channels * chunk
    forward, inward, near, far = tables(segments, length, width)
    assert channels < 8 and chunks > 2
    _, ends, _ = layout(segments, near, far)
    semaphores = pltpu.SemaphoreType.DMA((chunks, segments - 1))
    whole = pl.BlockSpec(memory_space=pl.ANY)
    return pl.pallas_call(
        functools.partial(step_kernel, segments, bands, chunk, near, far),
        out_shape=pltpu.VMEM(fields.shape, F32),
        in_specs=[whole] * 8,
        out_specs=pl.BlockSpec(memory_space=pltpu.VMEM),
        scratch_shapes=[
            pltpu.VMEM((channels, rows_dev + 16, length), F32),
            pltpu.VMEM((rows_dev, length), F32),
            pltpu.VMEM((rows_dev + 16, length), F32),
            pltpu.VMEM((1, cutoff.shape[0]), jnp.int32),
            pltpu.VMEM((1, damping.shape[0]), F32),
            pltpu.VMEM(ship_rows.shape, jnp.int32),
            pltpu.VMEM(forward.shape, BF16),
            pltpu.VMEM(inward.shape, BF16),
            pltpu.VMEM((2, rows_dev, 128), F32),
            pltpu.VMEM((3, rows_dev, 128), F32),
            pltpu.VMEM((2, rows_dev, width), F32),
            pltpu.VMEM((rows_dev, 128), F32),
            pltpu.VMEM((16, rows_dev), F32),
            pltpu.VMEM((16, rows_dev), F32),
            pltpu.VMEM((segments, 8, rows_dev), F32),
            pltpu.VMEM((rows_dev, 128), F32),
            pltpu.VMEM((channels, rows_dev, width), F32),
            pltpu.VMEM((2, 2 * lines, 2 * width), BF16),
            pltpu.VMEM((chunks, 2 * lines, width), F32),
            pltpu.VMEM((chunks, 2, 2 * near + far, lines), F32),
            pltpu.VMEM((chunks, 2, ends, lines), F32),
            pltpu.SemaphoreType.DMA((3,)),
            pltpu.SemaphoreType.DMA((5,)),
            pltpu.SemaphoreType.DMA((5,)),
            pltpu.SemaphoreType.DMA((5,)),
            pltpu.SemaphoreType.DMA((segments - 1,)),
            pltpu.SemaphoreType.DMA((segments - 1,)),
            semaphores, semaphores,
        ],
        compiler_params=pltpu.CompilerParams(
            collective_id=0, has_side_effects=True, vmem_limit_bytes=36 * 1024 * 1024
        ),
    )(
        *(
            pltpu.with_memory_space_constraint(value, pltpu.HBM)
            for value in (
                fields, east_courant, north_courant, cutoff[None, :], damping[None, :], ship_rows,
                jnp.asarray(forward), jnp.asarray(inward),
            )
        )
    )


def solution(mesh):
    placed = (P(None, "lat", "lon"), P("lat", "lon"), P("lat", "lon"), P(), P(), P())
    return jax.shard_map(
        per_device, mesh=mesh, in_specs=placed, out_specs=P(None, "lat", "lon"), check_vma=False
    )
```

```python
import functools
import math

import jax
import jax.numpy as jnp
import numpy as np
from jax import lax
from jax.experimental import pallas as pl
from jax.experimental.pallas import tpu as pltpu
from jax.sharding import PartitionSpec as P

MESH = pl.DeviceIdType.MESH
BF16 = jnp.bfloat16
F32 = jnp.float32
BLOCK = 16
SIN = (3.14159265357, -5.1677127773, 2.55016398193, -0.59926406421, 0.0821440508123,
       -0.00736648693826, 0.000461586773619, -1.89446619668e-05)
COS = (0.999999999886, -4.93480218586, 4.05871181724, -1.33526028616, 0.235320825531,
       -0.0257858087643, 0.00190432895602, -8.86909350679e-05)


def ceil_to(value, unit):
    return -(-value // unit) * unit


def elliptic_dn(fraction, complement):
    a, b = [1.0], [math.sqrt(complement)]
    c = [math.sqrt(1.0 - complement)]
    for _ in range(12):
        x, y = a[-1], b[-1]
        a.append((x + y) / 2)
        b.append(math.sqrt(x * y))
        c.append((x - y) / 2)
    phi = 2.0 ** 12 * fraction * math.pi / 2
    for i in range(12, 0, -1):
        phi = (phi + math.asin(max(-1.0, min(1.0, c[i] * math.sin(phi) / a[i])))) / 2
    return math.sqrt(1.0 - (1.0 - complement) * math.sin(phi) ** 2)


def zolotarev(a, b, c, d, count):
    gamma = (c - a) * (d - b) / ((c - b) * (d - a))
    alpha = 2 * gamma - 1 + 2 * math.sqrt(gamma * gamma - gamma)

    def moebius(z):
        q = (z + alpha) * -2.0 / ((z - 1.0) * (alpha - 1.0)) * (b - a) / (b - c)
        return (a - q * c) / (1.0 - q)

    values = [alpha * elliptic_dn((i + 0.5) / count, 1.0 / alpha ** 2) for i in range(count)]
    return [moebius(-v) for v in values], [moebius(v) for v in values]


def cosecant(total, target, source):
    away = target[None, :] - source[:, None]
    with np.errstate(divide="ignore"):
        return np.where(away == 0, 0.0, 1.0 / (total * np.sin(np.pi / total * away)))


def factor(total, length, low, high, pole):
    step = math.pi / total
    ref = pole - total / 2

    def turn(n):
        return (n - ref + total / 2) % total - total / 2

    def tangent(n):
        return math.tan(step * turn(n))

    here, there = (tangent(0), tangent(length - 1)), (tangent(low), tangent(high))
    cell = np.array([tangent(m) for m in range(length)])
    cosine = np.array([math.cos(step * turn(m)) for m in range(length)])
    source, target = np.arange(length, dtype=np.float64), np.arange(low, high + 1, dtype=np.float64)
    exact = cosecant(total, target, source)
    for count in range(8, 64, 8):
        if here[0] < there[0]:
            y, x = zolotarev(*here, *there, count)
        else:
            x, y = zolotarev(*there, *here, count)
        rows, nodes = [], []
        for k in range(count):
            angle = math.atan(y[k])
            value = math.cos(angle) / cosine
            for j in range(count):
                if j != k:
                    value = value * ((cell - y[j]) / (y[k] - y[j]))
                value = value * ((x[j] - y[k]) / (x[j] - cell))
            rows.append(value)
            nodes.append(angle / step - turn(0))
        charge, nodes = np.stack(rows, axis=1), np.array(nodes)
        if np.abs(charge @ cosecant(total, target, nodes) / exact - 1.0).max() < 2.0 ** -23:
            break
    return charge, nodes


def split3(matrix):
    hi = matrix.astype(np.float32).astype(BF16)
    lo = (matrix - hi.astype(np.float64)).astype(np.float32).astype(BF16)
    return np.concatenate([hi, hi, lo], axis=0)


def layout(segments, near, far):
    chips = segments // 2
    start = {1: near, chips - 1: 2 * near}
    for away in range(2, chips - 1):
        start[away] = 3 * near + (away - 2) * far
    ends = 3 * near + (chips - 3) * far
    return start, ends, ends + 2 * segments


def tables(segments, length, width):
    total, chip, chips = segments * length, 2 * length, segments // 2
    cells = np.arange(length, dtype=np.float64)
    beside = [
        factor(total, length, length, chip - 1, total / 2 + length),
        factor(total, length, total - length, total - 1, total / 2),
    ]
    right, right_nodes = factor(total, chip, chip, 2 * chip - 1, total / 2 + chip)
    left, left_nodes = factor(total, chip, total - chip, total - 1, total / 2)
    others, far_nodes = factor(total, chip, 2 * chip, total - chip - 1, 1.5 * chip - 0.5)
    near, far = right.shape[1], others.shape[1]
    assert left.shape[1] == near and beside[0][0].shape[1] == near and beside[1][0].shape[1] == near
    start, ends, rows = layout(segments, near, far)
    own = np.zeros((width, width))
    own[:length, :length] = cosecant(total, cells, cells)
    forward = np.zeros((2, width, ceil_to(3 * near + far, 128)))
    inward = np.zeros((2, ceil_to(rows, 128), width))
    for core in range(2):
        mine = slice(core * length, (core + 1) * length)
        blocks = [beside[core][0], right[mine], left[mine], others[mine]]
        forward[core, :length, : 3 * near + far] = np.concatenate(blocks, axis=1)
        inward[core, :near, :length] = cosecant(total, cells + (2 * core - 1) * length, beside[1 - core][1])
        for away, at in start.items():
            nodes = {1: right_nodes, chips - 1: left_nodes}.get(away, far_nodes)
            target = cells + core * length + away * chip
            inward[core, at : at + nodes.size, :length] = cosecant(total, target, nodes)
        for delta in range(segments):
            target = cells + delta * length
            inward[core, ends + delta, :length] = cosecant(total, target, np.array([length - 1.0]))[0]
            inward[core, ends + segments + delta, :length] = cosecant(total, target, np.array([0.0]))[0]
    pairs = [np.stack([split3(table[core]) for core in range(2)]) for table in (forward, inward)]
    return split3(own), *pairs, near, far


def series(terms, square):
    value = jnp.full_like(square, terms[-1])
    for term in terms[-2::-1]:
        value = value * square + term
    return value


def pad_lanes(value, width):
    rows, length = value.shape
    if width == length:
        return value
    return jnp.concatenate([value, jnp.zeros((rows, width - length), value.dtype)], axis=1)


def halves(value):
    hi = value.astype(BF16)
    return hi, (value - hi.astype(F32)).astype(BF16)


def step_kernel(
    segments, bands, chunk, near, far,
    fields_hbm, east_hbm, north_hbm, cutoff_hbm, damping_hbm, ship_hbm, own_hbm, forward_hbm, inward_hbm, result,
    cells, east, north, cutoff, damping, ship, own, forward, inward, facts, mix, sines, edge_pack, edge_out, edge_in,
    faces, face_columns, advected, spread, near_part, charges, partial, summed, arrived,
    load_sem, small_sem, halo_send, halo_recv, face_send, face_recv, side_send, side_recv,
    send_sem, recv_sem, pass_send, pass_recv,
):
    channels, rows_dev, length = fields_hbm.shape
    width = advected.shape[2]
    total = segments * length
    lat_count = rows_dev * bands
    chunks = rows_dev // chunk
    lines = channels * chunk
    start, ends, slots = layout(segments, near, far)
    me, band = lax.axis_index("lon"), lax.axis_index("lat")
    right, left = lax.rem(me + 1, segments), lax.rem(me + segments - 1, segments)
    peers = [lax.rem(me + p, segments) for p in range(1, segments)]
    chips, chip, core = segments // 2, me // 2, lax.rem(me, 2)
    sibling = {"lon": me + 1 - 2 * core}
    partners = [{"lon": 2 * lax.rem(chip + p, chips) + core} for p in range(1, chips)]
    small = [
        pltpu.make_async_copy(cutoff_hbm, cutoff, small_sem.at[0]),
        pltpu.make_async_copy(damping_hbm, damping, small_sem.at[1]),
        pltpu.make_async_copy(ship_hbm, ship, small_sem.at[2]),
        pltpu.make_async_copy(forward_hbm.at[core], forward, small_sem.at[3]),
        pltpu.make_async_copy(inward_hbm.at[core], inward, small_sem.at[4]),
        pltpu.make_async_copy(own_hbm, own, small_sem.at[5]),
    ]
    body = pl.ds(8, rows_dev)
    loads = [
        pltpu.make_async_copy(fields_hbm, cells.at[:, body], load_sem.at[0]),
        pltpu.make_async_copy(east_hbm, east, load_sem.at[1]),
        pltpu.make_async_copy(north_hbm, north.at[body], load_sem.at[2]),
    ]
    barrier = pltpu.get_barrier_semaphore()
    for peer in peers:
        pl.semaphore_signal(barrier, inc=1, device_id={"lon": peer}, device_id_type=MESH)

    @pl.when(band > 0)
    def _():
        pl.semaphore_signal(barrier, inc=1, device_id={"lat": band - 1}, device_id_type=MESH)

    @pl.when(band < bands - 1)
    def _():
        pl.semaphore_signal(barrier, inc=1, device_id={"lat": band + 1}, device_id_type=MESH)

    for load in small[:3] + loads + small[3:]:
        load.start()

    @pl.when(band == 0)
    def _():
        cells[:, 0:8, :] = jnp.zeros((channels, 8, length), F32)
        north[0:8, :] = jnp.zeros((8, length), F32)

    @pl.when(band == bands - 1)
    def _():
        cells[:, rows_dev + 8 : rows_dev + 16, :] = jnp.zeros((channels, 8, length), F32)

    def sine(k):
        z = jnp.minimum(k, lat_count - k) * (1.0 / lat_count)
        return z * series(SIN, z * z)

    def waves_at(turns):
        part = turns - jnp.floor(turns * (0.5 / total) + 0.5) * (2.0 * total)
        z = part * (1.0 / total)
        square = z * z
        return z * series(SIN, square), series(COS, square)

    for r in range(0, rows_dev, 8):
        row = (band * rows_dev + r + lax.broadcasted_iota(jnp.int32, (8, 128), 0)).astype(F32)
        inverse = 1.0 / sine(row + 0.5)
        facts[0, r : r + 8, :] = jnp.where(row < lat_count - 1, sine(row + 1.0), 0.0) * inverse
        facts[1, r : r + 8, :] = jnp.where(row > 0, sine(row), 0.0) * inverse

    for load in small[:3]:
        load.wait()
    repeat = width // 128

    def wide(value):
        return jnp.concatenate([value] * repeat, axis=1)

    column = lax.broadcasted_iota(jnp.int32, (BLOCK, width), 1)
    place = (me * length + column).astype(F32)
    every = lax.broadcasted_iota(jnp.int32, (BLOCK, lat_count), 1)
    local = lax.broadcasted_iota(jnp.int32, (BLOCK, lat_count), 0)
    slot_row = lax.broadcasted_iota(jnp.int32, (BLOCK, ship.shape[2]), 0)
    for r in range(0, rows_dev, BLOCK):
        here = slice(r, r + BLOCK)
        hit = every == local + (band * rows_dev + r)
        cut = jnp.sum(jnp.where(hit, cutoff[...].astype(F32), 0.0), axis=1, keepdims=True)
        damp = jnp.sum(jnp.where(hit, damping[...], 0.0), axis=1, keepdims=True)
        listed = jnp.zeros((BLOCK, ship.shape[2]), F32)
        for d in range(bands):
            listed = listed + jnp.where(ship[band, d : d + 1, :] == slot_row + r, 1.0, 0.0)
        polar = jnp.sum(listed, axis=1, keepdims=True) > 0.0
        waves = 2.0 * cut + 1.0
        mix[0, here, :] = jnp.broadcast_to(
            jnp.where(polar, damp + (1.0 - damp) * (waves * (1.0 / total)), 1.0), (BLOCK, 128)
        )
        mix[1, here, :] = jnp.broadcast_to(jnp.where(polar, 1.0 - damp, 0.0), (BLOCK, 128))
        mix[2, here, :] = jnp.broadcast_to(waves, (BLOCK, 128))
        sines[0, here, :], sines[1, here, :] = waves_at(waves * place)

    beside = jnp.where(band > 0, 1, 0) + jnp.where(band < bands - 1, 1, 0)
    pl.semaphore_wait(barrier, segments - 1 + beside)

    def halo(source, target, slot, device):
        return pltpu.make_async_remote_copy(
            src_ref=source, dst_ref=target, send_sem=halo_send.at[slot],
            recv_sem=halo_recv.at[slot], device_id=device, device_id_type=MESH,
        )

    up = {"lat": jnp.minimum(band + 1, bands - 1)}
    down = {"lat": jnp.maximum(band - 1, 0)}
    first, last = pl.ds(0, 1), pl.ds(rows_dev - 1, 1)
    northward = [
        halo(fields_hbm.at[:, last], cells.at[:, pl.ds(7, 1)], 0, up),
        halo(north_hbm.at[last], north.at[pl.ds(7, 1)], 1, up),
    ]
    southward = halo(fields_hbm.at[:, first], cells.at[:, pl.ds(rows_dev + 8, 1)], 2, down)

    @pl.when(band < bands - 1)
    def _():
        for copy in northward:
            copy.start()

    @pl.when(band > 0)
    def _():
        southward.start()

    for load in loads:
        load.wait()
    lane = lax.broadcasted_iota(jnp.int32, (BLOCK, 128), 1)
    for r in range(0, rows_dev, BLOCK):
        packed = jnp.zeros((BLOCK, 128), F32)
        for c in range(channels):
            packed = jnp.where(lane == c, cells[c, 8 + r : 8 + r + BLOCK, 0:1], packed)
            packed = jnp.where(lane == 8 + c, cells[c, 8 + r : 8 + r + BLOCK, length - 1 : length], packed)
        edge_pack[r : r + BLOCK, :] = jnp.where(
            lane == 8 + channels, east[r : r + BLOCK, length - 1 : length], packed
        )
    edge_out[...] = edge_pack[...].T[0:16, :]
    sideways = [
        halo(edge_out.at[pl.ds(8, 8)], edge_in.at[pl.ds(8, 8)], 3, {"lon": right}),
        halo(edge_out.at[pl.ds(0, 8)], edge_in.at[pl.ds(0, 8)], 4, {"lon": left}),
    ]
    for copy in sideways:
        copy.start()
    small[3].wait()

    def advect(k):
        for r in range(k * chunk, (k + 1) * chunk, BLOCK):
            here = slice(r, r + BLOCK)
            ce = jnp.where(column == length - 1, 0.0, pad_lanes(east[here, :], width))
            cw = pltpu.roll(ce, 1, 1)
            cn = pad_lanes(north[8 + r : 8 + r + BLOCK, :], width) * wide(facts[0, here, :])
            cs = pad_lanes(north[7 + r : 7 + r + BLOCK, :], width) * wide(facts[1, here, :])
            at_east, at_west = jnp.minimum(ce, 0.0), jnp.maximum(cw, 0.0)
            at_north, at_south = jnp.minimum(cn, 0.0), jnp.maximum(cs, 0.0)
            at_home = 1.0 - (ce - at_east) + (cw - at_west) - (cn - at_north) + (cs - at_south)
            sin, cos = sines[0, here, :], sines[1, here, :]
            for c in range(channels):
                field = pad_lanes(cells[c, 8 + r : 8 + r + BLOCK, :], width)
                upper = pad_lanes(cells[c, 9 + r : 9 + r + BLOCK, :], width)
                lower = pad_lanes(cells[c, 7 + r : 7 + r + BLOCK, :], width)
                ahead, behind = pltpu.roll(field, width - 1, 1), pltpu.roll(field, 1, 1)
                value = at_home * field - at_east * ahead + at_west * behind - at_north * upper + at_south * lower
                advected[c, here, :] = value
                line = c * chunk + r - k * chunk
                for q, wave in enumerate((sin, cos)):
                    hi, lo = halves(value * wave)
                    spread[k, q * lines + line : q * lines + line + BLOCK, 0:width] = hi
                    spread[k, q * lines + line : q * lines + line + BLOCK, width : 2 * width] = lo

    def remote(source, target, send, recv, device):
        return pltpu.make_async_remote_copy(
            src_ref=source, dst_ref=target, send_sem=send, recv_sem=recv, device_id=device, device_id_type=MESH
        )

    def matmul(source, table):
        depth = table.shape[0] // 3
        return jnp.dot(
            source[:, 0 : 2 * depth], table[0 : 2 * depth, :], preferred_element_type=F32
        ) + jnp.dot(source[:, 0:depth], table[2 * depth : 3 * depth, :], preferred_element_type=F32)

    near_rows, chip_rows = pl.ds(0, near), pl.ds(near, 2 * near + far)
    other_rows = pl.ds(near, ends - near)
    to_side, to_chips, passed = {}, {}, {}

    def leave(k):
        advect(k)
        product = matmul(spread.at[k], forward)
        for q in range(2):
            charges[k, q] = product[q * lines : (q + 1) * lines, :].T[0 : 3 * near + far, :]
        to_side[k] = [
            remote(
                charges.at[k, 1 - core, chip_rows], partial.at[k], side_send.at[k, 0], side_recv.at[k, 0], sibling
            ),
            remote(
                charges.at[k, :, near_rows], arrived.at[k, :, near_rows], side_send.at[k, 1], side_recv.at[k, 1], sibling
            ),
        ]
        for copy in to_side[k]:
            copy.start()

    def spread_out(k):
        to_side[k][0].wait_recv()
        summed[k] = partial[k] + charges[k, core, chip_rows, :]
        to_chips[k] = []
        for p, partner in enumerate(partners):
            away = p + 1
            count = near if away in (1, chips - 1) else far
            at = {1: 0, chips - 1: near}.get(away, 2 * near)
            copy = remote(
                summed.at[k, pl.ds(at, count)], arrived.at[k, core, pl.ds(start[away], count)],
                send_sem.at[k, p], recv_sem.at[k, p], partner,
            )
            copy.start()
            to_chips[k].append(copy)

    def hand_on(k):
        for copy in to_chips[k]:
            copy.wait_recv()
        passed[k] = remote(
            arrived.at[k, core, other_rows], arrived.at[k, core, other_rows], pass_send.at[k], pass_recv.at[k], sibling
        )
        passed[k].start()

    def stay(k):
        near_part[k] = matmul(spread.at[k], own)

    order = list(range(1, chunks - 1)) + [0, chunks - 1]
    inner = order[:-2]
    for i, k in enumerate(inner):
        leave(k)
        if i > 0:
            spread_out(inner[i - 1])

    for copy in sideways:
        copy.wait()
    courant, courant_left = edge_out[8 + channels : 9 + channels, :], edge_in[8 + channels : 9 + channels, :]
    eastern = courant * jnp.where(courant > 0, edge_out[8:16, :], edge_in[0:8, :])
    western = courant_left * jnp.where(courant_left > 0, edge_in[8:16, :], edge_out[0:8, :])
    faces[0] = eastern
    around = []
    for p, peer in enumerate(peers):
        copy = pltpu.make_async_remote_copy(
            src_ref=faces.at[0], dst_ref=faces.at[p + 1], send_sem=face_send.at[p], recv_sem=face_recv.at[p],
            device_id={"lon": peer}, device_id_type=MESH,
        )
        copy.start()
        around.append(copy)
    face_columns[:, 0:16] = jnp.concatenate([western, eastern], axis=0).T

    @pl.when(band < bands - 1)
    def _():
        for copy in northward:
            copy.wait_send()
        southward.wait_recv()

    @pl.when(band > 0)
    def _():
        southward.wait_send()
        for copy in northward:
            copy.wait_recv()

    spread_out(inner[-1])
    leave(order[-2])
    leave(order[-1])
    spread_out(order[-2])
    small[5].wait()
    stay(order[0])
    spread_out(order[-1])
    for k in order[1:-2]:
        stay(k)
    for k in order[:-2]:
        hand_on(k)
    for k in order[-2:]:
        stay(k)
    small[4].wait()

    delta = lax.broadcasted_iota(jnp.int32, (2 * segments, rows_dev), 0)
    owner = me - jnp.where(delta < segments, delta, delta - segments)
    owner = jnp.where(owner < 0, owner + segments, owner) * length + jnp.where(delta < segments, length - 1, 0)
    end_waves = waves_at(mix[2].T[0 : 2 * segments, :] * owner.astype(F32))
    for copy in around:
        copy.wait_recv()
    end_charges = []
    for c in range(channels):
        face = faces[:, c, :]
        face = jnp.concatenate([-face, face[1:segments], face[0:1]], axis=0)
        end_charges.append([face * wave for wave in end_waves])

    slot = lax.broadcasted_iota(jnp.int32, (slots, lines), 0)
    bound = jnp.where(slot < ends, 3 * near + (chip - 1) * far, ends + me + 1)
    bound = jnp.where(slot < ends + segments, bound, ends + segments + me + 1)
    bound = jnp.where(slot < 3 * near, jnp.where(chip >= chips - 1, 3 * near, 0), bound)
    bound = jnp.where(slot < 2 * near, jnp.where(chip >= 1, 2 * near, 0), bound)
    sign = jnp.where((slot < bound) | (slot < near), 1.0, -1.0)
    deep = inward.shape[0] // 3
    for i, k in enumerate(order):
        if i in (1, 3):
            hand_on(order[-2 + i // 2])
        to_side[k][1].wait_recv()
        passed[k].wait_recv()
        sums = []
        for q in range(2):
            ended = jnp.concatenate([e[q][:, k * chunk : (k + 1) * chunk] for e in end_charges], axis=1)
            gathered = jnp.concatenate([arrived[k, q], ended], axis=0)
            hi, lo = halves(pad_lanes((gathered * sign).T, deep))
            sums.append(
                jnp.dot(jnp.concatenate([hi, lo], axis=1), inward[0 : 2 * deep, :], preferred_element_type=F32)
                + jnp.dot(hi, inward[2 * deep : 3 * deep, :], preferred_element_type=F32)
            )
        for r in range(k * chunk, (k + 1) * chunk, BLOCK):
            here = slice(r, r + BLOCK)
            keep, share = wide(mix[0, here, :]), wide(mix[1, here, :])
            sin, cos = sines[0, here, :] * share, sines[1, here, :] * share
            for c in range(channels):
                line = c * chunk + r - k * chunk
                u = near_part[k, line : line + BLOCK, :] + sums[0][line : line + BLOCK, :]
                v = near_part[k, lines + line : lines + line + BLOCK, :] + sums[1][line : line + BLOCK, :]
                value = advected[c, here, :]
                value = jnp.where(column == 0, value + face_columns[here, c : c + 1], value)
                value = jnp.where(column == length - 1, value - face_columns[here, 8 + c : 9 + c], value)
                value = keep * value + (sin * v - cos * u)
                result[c, here, :] = value[:, 0:length]
    for k in order:
        for copy in to_side[k] + to_chips[k] + [passed[k]]:
            copy.wait_send()
    for copy in around:
        copy.wait_send()


def per_device(fields, east_courant, north_courant, cutoff, damping, ship_rows):
    channels, rows_dev, length = fields.shape
    segments, bands = lax.axis_size("lon"), lax.axis_size("lat")
    width = ceil_to(length, 128)
    chunk = max(c for c in range(BLOCK, 49, BLOCK) if rows_dev % c == 0)
    chunks = rows_dev // chunk
    lines = channels * chunk
    own, forward, inward, near, far = tables(segments, length, width)
    assert channels < 8 and chunks > 3 and segments % 2 == 0
    _, ends, _ = layout(segments, near, far)
    semaphores = pltpu.SemaphoreType.DMA((chunks, segments // 2 - 1))
    whole = pl.BlockSpec(memory_space=pl.ANY)
    return pl.pallas_call(
        functools.partial(step_kernel, segments, bands, chunk, near, far),
        out_shape=pltpu.VMEM(fields.shape, F32),
        in_specs=[whole] * 9,
        out_specs=pl.BlockSpec(memory_space=pltpu.VMEM),
        scratch_shapes=[
            pltpu.VMEM((channels, rows_dev + 16, length), F32),
            pltpu.VMEM((rows_dev, length), F32),
            pltpu.VMEM((rows_dev + 16, length), F32),
            pltpu.VMEM((1, cutoff.shape[0]), jnp.int32),
            pltpu.VMEM((1, damping.shape[0]), F32),
            pltpu.VMEM(ship_rows.shape, jnp.int32),
            pltpu.VMEM(own.shape, BF16),
            pltpu.VMEM(forward.shape[1:], BF16),
            pltpu.VMEM(inward.shape[1:], BF16),
            pltpu.VMEM((2, rows_dev, 128), F32),
            pltpu.VMEM((3, rows_dev, 128), F32),
            pltpu.VMEM((2, rows_dev, width), F32),
            pltpu.VMEM((rows_dev, 128), F32),
            pltpu.VMEM((16, rows_dev), F32),
            pltpu.VMEM((16, rows_dev), F32),
            pltpu.VMEM((segments, 8, rows_dev), F32),
            pltpu.VMEM((rows_dev, 128), F32),
            pltpu.VMEM((channels, rows_dev, width), F32),
            pltpu.VMEM((chunks, 2 * lines, 2 * width), BF16),
            pltpu.VMEM((chunks, 2 * lines, width), F32),
            pltpu.VMEM((chunks, 2, 3 * near + far, lines), F32),
            pltpu.VMEM((chunks, 2 * near + far, lines), F32),
            pltpu.VMEM((chunks, 2 * near + far, lines), F32),
            pltpu.VMEM((chunks, 2, ends, lines), F32),
            pltpu.SemaphoreType.DMA((3,)),
            pltpu.SemaphoreType.DMA((6,)),
            pltpu.SemaphoreType.DMA((5,)),
            pltpu.SemaphoreType.DMA((5,)),
            pltpu.SemaphoreType.DMA((segments - 1,)),
            pltpu.SemaphoreType.DMA((segments - 1,)),
            pltpu.SemaphoreType.DMA((chunks, 2)),
            pltpu.SemaphoreType.DMA((chunks, 2)),
            semaphores, semaphores,
            pltpu.SemaphoreType.DMA((chunks,)),
            pltpu.SemaphoreType.DMA((chunks,)),
        ],
        compiler_params=pltpu.CompilerParams(
            collective_id=0, has_side_effects=True, vmem_limit_bytes=36 * 1024 * 1024
        ),
    )(
        *(
            pltpu.with_memory_space_constraint(value, pltpu.HBM)
            for value in (
                fields, east_courant, north_courant, cutoff[None, :], damping[None, :], ship_rows,
                jnp.asarray(own), jnp.asarray(forward), jnp.asarray(inward),
            )
        )
    )


def solution(mesh):
    placed = (P(None, "lat", "lon"), P("lat", "lon"), P("lat", "lon"), P(), P(), P())
    return jax.shard_map(
        per_device, mesh=mesh, in_specs=placed, out_specs=P(None, "lat", "lon"), check_vma=False
    )
```

```python
import functools
import math

import jax
import jax.numpy as jnp
import numpy as np
from jax import lax
from jax.experimental import pallas as pl
from jax.experimental.pallas import tpu as pltpu
from jax.sharding import PartitionSpec as P

MESH = pl.DeviceIdType.MESH
BF16 = jnp.bfloat16
F32 = jnp.float32
BLOCK = 16
SIN = (3.14159265357, -5.1677127773, 2.55016398193, -0.59926406421, 0.0821440508123,
       -0.00736648693826, 0.000461586773619, -1.89446619668e-05)
COS = (0.999999999886, -4.93480218586, 4.05871181724, -1.33526028616, 0.235320825531,
       -0.0257858087643, 0.00190432895602, -8.86909350679e-05)


def ceil_to(value, unit):
    return -(-value // unit) * unit


def elliptic_dn(fraction, complement):
    a, b = [1.0], [math.sqrt(complement)]
    c = [math.sqrt(1.0 - complement)]
    for _ in range(12):
        x, y = a[-1], b[-1]
        a.append((x + y) / 2)
        b.append(math.sqrt(x * y))
        c.append((x - y) / 2)
    phi = 2.0 ** 12 * fraction * math.pi / 2
    for i in range(12, 0, -1):
        phi = (phi + math.asin(max(-1.0, min(1.0, c[i] * math.sin(phi) / a[i])))) / 2
    return math.sqrt(1.0 - (1.0 - complement) * math.sin(phi) ** 2)


def zolotarev(a, b, c, d, count):
    gamma = (c - a) * (d - b) / ((c - b) * (d - a))
    alpha = 2 * gamma - 1 + 2 * math.sqrt(gamma * gamma - gamma)

    def moebius(z):
        q = (z + alpha) * -2.0 / ((z - 1.0) * (alpha - 1.0)) * (b - a) / (b - c)
        return (a - q * c) / (1.0 - q)

    values = [alpha * elliptic_dn((i + 0.5) / count, 1.0 / alpha ** 2) for i in range(count)]
    return [moebius(-v) for v in values], [moebius(v) for v in values]


def cosecant(total, target, source):
    away = target[None, :] - source[:, None]
    with np.errstate(divide="ignore"):
        return np.where(away == 0, 0.0, 1.0 / (total * np.sin(np.pi / total * away)))


def factor(total, length, low, high, pole):
    step = math.pi / total
    ref = pole - total / 2

    def turn(n):
        return (n - ref + total / 2) % total - total / 2

    def tangent(n):
        return math.tan(step * turn(n))

    here, there = (tangent(0), tangent(length - 1)), (tangent(low), tangent(high))
    cell = np.array([tangent(m) for m in range(length)])
    cosine = np.array([math.cos(step * turn(m)) for m in range(length)])
    source, target = np.arange(length, dtype=np.float64), np.arange(low, high + 1, dtype=np.float64)
    exact = cosecant(total, target, source)
    for count in range(8, 64, 8):
        if here[0] < there[0]:
            y, x = zolotarev(*here, *there, count)
        else:
            x, y = zolotarev(*there, *here, count)
        rows, nodes = [], []
        for k in range(count):
            angle = math.atan(y[k])
            value = math.cos(angle) / cosine
            for j in range(count):
                if j != k:
                    value = value * ((cell - y[j]) / (y[k] - y[j]))
                value = value * ((x[j] - y[k]) / (x[j] - cell))
            rows.append(value)
            nodes.append(angle / step - turn(0))
        charge, nodes = np.stack(rows, axis=1), np.array(nodes)
        if np.abs(charge @ cosecant(total, target, nodes) / exact - 1.0).max() < 2.0 ** -23:
            break
    return charge, nodes


def split3(matrix):
    hi = matrix.astype(np.float32).astype(BF16)
    lo = (matrix - hi.astype(np.float64)).astype(np.float32).astype(BF16)
    return np.concatenate([hi, hi, lo], axis=0)


def layout(segments, near, far):
    chips = segments // 2
    start = {1: near, chips - 1: 2 * near}
    for away in range(2, chips - 1):
        start[away] = 3 * near + (away - 2) * far
    ends = 3 * near + (chips - 3) * far
    return start, ends, ceil_to(ends + 2 * segments, 16)


def tables(segments, length, width):
    total, chip, chips = segments * length, 2 * length, segments // 2
    cells = np.arange(length, dtype=np.float64)
    beside = [
        factor(total, length, length, chip - 1, total / 2 + length),
        factor(total, length, total - length, total - 1, total / 2),
    ]
    right, right_nodes = factor(total, chip, chip, 2 * chip - 1, total / 2 + chip)
    left, left_nodes = factor(total, chip, total - chip, total - 1, total / 2)
    others, far_nodes = factor(total, chip, 2 * chip, total - chip - 1, 1.5 * chip - 0.5)
    near, far = right.shape[1], others.shape[1]
    assert left.shape[1] == near and beside[0][0].shape[1] == near and beside[1][0].shape[1] == near
    start, ends, rows = layout(segments, near, far)
    own = np.zeros((width, width))
    own[:length, :length] = cosecant(total, cells, cells)
    forward = np.zeros((2, width, width + ceil_to(3 * near + far, 128)))
    inward = np.zeros((2, rows, width))
    for core in range(2):
        mine = slice(core * length, (core + 1) * length)
        blocks = [beside[core][0], right[mine], left[mine], others[mine]]
        forward[core, :width, :width] = own
        forward[core, :length, width : width + 3 * near + far] = np.concatenate(blocks, axis=1)
        inward[core, :near, :length] = cosecant(total, cells + (2 * core - 1) * length, beside[1 - core][1])
        for away, at in start.items():
            nodes = {1: right_nodes, chips - 1: left_nodes}.get(away, far_nodes)
            target = cells + core * length + away * chip
            inward[core, at : at + nodes.size, :length] = cosecant(total, target, nodes)
        for delta in range(segments):
            target = cells + delta * length
            inward[core, ends + delta, :length] = cosecant(total, target, np.array([length - 1.0]))[0]
            inward[core, ends + segments + delta, :length] = cosecant(total, target, np.array([0.0]))[0]
    pairs = [np.stack([split3(table[core]) for core in range(2)]) for table in (forward, inward)]
    return *pairs, near, far


def series(terms, square):
    value = jnp.full_like(square, terms[-1])
    for term in terms[-2::-1]:
        value = value * square + term
    return value


def pad_lanes(value, width):
    rows, length = value.shape
    if width == length:
        return value
    return jnp.concatenate([value, jnp.zeros((rows, width - length), value.dtype)], axis=1)


def halves(value):
    hi = value.astype(BF16)
    return hi, (value - hi.astype(F32)).astype(BF16)


def step_kernel(
    segments, bands, chunk, near, far,
    fields_hbm, east_hbm, north_hbm, cutoff_hbm, damping_hbm, ship_hbm, forward_hbm, inward_hbm, result,
    cells, east, north, cutoff, damping, ship, forward, inward, facts, mix, sines, edge_pack, edge_out, edge_in,
    faces, face_columns, advected, spread, near_part, charges, partial, summed, arrived,
    load_sem, small_sem, halo_send, halo_recv, face_send, face_recv, side_send, side_recv,
    send_sem, recv_sem, pass_send, pass_recv,
):
    channels, rows_dev, length = fields_hbm.shape
    width = advected.shape[2]
    total = segments * length
    lat_count = rows_dev * bands
    chunks = rows_dev // chunk
    lines = channels * chunk
    start, ends, slots = layout(segments, near, far)
    me, band = lax.axis_index("lon"), lax.axis_index("lat")
    right, left = lax.rem(me + 1, segments), lax.rem(me + segments - 1, segments)
    peers = [lax.rem(me + p, segments) for p in range(1, segments)]
    chips, chip, core = segments // 2, me // 2, lax.rem(me, 2)
    sibling = {"lon": me + 1 - 2 * core}
    partners = [{"lon": 2 * lax.rem(chip + p, chips) + core} for p in range(1, chips)]
    small = [
        pltpu.make_async_copy(cutoff_hbm, cutoff, small_sem.at[0]),
        pltpu.make_async_copy(damping_hbm, damping, small_sem.at[1]),
        pltpu.make_async_copy(ship_hbm, ship, small_sem.at[2]),
        pltpu.make_async_copy(forward_hbm.at[core], forward, small_sem.at[3]),
        pltpu.make_async_copy(inward_hbm.at[core], inward, small_sem.at[4]),
    ]
    body = pl.ds(8, rows_dev)
    loads = [
        pltpu.make_async_copy(fields_hbm, cells.at[:, body], load_sem.at[0]),
        pltpu.make_async_copy(east_hbm, east, load_sem.at[1]),
        pltpu.make_async_copy(north_hbm, north.at[body], load_sem.at[2]),
    ]
    barrier = pltpu.get_barrier_semaphore()
    for peer in peers:
        pl.semaphore_signal(barrier, inc=1, device_id={"lon": peer}, device_id_type=MESH)

    @pl.when(band > 0)
    def _():
        pl.semaphore_signal(barrier, inc=1, device_id={"lat": band - 1}, device_id_type=MESH)

    @pl.when(band < bands - 1)
    def _():
        pl.semaphore_signal(barrier, inc=1, device_id={"lat": band + 1}, device_id_type=MESH)

    for load in small[:3] + loads + small[3:]:
        load.start()

    @pl.when(band == 0)
    def _():
        cells[:, 0:8, :] = jnp.zeros((channels, 8, length), F32)
        north[0:8, :] = jnp.zeros((8, length), F32)

    @pl.when(band == bands - 1)
    def _():
        cells[:, rows_dev + 8 : rows_dev + 16, :] = jnp.zeros((channels, 8, length), F32)

    def sine(k):
        z = jnp.minimum(k, lat_count - k) * (1.0 / lat_count)
        return z * series(SIN, z * z)

    def waves_at(turns):
        part = turns - jnp.floor(turns * (0.5 / total) + 0.5) * (2.0 * total)
        z = part * (1.0 / total)
        square = z * z
        return z * series(SIN, square), series(COS, square)

    for r in range(0, rows_dev, 8):
        row = (band * rows_dev + r + lax.broadcasted_iota(jnp.int32, (8, 128), 0)).astype(F32)
        inverse = 1.0 / sine(row + 0.5)
        facts[0, r : r + 8, :] = jnp.where(row < lat_count - 1, sine(row + 1.0), 0.0) * inverse
        facts[1, r : r + 8, :] = jnp.where(row > 0, sine(row), 0.0) * inverse

    for load in small[:3]:
        load.wait()
    repeat = width // 128

    def wide(value):
        return jnp.concatenate([value] * repeat, axis=1)

    column = lax.broadcasted_iota(jnp.int32, (BLOCK, width), 1)
    place = (me * length + column).astype(F32)
    every = lax.broadcasted_iota(jnp.int32, (BLOCK, lat_count), 1)
    local = lax.broadcasted_iota(jnp.int32, (BLOCK, lat_count), 0)
    slot_row = lax.broadcasted_iota(jnp.int32, (BLOCK, ship.shape[2]), 0)
    for r in range(0, rows_dev, BLOCK):
        here = slice(r, r + BLOCK)
        hit = every == local + (band * rows_dev + r)
        cut = jnp.sum(jnp.where(hit, cutoff[...].astype(F32), 0.0), axis=1, keepdims=True)
        damp = jnp.sum(jnp.where(hit, damping[...], 0.0), axis=1, keepdims=True)
        listed = jnp.zeros((BLOCK, ship.shape[2]), F32)
        for d in range(bands):
            listed = listed + jnp.where(ship[band, d : d + 1, :] == slot_row + r, 1.0, 0.0)
        polar = jnp.sum(listed, axis=1, keepdims=True) > 0.0
        waves = 2.0 * cut + 1.0
        mix[0, here, :] = jnp.broadcast_to(
            jnp.where(polar, damp + (1.0 - damp) * (waves * (1.0 / total)), 1.0), (BLOCK, 128)
        )
        mix[1, here, :] = jnp.broadcast_to(jnp.where(polar, 1.0 - damp, 0.0), (BLOCK, 128))
        mix[2, here, :] = jnp.broadcast_to(waves, (BLOCK, 128))
        sines[0, here, :], sines[1, here, :] = waves_at(waves * place)

    beside = jnp.where(band > 0, 1, 0) + jnp.where(band < bands - 1, 1, 0)
    pl.semaphore_wait(barrier, segments - 1 + beside)

    def halo(source, target, slot, device):
        return pltpu.make_async_remote_copy(
            src_ref=source, dst_ref=target, send_sem=halo_send.at[slot],
            recv_sem=halo_recv.at[slot], device_id=device, device_id_type=MESH,
        )

    up = {"lat": jnp.minimum(band + 1, bands - 1)}
    down = {"lat": jnp.maximum(band - 1, 0)}
    first, last = pl.ds(0, 1), pl.ds(rows_dev - 1, 1)
    northward = [
        halo(fields_hbm.at[:, last], cells.at[:, pl.ds(7, 1)], 0, up),
        halo(north_hbm.at[last], north.at[pl.ds(7, 1)], 1, up),
    ]
    southward = halo(fields_hbm.at[:, first], cells.at[:, pl.ds(rows_dev + 8, 1)], 2, down)

    @pl.when(band < bands - 1)
    def _():
        for copy in northward:
            copy.start()

    @pl.when(band > 0)
    def _():
        southward.start()

    for load in loads:
        load.wait()
    lane = lax.broadcasted_iota(jnp.int32, (BLOCK, 128), 1)
    for r in range(0, rows_dev, BLOCK):
        packed = jnp.zeros((BLOCK, 128), F32)
        for c in range(channels):
            packed = jnp.where(lane == c, cells[c, 8 + r : 8 + r + BLOCK, 0:1], packed)
            packed = jnp.where(lane == 8 + c, cells[c, 8 + r : 8 + r + BLOCK, length - 1 : length], packed)
        edge_pack[r : r + BLOCK, :] = jnp.where(
            lane == 8 + channels, east[r : r + BLOCK, length - 1 : length], packed
        )
    edge_out[...] = edge_pack[...].T[0:16, :]
    sideways = [
        halo(edge_out.at[pl.ds(8, 8)], edge_in.at[pl.ds(8, 8)], 3, {"lon": right}),
        halo(edge_out.at[pl.ds(0, 8)], edge_in.at[pl.ds(0, 8)], 4, {"lon": left}),
    ]
    for copy in sideways:
        copy.start()
    small[3].wait()

    def advect(k):
        for r in range(k * chunk, (k + 1) * chunk, BLOCK):
            here = slice(r, r + BLOCK)
            ce = jnp.where(column == length - 1, 0.0, pad_lanes(east[here, :], width))
            cw = pltpu.roll(ce, 1, 1)
            cn = pad_lanes(north[8 + r : 8 + r + BLOCK, :], width) * wide(facts[0, here, :])
            cs = pad_lanes(north[7 + r : 7 + r + BLOCK, :], width) * wide(facts[1, here, :])
            at_east, at_west = jnp.minimum(ce, 0.0), jnp.maximum(cw, 0.0)
            at_north, at_south = jnp.minimum(cn, 0.0), jnp.maximum(cs, 0.0)
            at_home = 1.0 - (ce - at_east) + (cw - at_west) - (cn - at_north) + (cs - at_south)
            sin, cos = sines[0, here, :], sines[1, here, :]
            for c in range(channels):
                field = pad_lanes(cells[c, 8 + r : 8 + r + BLOCK, :], width)
                upper = pad_lanes(cells[c, 9 + r : 9 + r + BLOCK, :], width)
                lower = pad_lanes(cells[c, 7 + r : 7 + r + BLOCK, :], width)
                ahead, behind = pltpu.roll(field, width - 1, 1), pltpu.roll(field, 1, 1)
                value = at_home * field - at_east * ahead + at_west * behind - at_north * upper + at_south * lower
                advected[c, here, :] = value
                line = c * chunk + r - k * chunk
                for q, wave in enumerate((sin, cos)):
                    hi, lo = halves(value * wave)
                    spread[k, q * lines + line : q * lines + line + BLOCK, 0:width] = hi
                    spread[k, q * lines + line : q * lines + line + BLOCK, width : 2 * width] = lo

    def remote(source, target, send, recv, device):
        return pltpu.make_async_remote_copy(
            src_ref=source, dst_ref=target, send_sem=send, recv_sem=recv, device_id=device, device_id_type=MESH
        )

    def matmul(k, columns):
        return jnp.dot(
            spread[k], forward[0 : 2 * width, columns], preferred_element_type=F32
        ) + jnp.dot(spread[k, :, 0:width], forward[2 * width : 3 * width, columns], preferred_element_type=F32)

    near_rows, chip_rows = pl.ds(0, near), pl.ds(near, 2 * near + far)
    other_rows = pl.ds(near, ends - near)
    to_side, to_chips, passed = {}, {}, {}

    inner_columns, charge_columns = slice(0, width), slice(width, forward.shape[1])

    def charge(k, product):
        for q in range(2):
            charges[k, q] = product[q * lines : (q + 1) * lines, :].T[0 : 3 * near + far, :]

    def stay(k):
        near_part[k] = matmul(k, inner_columns)

    def both(k):
        product = matmul(k, slice(0, forward.shape[1]))
        charge(k, product[:, width:])
        near_part[k] = product[:, 0:width]

    def to_sibling(k):
        to_side[k] = [
            remote(
                charges.at[k, 1 - core, chip_rows], partial.at[k], side_send.at[k, 0], side_recv.at[k, 0], sibling
            ),
            remote(
                charges.at[k, :, near_rows], arrived.at[k, :, near_rows], side_send.at[k, 1], side_recv.at[k, 1], sibling
            ),
        ]
        for copy in to_side[k]:
            copy.start()

    def spread_out(k):
        to_side[k][0].wait_recv()
        summed[k] = partial[k] + charges[k, core, chip_rows, :]
        to_chips[k] = []
        for p, partner in enumerate(partners):
            away = p + 1
            count = near if away in (1, chips - 1) else far
            at = {1: 0, chips - 1: near}.get(away, 2 * near)
            copy = remote(
                summed.at[k, pl.ds(at, count)], arrived.at[k, core, pl.ds(start[away], count)],
                send_sem.at[k, p], recv_sem.at[k, p], partner,
            )
            copy.start()
            to_chips[k].append(copy)

    def hand_on(k):
        for copy in to_chips[k]:
            copy.wait_recv()
        passed[k] = remote(
            arrived.at[k, core, other_rows], arrived.at[k, core, other_rows], pass_send.at[k], pass_recv.at[k], sibling
        )
        passed[k].start()

    order = list(range(1, chunks - 1)) + [0, chunks - 1]
    around = []

    def meet():
        for copy in sideways:
            copy.wait()
        courant, courant_left = edge_out[8 + channels : 9 + channels, :], edge_in[8 + channels : 9 + channels, :]
        faces[0] = courant * jnp.where(courant > 0, edge_out[8:16, :], edge_in[0:8, :])
        faces[segments] = courant_left * jnp.where(courant_left > 0, edge_in[8:16, :], edge_out[0:8, :])
        for p, peer in enumerate(peers):
            copy = remote(faces.at[0], faces.at[p + 1], face_send.at[p], face_recv.at[p], {"lon": peer})
            copy.start()
            around.append(copy)

    advect(order[0])
    for i, k in enumerate(order):
        if i == chunks - 3:

            @pl.when(band < bands - 1)
            def _():
                for copy in northward:
                    copy.wait_send()
                southward.wait_recv()

            @pl.when(band > 0)
            def _():
                southward.wait_send()
                for copy in northward:
                    copy.wait_recv()

        if i < chunks - 2:
            both(k)
        else:
            charge(k, matmul(k, charge_columns))
        if i < chunks - 1:
            advect(order[i + 1])
        to_sibling(k)
        if i > 0:
            spread_out(order[i - 1])
        if i == chunks - 2:
            meet()
    stay(order[-2])
    spread_out(order[-1])
    for k in order[:-2]:
        hand_on(k)
    small[4].wait()
    stay(order[-1])
    face_columns[:, 0:16] = jnp.concatenate([faces[segments], faces[0]], axis=0).T

    delta = lax.broadcasted_iota(jnp.int32, (2 * segments, rows_dev), 0)
    owner = me - jnp.where(delta < segments, delta, delta - segments)
    owner = jnp.where(owner < 0, owner + segments, owner) * length + jnp.where(delta < segments, length - 1, 0)
    end_waves = waves_at(mix[2].T[0 : 2 * segments, :] * owner.astype(F32))
    for copy in around:
        copy.wait_recv()
    end_charges = []
    for c in range(channels):
        face = faces[0:segments, c, :]
        face = jnp.concatenate([-face, face[1:segments], face[0:1]], axis=0)
        end_charges.append([face * wave for wave in end_waves])

    slot = lax.broadcasted_iota(jnp.int32, (slots, lines), 0)
    bound = jnp.where(slot < ends, 3 * near + (chip - 1) * far, ends + me + 1)
    bound = jnp.where(slot < ends + segments, bound, ends + segments + me + 1)
    bound = jnp.where(slot < 3 * near, jnp.where(chip >= chips - 1, 3 * near, 0), bound)
    bound = jnp.where(slot < 2 * near, jnp.where(chip >= 1, 2 * near, 0), bound)
    sign = jnp.where((slot < bound) | (slot < near), 1.0, -1.0)
    for i, k in enumerate(order):
        if i in (1, 3):
            hand_on(order[-2 + i // 2])
        to_side[k][1].wait_recv()
        passed[k].wait_recv()
        sums = []
        for q in range(2):
            ended = jnp.concatenate([e[q][:, k * chunk : (k + 1) * chunk] for e in end_charges], axis=1)
            gathered = jnp.concatenate([arrived[k, q], ended, jnp.zeros((slots - ends - 2 * segments, lines), F32)], axis=0)
            hi, lo = halves(gathered * sign)
            sums.append(jnp.dot(jnp.concatenate([hi, lo, hi], axis=0).T, inward[...], preferred_element_type=F32))
        for r in range(k * chunk, (k + 1) * chunk, BLOCK):
            here = slice(r, r + BLOCK)
            keep, share = wide(mix[0, here, :]), wide(mix[1, here, :])
            sin, cos = sines[0, here, :] * share, sines[1, here, :] * share
            for c in range(channels):
                line = c * chunk + r - k * chunk
                u = near_part[k, line : line + BLOCK, :] + sums[0][line : line + BLOCK, :]
                v = near_part[k, lines + line : lines + line + BLOCK, :] + sums[1][line : line + BLOCK, :]
                value = advected[c, here, :]
                value = jnp.where(column == 0, value + face_columns[here, c : c + 1], value)
                value = jnp.where(column == length - 1, value - face_columns[here, 8 + c : 9 + c], value)
                value = keep * value + (sin * v - cos * u)
                result[c, here, :] = value[:, 0:length]
    for k in order:
        for copy in to_side[k] + to_chips[k] + [passed[k]]:
            copy.wait_send()
    for copy in around:
        copy.wait_send()


def per_device(fields, east_courant, north_courant, cutoff, damping, ship_rows):
    channels, rows_dev, length = fields.shape
    segments, bands = lax.axis_size("lon"), lax.axis_size("lat")
    width = ceil_to(length, 128)
    chunk = max(c for c in range(BLOCK, 49, BLOCK) if rows_dev % c == 0)
    chunks = rows_dev // chunk
    lines = channels * chunk
    forward, inward, near, far = tables(segments, length, width)
    assert channels < 8 and chunks > 3 and segments % 2 == 0
    _, ends, _ = layout(segments, near, far)
    semaphores = pltpu.SemaphoreType.DMA((chunks, segments // 2 - 1))
    whole = pl.BlockSpec(memory_space=pl.ANY)
    return pl.pallas_call(
        functools.partial(step_kernel, segments, bands, chunk, near, far),
        out_shape=pltpu.VMEM(fields.shape, F32),
        in_specs=[whole] * 8,
        out_specs=pl.BlockSpec(memory_space=pltpu.VMEM),
        scratch_shapes=[
            pltpu.VMEM((channels, rows_dev + 16, length), F32),
            pltpu.VMEM((rows_dev, length), F32),
            pltpu.VMEM((rows_dev + 16, length), F32),
            pltpu.VMEM((1, cutoff.shape[0]), jnp.int32),
            pltpu.VMEM((1, damping.shape[0]), F32),
            pltpu.VMEM(ship_rows.shape, jnp.int32),
            pltpu.VMEM(forward.shape[1:], BF16),
            pltpu.VMEM(inward.shape[1:], BF16),
            pltpu.VMEM((2, rows_dev, 128), F32),
            pltpu.VMEM((3, rows_dev, 128), F32),
            pltpu.VMEM((2, rows_dev, width), F32),
            pltpu.VMEM((rows_dev, 128), F32),
            pltpu.VMEM((16, rows_dev), F32),
            pltpu.VMEM((16, rows_dev), F32),
            pltpu.VMEM((segments + 1, 8, rows_dev), F32),
            pltpu.VMEM((rows_dev, 128), F32),
            pltpu.VMEM((channels, rows_dev, width), F32),
            pltpu.VMEM((chunks, 2 * lines, 2 * width), BF16),
            pltpu.VMEM((chunks, 2 * lines, width), F32),
            pltpu.VMEM((chunks, 2, 3 * near + far, lines), F32),
            pltpu.VMEM((chunks, 2 * near + far, lines), F32),
            pltpu.VMEM((chunks, 2 * near + far, lines), F32),
            pltpu.VMEM((chunks, 2, ends, lines), F32),
            pltpu.SemaphoreType.DMA((3,)),
            pltpu.SemaphoreType.DMA((5,)),
            pltpu.SemaphoreType.DMA((5,)),
            pltpu.SemaphoreType.DMA((5,)),
            pltpu.SemaphoreType.DMA((segments - 1,)),
            pltpu.SemaphoreType.DMA((segments - 1,)),
            pltpu.SemaphoreType.DMA((chunks, 2)),
            pltpu.SemaphoreType.DMA((chunks, 2)),
            semaphores, semaphores,
            pltpu.SemaphoreType.DMA((chunks,)),
            pltpu.SemaphoreType.DMA((chunks,)),
        ],
        compiler_params=pltpu.CompilerParams(
            collective_id=0, has_side_effects=True, vmem_limit_bytes=36 * 1024 * 1024
        ),
    )(
        *(
            pltpu.with_memory_space_constraint(value, pltpu.HBM)
            for value in (
                fields, east_courant, north_courant, cutoff[None, :], damping[None, :], ship_rows,
                jnp.asarray(forward), jnp.asarray(inward),
            )
        )
    )


def solution(mesh):
    placed = (P(None, "lat", "lon"), P("lat", "lon"), P("lat", "lon"), P(), P(), P())
    return jax.shard_map(
        per_device, mesh=mesh, in_specs=placed, out_specs=P(None, "lat", "lon"), check_vma=False
    )
```

```python
import functools
import math

import jax
import jax.numpy as jnp
import numpy as np
from jax import lax
from jax.experimental import pallas as pl
from jax.experimental.pallas import tpu as pltpu
from jax.sharding import PartitionSpec as P

MESH = pl.DeviceIdType.MESH
BF16 = jnp.bfloat16
F32 = jnp.float32
BLOCK = 16
SIN = (3.14159265357, -5.1677127773, 2.55016398193, -0.59926406421, 0.0821440508123,
       -0.00736648693826, 0.000461586773619, -1.89446619668e-05)
COS = (0.999999999886, -4.93480218586, 4.05871181724, -1.33526028616, 0.235320825531,
       -0.0257858087643, 0.00190432895602, -8.86909350679e-05)


def ceil_to(value, unit):
    return -(-value // unit) * unit


def elliptic_dn(fraction, complement):
    a, b = [1.0], [math.sqrt(complement)]
    c = [math.sqrt(1.0 - complement)]
    for _ in range(12):
        x, y = a[-1], b[-1]
        a.append((x + y) / 2)
        b.append(math.sqrt(x * y))
        c.append((x - y) / 2)
    phi = 2.0 ** 12 * fraction * math.pi / 2
    for i in range(12, 0, -1):
        phi = (phi + math.asin(max(-1.0, min(1.0, c[i] * math.sin(phi) / a[i])))) / 2
    return math.sqrt(1.0 - (1.0 - complement) * math.sin(phi) ** 2)


def zolotarev(a, b, c, d, count):
    gamma = (c - a) * (d - b) / ((c - b) * (d - a))
    alpha = 2 * gamma - 1 + 2 * math.sqrt(gamma * gamma - gamma)

    def moebius(z):
        q = (z + alpha) * -2.0 / ((z - 1.0) * (alpha - 1.0)) * (b - a) / (b - c)
        return (a - q * c) / (1.0 - q)

    values = [alpha * elliptic_dn((i + 0.5) / count, 1.0 / alpha ** 2) for i in range(count)]
    return [moebius(-v) for v in values], [moebius(v) for v in values]


def cosecant(total, target, source):
    away = target[None, :] - source[:, None]
    with np.errstate(divide="ignore"):
        return np.where(away == 0, 0.0, 1.0 / (total * np.sin(np.pi / total * away)))


def factor(total, length, low, high, pole):
    step = math.pi / total
    ref = pole - total / 2

    def turn(n):
        return (n - ref + total / 2) % total - total / 2

    def tangent(n):
        return math.tan(step * turn(n))

    here, there = (tangent(0), tangent(length - 1)), (tangent(low), tangent(high))
    cell = np.array([tangent(m) for m in range(length)])
    cosine = np.array([math.cos(step * turn(m)) for m in range(length)])
    source, target = np.arange(length, dtype=np.float64), np.arange(low, high + 1, dtype=np.float64)
    exact = cosecant(total, target, source)
    for count in range(8, 64, 8):
        if here[0] < there[0]:
            y, x = zolotarev(*here, *there, count)
        else:
            x, y = zolotarev(*there, *here, count)
        rows, nodes = [], []
        for k in range(count):
            angle = math.atan(y[k])
            value = math.cos(angle) / cosine
            for j in range(count):
                if j != k:
                    value = value * ((cell - y[j]) / (y[k] - y[j]))
                value = value * ((x[j] - y[k]) / (x[j] - cell))
            rows.append(value)
            nodes.append(angle / step - turn(0))
        charge, nodes = np.stack(rows, axis=1), np.array(nodes)
        if np.abs(charge @ cosecant(total, target, nodes) / exact - 1.0).max() < 2.0 ** -23:
            break
    return charge, nodes


def split3(matrix):
    hi = matrix.astype(np.float32).astype(BF16)
    lo = (matrix - hi.astype(np.float64)).astype(np.float32).astype(BF16)
    return np.concatenate([hi, hi, lo], axis=0)


def layout(segments, near, far):
    chips = segments // 2
    start = {1: near, chips - 1: 2 * near}
    for away in range(2, chips - 1):
        start[away] = 3 * near + (away - 2) * far
    ends = 3 * near + (chips - 3) * far
    return start, ends, ceil_to(ends + 2 * segments, 16)


def tables(segments, length, width):
    total, chip, chips = segments * length, 2 * length, segments // 2
    cells = np.arange(length, dtype=np.float64)
    beside = [
        factor(total, length, length, chip - 1, total / 2 + length),
        factor(total, length, total - length, total - 1, total / 2),
    ]
    right, right_nodes = factor(total, chip, chip, 2 * chip - 1, total / 2 + chip)
    left, left_nodes = factor(total, chip, total - chip, total - 1, total / 2)
    others, far_nodes = factor(total, chip, 2 * chip, total - chip - 1, 1.5 * chip - 0.5)
    near, far = right.shape[1], others.shape[1]
    assert left.shape[1] == near and beside[0][0].shape[1] == near and beside[1][0].shape[1] == near
    start, ends, rows = layout(segments, near, far)
    own = np.zeros((width, width))
    own[:length, :length] = cosecant(total, cells, cells)
    forward = np.zeros((2, width, width + ceil_to(3 * near + far, 128)))
    inward = np.zeros((2, rows, width))
    for core in range(2):
        mine = slice(core * length, (core + 1) * length)
        blocks = [beside[core][0], right[mine], left[mine], others[mine]]
        forward[core, :width, :width] = own
        forward[core, :length, width : width + 3 * near + far] = np.concatenate(blocks, axis=1)
        inward[core, :near, :length] = cosecant(total, cells + (2 * core - 1) * length, beside[1 - core][1])
        for away, at in start.items():
            nodes = {1: right_nodes, chips - 1: left_nodes}.get(away, far_nodes)
            target = cells + core * length + away * chip
            inward[core, at : at + nodes.size, :length] = cosecant(total, target, nodes)
        for delta in range(segments):
            target = cells + delta * length
            inward[core, ends + delta, :length] = cosecant(total, target, np.array([length - 1.0]))[0]
            inward[core, ends + segments + delta, :length] = cosecant(total, target, np.array([0.0]))[0]
    pairs = [np.stack([split3(table[core]) for core in range(2)]) for table in (forward, inward)]
    return *pairs, near, far


def series(terms, square):
    value = jnp.full_like(square, terms[-1])
    for term in terms[-2::-1]:
        value = value * square + term
    return value


def pad_lanes(value, width):
    rows, length = value.shape
    if width == length:
        return value
    return jnp.concatenate([value, jnp.zeros((rows, width - length), value.dtype)], axis=1)


def halves(value):
    hi = value.astype(BF16)
    return hi, (value - hi.astype(F32)).astype(BF16)


def step_kernel(
    segments, bands, groups, near, far,
    fields_hbm, east_hbm, north_hbm, cutoff_hbm, damping_hbm, ship_hbm, forward_hbm, inward_hbm, result,
    cells, east, north, cutoff, damping, ship, forward, inward, facts, mix, sines, edge_pack, edge_out, edge_in,
    faces, face_columns, advected, spread, near_part, charges, kept, partial, summed, arrived,
    load_sem, small_sem, halo_send, halo_recv, face_send, face_recv, side_send, side_recv,
    send_sem, recv_sem, pass_send, pass_recv,
):
    channels, rows_dev, length = fields_hbm.shape
    width = advected.shape[2]
    total = segments * length
    lat_count = rows_dev * bands
    start, ends, slots = layout(segments, near, far)
    me, band = lax.axis_index("lon"), lax.axis_index("lat")
    right, left = lax.rem(me + 1, segments), lax.rem(me + segments - 1, segments)
    peers = [lax.rem(me + p, segments) for p in range(1, segments)]
    chips, chip, core = segments // 2, me // 2, lax.rem(me, 2)
    sibling = {"lon": me + 1 - 2 * core}
    partners = [{"lon": 2 * lax.rem(chip + p, chips) + core} for p in range(1, chips)]
    small = [
        pltpu.make_async_copy(cutoff_hbm, cutoff, small_sem.at[0]),
        pltpu.make_async_copy(damping_hbm, damping, small_sem.at[1]),
        pltpu.make_async_copy(ship_hbm, ship, small_sem.at[2]),
        pltpu.make_async_copy(forward_hbm.at[core], forward, small_sem.at[3]),
        pltpu.make_async_copy(inward_hbm.at[core], inward, small_sem.at[4]),
    ]
    body = pl.ds(8, rows_dev)
    loads = [
        pltpu.make_async_copy(fields_hbm, cells.at[:, body], load_sem.at[0]),
        pltpu.make_async_copy(east_hbm, east, load_sem.at[1]),
        pltpu.make_async_copy(north_hbm, north.at[body], load_sem.at[2]),
    ]
    barrier = pltpu.get_barrier_semaphore()
    for peer in peers:
        pl.semaphore_signal(barrier, inc=1, device_id={"lon": peer}, device_id_type=MESH)

    @pl.when(band > 0)
    def _():
        pl.semaphore_signal(barrier, inc=1, device_id={"lat": band - 1}, device_id_type=MESH)

    @pl.when(band < bands - 1)
    def _():
        pl.semaphore_signal(barrier, inc=1, device_id={"lat": band + 1}, device_id_type=MESH)

    for load in small[:3] + loads + small[3:]:
        load.start()

    @pl.when(band == 0)
    def _():
        cells[:, 0:8, :] = jnp.zeros((channels, 8, length), F32)
        north[0:8, :] = jnp.zeros((8, length), F32)

    @pl.when(band == bands - 1)
    def _():
        cells[:, rows_dev + 8 : rows_dev + 16, :] = jnp.zeros((channels, 8, length), F32)

    def sine(k):
        z = jnp.minimum(k, lat_count - k) * (1.0 / lat_count)
        return z * series(SIN, z * z)

    def waves_at(turns):
        part = turns - jnp.floor(turns * (0.5 / total) + 0.5) * (2.0 * total)
        z = part * (1.0 / total)
        square = z * z
        return z * series(SIN, square), series(COS, square)

    for r in range(0, rows_dev, 8):
        row = (band * rows_dev + r + lax.broadcasted_iota(jnp.int32, (8, 128), 0)).astype(F32)
        inverse = 1.0 / sine(row + 0.5)
        facts[0, r : r + 8, :] = jnp.where(row < lat_count - 1, sine(row + 1.0), 0.0) * inverse
        facts[1, r : r + 8, :] = jnp.where(row > 0, sine(row), 0.0) * inverse

    for load in small[:3]:
        load.wait()
    repeat = width // 128

    def wide(value):
        return jnp.concatenate([value] * repeat, axis=1)

    column = lax.broadcasted_iota(jnp.int32, (BLOCK, width), 1)
    place = (me * length + column).astype(F32)
    every = lax.broadcasted_iota(jnp.int32, (BLOCK, lat_count), 1)
    local = lax.broadcasted_iota(jnp.int32, (BLOCK, lat_count), 0)
    slot_row = lax.broadcasted_iota(jnp.int32, (BLOCK, ship.shape[2]), 0)
    for r in range(0, rows_dev, BLOCK):
        here = slice(r, r + BLOCK)
        hit = every == local + (band * rows_dev + r)
        cut = jnp.sum(jnp.where(hit, cutoff[...].astype(F32), 0.0), axis=1, keepdims=True)
        damp = jnp.sum(jnp.where(hit, damping[...], 0.0), axis=1, keepdims=True)
        listed = jnp.zeros((BLOCK, ship.shape[2]), F32)
        for d in range(bands):
            listed = listed + jnp.where(ship[band, d : d + 1, :] == slot_row + r, 1.0, 0.0)
        polar = jnp.sum(listed, axis=1, keepdims=True) > 0.0
        waves = 2.0 * cut + 1.0
        mix[0, here, :] = jnp.broadcast_to(
            jnp.where(polar, damp + (1.0 - damp) * (waves * (1.0 / total)), 1.0), (BLOCK, 128)
        )
        mix[1, here, :] = jnp.broadcast_to(jnp.where(polar, 1.0 - damp, 0.0), (BLOCK, 128))
        mix[2, here, :] = jnp.broadcast_to(waves, (BLOCK, 128))
        sines[0, here, :], sines[1, here, :] = waves_at(waves * place)

    beside = jnp.where(band > 0, 1, 0) + jnp.where(band < bands - 1, 1, 0)
    pl.semaphore_wait(barrier, segments - 1 + beside)

    def halo(source, target, slot, device):
        return pltpu.make_async_remote_copy(
            src_ref=source, dst_ref=target, send_sem=halo_send.at[slot],
            recv_sem=halo_recv.at[slot], device_id=device, device_id_type=MESH,
        )

    up = {"lat": jnp.minimum(band + 1, bands - 1)}
    down = {"lat": jnp.maximum(band - 1, 0)}
    first, last = pl.ds(0, 1), pl.ds(rows_dev - 1, 1)
    northward = [
        halo(fields_hbm.at[:, last], cells.at[:, pl.ds(7, 1)], 0, up),
        halo(north_hbm.at[last], north.at[pl.ds(7, 1)], 1, up),
    ]
    southward = halo(fields_hbm.at[:, first], cells.at[:, pl.ds(rows_dev + 8, 1)], 2, down)

    @pl.when(band < bands - 1)
    def _():
        for copy in northward:
            copy.start()

    @pl.when(band > 0)
    def _():
        southward.start()

    for load in loads:
        load.wait()
    lane = lax.broadcasted_iota(jnp.int32, (BLOCK, 128), 1)
    for r in range(0, rows_dev, BLOCK):
        packed = jnp.zeros((BLOCK, 128), F32)
        for c in range(channels):
            packed = jnp.where(lane == c, cells[c, 8 + r : 8 + r + BLOCK, 0:1], packed)
            packed = jnp.where(lane == 8 + c, cells[c, 8 + r : 8 + r + BLOCK, length - 1 : length], packed)
        edge_pack[r : r + BLOCK, :] = jnp.where(
            lane == 8 + channels, east[r : r + BLOCK, length - 1 : length], packed
        )
    edge_out[...] = edge_pack[...].T[0:16, :]
    sideways = [
        halo(edge_out.at[pl.ds(8, 8)], edge_in.at[pl.ds(8, 8)], 3, {"lon": right}),
        halo(edge_out.at[pl.ds(0, 8)], edge_in.at[pl.ds(0, 8)], 4, {"lon": left}),
    ]
    for copy in sideways:
        copy.start()
    small[3].wait()

    lines = [channels * BLOCK * len(group) for group in groups]

    def advect(k):
        for b, r in enumerate(groups[k]):
            here = slice(r, r + BLOCK)
            ce = jnp.where(column == length - 1, 0.0, pad_lanes(east[here, :], width))
            cw = pltpu.roll(ce, 1, 1)
            cn = pad_lanes(north[8 + r : 8 + r + BLOCK, :], width) * wide(facts[0, here, :])
            cs = pad_lanes(north[7 + r : 7 + r + BLOCK, :], width) * wide(facts[1, here, :])
            at_east, at_west = jnp.minimum(ce, 0.0), jnp.maximum(cw, 0.0)
            at_north, at_south = jnp.minimum(cn, 0.0), jnp.maximum(cs, 0.0)
            at_home = 1.0 - (ce - at_east) + (cw - at_west) - (cn - at_north) + (cs - at_south)
            sin, cos = sines[0, here, :], sines[1, here, :]
            for c in range(channels):
                field = pad_lanes(cells[c, 8 + r : 8 + r + BLOCK, :], width)
                upper = pad_lanes(cells[c, 9 + r : 9 + r + BLOCK, :], width)
                lower = pad_lanes(cells[c, 7 + r : 7 + r + BLOCK, :], width)
                ahead, behind = pltpu.roll(field, width - 1, 1), pltpu.roll(field, 1, 1)
                value = at_home * field - at_east * ahead + at_west * behind - at_north * upper + at_south * lower
                advected[c, here, :] = value
                line = (c * len(groups[k]) + b) * BLOCK
                for q, wave in enumerate((sin, cos)):
                    hi, lo = halves(value * wave)
                    spread[k][q * lines[k] + line : q * lines[k] + line + BLOCK, 0:width] = hi
                    spread[k][q * lines[k] + line : q * lines[k] + line + BLOCK, width : 2 * width] = lo

    def remote(source, target, send, recv, device):
        return pltpu.make_async_remote_copy(
            src_ref=source, dst_ref=target, send_sem=send, recv_sem=recv, device_id=device, device_id_type=MESH
        )

    def matmul(k, columns):
        return jnp.dot(
            spread[k][...], forward[0 : 2 * width, columns], preferred_element_type=F32
        ) + jnp.dot(spread[k][:, 0:width], forward[2 * width : 3 * width, columns], preferred_element_type=F32)

    inner_columns, charge_columns = slice(0, width), slice(width, forward.shape[1])
    to_side, to_chips, passed, around = {}, {}, {}, []

    def charge(k, product):
        sine_part, cosine_part = (product[q * lines[k] : (q + 1) * lines[k], :].T for q in range(2))
        charges[k][0:near, :] = sine_part[0:near, :]
        charges[k][near : 2 * near, :] = cosine_part[0:near, :]
        sine_part, cosine_part = (part[near : 3 * near + far, :] for part in (sine_part, cosine_part))
        charges[k][2 * near :, :] = jnp.where(core == 0, cosine_part, sine_part)
        kept[k][...] = jnp.where(core == 0, sine_part, cosine_part)

    def stay(k):
        near_part[k][...] = matmul(k, inner_columns)

    def both(k):
        product = matmul(k, slice(0, forward.shape[1]))
        charge(k, product[:, width:])
        near_part[k][...] = product[:, 0:width]

    def to_sibling(k):
        to_side[k] = remote(charges[k], partial[k], side_send.at[k], side_recv.at[k], sibling)
        to_side[k].start()

    def spread_out(k):
        to_side[k].wait_recv()
        summed[k][...] = partial[k][2 * near :, :] + kept[k][...]
        to_chips[k] = []
        for p, partner in enumerate(partners):
            away = p + 1
            size = near if away in (1, chips - 1) else far
            at = {1: 0, chips - 1: near}.get(away, 2 * near)
            copy = remote(
                summed[k].at[pl.ds(at, size)], arrived[k].at[core, pl.ds(start[away] - near, size)],
                send_sem.at[k, p], recv_sem.at[k, p], partner,
            )
            copy.start()
            to_chips[k].append(copy)

    def hand_on(k):
        for copy in to_chips[k]:
            copy.wait_recv()
        passed[k] = remote(arrived[k].at[core], arrived[k].at[core], pass_send.at[k], pass_recv.at[k], sibling)
        passed[k].start()

    def meet():
        for copy in sideways:
            copy.wait()
        courant, courant_left = edge_out[8 + channels : 9 + channels, :], edge_in[8 + channels : 9 + channels, :]
        faces[0] = courant * jnp.where(courant > 0, edge_out[8:16, :], edge_in[0:8, :])
        faces[segments] = courant_left * jnp.where(courant_left > 0, edge_in[8:16, :], edge_out[0:8, :])
        for p, peer in enumerate(peers):
            copy = remote(faces.at[0], faces.at[p + 1], face_send.at[p], face_recv.at[p], {"lon": peer})
            copy.start()
            around.append(copy)

    count = len(groups)
    advect(0)
    for k in range(count):
        if k == count - 3:

            @pl.when(band < bands - 1)
            def _():
                for copy in northward:
                    copy.wait_send()
                southward.wait_recv()

            @pl.when(band > 0)
            def _():
                southward.wait_send()
                for copy in northward:
                    copy.wait_recv()

        if k < count - 2:
            both(k)
        else:
            charge(k, matmul(k, charge_columns))
        if k < count - 1:
            advect(k + 1)
        to_sibling(k)
        if k > 0:
            spread_out(k - 1)
        if k == count - 4:
            meet()
    stay(count - 2)
    spread_out(count - 1)
    hand_on(0)
    small[4].wait()
    stay(count - 1)
    for k in range(1, count - 2):
        hand_on(k)
    face_columns[:, 0:16] = jnp.concatenate([faces[segments], faces[0]], axis=0).T

    delta = lax.broadcasted_iota(jnp.int32, (2 * segments, rows_dev), 0)
    owner = me - jnp.where(delta < segments, delta, delta - segments)
    owner = jnp.where(owner < 0, owner + segments, owner) * length + jnp.where(delta < segments, length - 1, 0)
    end_waves = waves_at(mix[2].T[0 : 2 * segments, :] * owner.astype(F32))
    for copy in around:
        copy.wait_recv()
    end_charges = []
    for c in range(channels):
        face = faces[0:segments, c, :]
        face = jnp.concatenate([-face, face[1:segments], face[0:1]], axis=0)
        end_charges.append([face * wave for wave in end_waves])

    def signs(k):
        slot = lax.broadcasted_iota(jnp.int32, (slots, lines[k]), 0)
        bound = jnp.where(slot < ends, 3 * near + (chip - 1) * far, ends + me + 1)
        bound = jnp.where(slot < ends + segments, bound, ends + segments + me + 1)
        bound = jnp.where(slot < 3 * near, jnp.where(chip >= chips - 1, 3 * near, 0), bound)
        bound = jnp.where(slot < 2 * near, jnp.where(chip >= 1, 2 * near, 0), bound)
        return jnp.where((slot < bound) | (slot < near), 1.0, -1.0)

    def finish(k):
        sign, sums = signs(k), []
        spare = jnp.zeros((slots - ends - 2 * segments, lines[k]), F32)
        for q in range(2):
            ended = jnp.concatenate([end[q][:, r : r + BLOCK] for end in end_charges for r in groups[k]], axis=1)
            gathered = jnp.concatenate([partial[k][q * near : (q + 1) * near, :], arrived[k][q], ended, spare], axis=0)
            hi, lo = halves(gathered * sign)
            sums.append(jnp.dot(jnp.concatenate([hi, lo, hi], axis=0).T, inward[...], preferred_element_type=F32))
        for b, r in enumerate(groups[k]):
            here = slice(r, r + BLOCK)
            keep, share = wide(mix[0, here, :]), wide(mix[1, here, :])
            sin, cos = sines[0, here, :] * share, sines[1, here, :] * share
            for c in range(channels):
                line = (c * len(groups[k]) + b) * BLOCK
                u = near_part[k][line : line + BLOCK, :] + sums[0][line : line + BLOCK, :]
                v = near_part[k][lines[k] + line : lines[k] + line + BLOCK, :] + sums[1][line : line + BLOCK, :]
                value = advected[c, here, :]
                value = jnp.where(column == 0, value + face_columns[here, c : c + 1], value)
                value = jnp.where(column == length - 1, value - face_columns[here, 8 + c : 9 + c], value)
                value = keep * value + (sin * v - cos * u)
                result[c, here, :] = value[:, 0:length]

    for k in range(count):
        if k in (1, 3):
            hand_on(count - 2 + k // 2)
        passed[k].wait_recv()
        finish(k)
    for k in range(len(groups)):
        for copy in [to_side[k], *to_chips[k], passed[k]]:
            copy.wait_send()
    for copy in around:
        copy.wait_send()


def per_device(fields, east_courant, north_courant, cutoff, damping, ship_rows):
    channels, rows_dev, length = fields.shape
    segments, bands = lax.axis_size("lon"), lax.axis_size("lat")
    width = ceil_to(length, 128)
    blocks = rows_dev // BLOCK
    outer = blocks // 5
    rows = [BLOCK * b for b in range(blocks)]
    inner = [rows[at : min(at + outer, blocks - outer)] for at in range(outer, blocks - outer, outer)]
    groups = inner + [rows[:outer], rows[-outer:]]
    lines = [channels * BLOCK * len(group) for group in groups]
    forward, inward, near, far = tables(segments, length, width)
    assert channels < 8 and outer > 0 and rows_dev % BLOCK == 0 and segments % 2 == 0
    _, ends, _ = layout(segments, near, far)
    semaphores = pltpu.SemaphoreType.DMA((len(groups), segments // 2 - 1))
    semaphore = pltpu.SemaphoreType.DMA((len(groups),))
    whole = pl.BlockSpec(memory_space=pl.ANY)
    return pl.pallas_call(
        functools.partial(step_kernel, segments, bands, groups, near, far),
        out_shape=pltpu.VMEM(fields.shape, F32),
        in_specs=[whole] * 8,
        out_specs=pl.BlockSpec(memory_space=pltpu.VMEM),
        scratch_shapes=[
            pltpu.VMEM((channels, rows_dev + 16, length), F32),
            pltpu.VMEM((rows_dev, length), F32),
            pltpu.VMEM((rows_dev + 16, length), F32),
            pltpu.VMEM((1, cutoff.shape[0]), jnp.int32),
            pltpu.VMEM((1, damping.shape[0]), F32),
            pltpu.VMEM(ship_rows.shape, jnp.int32),
            pltpu.VMEM(forward.shape[1:], BF16),
            pltpu.VMEM(inward.shape[1:], BF16),
            pltpu.VMEM((2, rows_dev, 128), F32),
            pltpu.VMEM((3, rows_dev, 128), F32),
            pltpu.VMEM((2, rows_dev, width), F32),
            pltpu.VMEM((rows_dev, 128), F32),
            pltpu.VMEM((16, rows_dev), F32),
            pltpu.VMEM((16, rows_dev), F32),
            pltpu.VMEM((segments + 1, 8, rows_dev), F32),
            pltpu.VMEM((rows_dev, 128), F32),
            pltpu.VMEM((channels, rows_dev, width), F32),
            [pltpu.VMEM((2 * count, 2 * width), BF16) for count in lines],
            [pltpu.VMEM((2 * count, width), F32) for count in lines],
            [pltpu.VMEM((4 * near + far, count), F32) for count in lines],
            [pltpu.VMEM((2 * near + far, count), F32) for count in lines],
            [pltpu.VMEM((4 * near + far, count), F32) for count in lines],
            [pltpu.VMEM((2 * near + far, count), F32) for count in lines],
            [pltpu.VMEM((2, ends - near, count), F32) for count in lines],
            pltpu.SemaphoreType.DMA((3,)),
            pltpu.SemaphoreType.DMA((5,)),
            pltpu.SemaphoreType.DMA((5,)),
            pltpu.SemaphoreType.DMA((5,)),
            pltpu.SemaphoreType.DMA((segments - 1,)),
            pltpu.SemaphoreType.DMA((segments - 1,)),
            semaphore, semaphore, semaphores, semaphores, semaphore, semaphore,
        ],
        compiler_params=pltpu.CompilerParams(
            collective_id=0, has_side_effects=True, vmem_limit_bytes=36 * 1024 * 1024
        ),
    )(
        *(
            pltpu.with_memory_space_constraint(value, pltpu.HBM)
            for value in (
                fields, east_courant, north_courant, cutoff[None, :], damping[None, :], ship_rows,
                jnp.asarray(forward), jnp.asarray(inward),
            )
        )
    )


def solution(mesh):
    placed = (P(None, "lat", "lon"), P("lat", "lon"), P("lat", "lon"), P(), P(), P())
    return jax.shard_map(
        per_device, mesh=mesh, in_specs=placed, out_specs=P(None, "lat", "lon"), check_vma=False
    )
```

```python
import functools
import math

import jax
import jax.numpy as jnp
import numpy as np
from jax import lax
from jax.experimental import pallas as pl
from jax.experimental.pallas import tpu as pltpu
from jax.sharding import PartitionSpec as P

MESH = pl.DeviceIdType.MESH
BF16 = jnp.bfloat16
F32 = jnp.float32
BLOCK = 16
SIN = (3.14159265357, -5.1677127773, 2.55016398193, -0.59926406421, 0.0821440508123,
       -0.00736648693826, 0.000461586773619, -1.89446619668e-05)
COS = (0.999999999886, -4.93480218586, 4.05871181724, -1.33526028616, 0.235320825531,
       -0.0257858087643, 0.00190432895602, -8.86909350679e-05)


def ceil_to(value, unit):
    return -(-value // unit) * unit


def elliptic_dn(fraction, complement):
    a, b = [1.0], [math.sqrt(complement)]
    c = [math.sqrt(1.0 - complement)]
    for _ in range(12):
        x, y = a[-1], b[-1]
        a.append((x + y) / 2)
        b.append(math.sqrt(x * y))
        c.append((x - y) / 2)
    phi = 2.0 ** 12 * fraction * math.pi / 2
    for i in range(12, 0, -1):
        phi = (phi + math.asin(max(-1.0, min(1.0, c[i] * math.sin(phi) / a[i])))) / 2
    return math.sqrt(1.0 - (1.0 - complement) * math.sin(phi) ** 2)


def zolotarev(a, b, c, d, count):
    gamma = (c - a) * (d - b) / ((c - b) * (d - a))
    alpha = 2 * gamma - 1 + 2 * math.sqrt(gamma * gamma - gamma)

    def moebius(z):
        q = (z + alpha) * -2.0 / ((z - 1.0) * (alpha - 1.0)) * (b - a) / (b - c)
        return (a - q * c) / (1.0 - q)

    values = [alpha * elliptic_dn((i + 0.5) / count, 1.0 / alpha ** 2) for i in range(count)]
    return [moebius(-v) for v in values], [moebius(v) for v in values]


def cosecant(total, target, source):
    away = target[None, :] - source[:, None]
    with np.errstate(divide="ignore"):
        return np.where(away == 0, 0.0, 1.0 / (total * np.sin(np.pi / total * away)))


def factor(total, length, low, high, pole):
    step = math.pi / total
    ref = pole - total / 2

    def turn(n):
        return (n - ref + total / 2) % total - total / 2

    def tangent(n):
        return math.tan(step * turn(n))

    here, there = (tangent(0), tangent(length - 1)), (tangent(low), tangent(high))
    cell = np.array([tangent(m) for m in range(length)])
    cosine = np.array([math.cos(step * turn(m)) for m in range(length)])
    source, target = np.arange(length, dtype=np.float64), np.arange(low, high + 1, dtype=np.float64)
    exact = cosecant(total, target, source)
    for count in range(8, 64, 8):
        if here[0] < there[0]:
            y, x = zolotarev(*here, *there, count)
        else:
            x, y = zolotarev(*there, *here, count)
        rows, nodes = [], []
        for k in range(count):
            angle = math.atan(y[k])
            value = math.cos(angle) / cosine
            for j in range(count):
                if j != k:
                    value = value * ((cell - y[j]) / (y[k] - y[j]))
                value = value * ((x[j] - y[k]) / (x[j] - cell))
            rows.append(value)
            nodes.append(angle / step - turn(0))
        charge, nodes = np.stack(rows, axis=1), np.array(nodes)
        if np.abs(charge @ cosecant(total, target, nodes) / exact - 1.0).max() < 2.0 ** -23:
            break
    return charge, nodes


def split3(matrix):
    hi = matrix.astype(np.float32).astype(BF16)
    lo = (matrix - hi.astype(np.float64)).astype(np.float32).astype(BF16)
    return np.concatenate([hi, hi, lo], axis=0)


def layout(segments, near, far):
    chips = segments // 2
    start = {1: near, chips - 1: 2 * near}
    for away in range(2, chips - 1):
        start[away] = 3 * near + (away - 2) * far
    ends = 3 * near + (chips - 3) * far
    return start, ends, ceil_to(ends + 2 * segments, 16)


def tables(segments, length, width):
    total, chip, chips = segments * length, 2 * length, segments // 2
    cells = np.arange(length, dtype=np.float64)
    beside = [
        factor(total, length, length, chip - 1, total / 2 + length),
        factor(total, length, total - length, total - 1, total / 2),
    ]
    right, right_nodes = factor(total, chip, chip, 2 * chip - 1, total / 2 + chip)
    left, left_nodes = factor(total, chip, total - chip, total - 1, total / 2)
    others, far_nodes = factor(total, chip, 2 * chip, total - chip - 1, 1.5 * chip - 0.5)
    near, far = right.shape[1], others.shape[1]
    assert left.shape[1] == near and beside[0][0].shape[1] == near and beside[1][0].shape[1] == near
    start, ends, rows = layout(segments, near, far)
    own = np.zeros((width, width))
    own[:length, :length] = cosecant(total, cells, cells)
    forward = np.zeros((2, width, width + ceil_to(3 * near + far, 128)))
    inward = np.zeros((2, rows, width))
    for core in range(2):
        mine = slice(core * length, (core + 1) * length)
        blocks = [beside[core][0], right[mine], left[mine], others[mine]]
        forward[core, :width, :width] = own
        forward[core, :length, width : width + 3 * near + far] = np.concatenate(blocks, axis=1)
        inward[core, :near, :length] = cosecant(total, cells + (2 * core - 1) * length, beside[1 - core][1])
        for away, at in start.items():
            nodes = {1: right_nodes, chips - 1: left_nodes}.get(away, far_nodes)
            target = cells + core * length + away * chip
            inward[core, at : at + nodes.size, :length] = cosecant(total, target, nodes)
        for delta in range(segments):
            target = cells + delta * length
            inward[core, ends + delta, :length] = cosecant(total, target, np.array([length - 1.0]))[0]
            inward[core, ends + segments + delta, :length] = cosecant(total, target, np.array([0.0]))[0]
    pairs = [np.stack([split3(table[core]) for core in range(2)]) for table in (forward, inward)]
    return *pairs, near, far


def series(terms, square):
    value = jnp.full_like(square, terms[-1])
    for term in terms[-2::-1]:
        value = value * square + term
    return value


def pad_lanes(value, width):
    rows, length = value.shape
    if width == length:
        return value
    return jnp.concatenate([value, jnp.zeros((rows, width - length), value.dtype)], axis=1)


def halves(value):
    hi = value.astype(BF16)
    return hi, (value - hi.astype(F32)).astype(BF16)


def step_kernel(
    segments, bands, groups, near, far,
    fields_hbm, east_hbm, north_hbm, cutoff_hbm, damping_hbm, ship_hbm, forward_hbm, inward_hbm, result,
    cells, east, north, cutoff, damping, ship, forward, inward, facts, mix, sines, edge_pack, edge_out, edge_in,
    faces, face_columns, advected, spread, near_part, charges, kept, partial, summed, arrived,
    load_sem, small_sem, halo_send, halo_recv, face_send, face_recv, side_send, side_recv,
    send_sem, recv_sem, pass_send, pass_recv,
):
    channels, rows_dev, length = fields_hbm.shape
    width = advected.shape[2]
    total = segments * length
    lat_count = rows_dev * bands
    start, ends, slots = layout(segments, near, far)
    me, band = lax.axis_index("lon"), lax.axis_index("lat")
    right, left = lax.rem(me + 1, segments), lax.rem(me + segments - 1, segments)
    peers = [lax.rem(me + p, segments) for p in range(1, segments)]
    chips, chip, core = segments // 2, me // 2, lax.rem(me, 2)
    sibling = {"lon": me + 1 - 2 * core}
    partners = [{"lon": 2 * lax.rem(chip + p, chips) + core} for p in range(1, chips)]
    small = [
        pltpu.make_async_copy(cutoff_hbm, cutoff, small_sem.at[0]),
        pltpu.make_async_copy(damping_hbm, damping, small_sem.at[1]),
        pltpu.make_async_copy(ship_hbm, ship, small_sem.at[2]),
        pltpu.make_async_copy(forward_hbm.at[core], forward, small_sem.at[3]),
        pltpu.make_async_copy(inward_hbm.at[core], inward, small_sem.at[4]),
    ]
    body = pl.ds(8, rows_dev)
    loads = [
        pltpu.make_async_copy(fields_hbm, cells.at[:, body], load_sem.at[0]),
        pltpu.make_async_copy(east_hbm, east, load_sem.at[1]),
        pltpu.make_async_copy(north_hbm, north.at[body], load_sem.at[2]),
    ]
    barrier = pltpu.get_barrier_semaphore()
    for peer in peers:
        pl.semaphore_signal(barrier, inc=1, device_id={"lon": peer}, device_id_type=MESH)

    @pl.when(band > 0)
    def _():
        pl.semaphore_signal(barrier, inc=1, device_id={"lat": band - 1}, device_id_type=MESH)

    @pl.when(band < bands - 1)
    def _():
        pl.semaphore_signal(barrier, inc=1, device_id={"lat": band + 1}, device_id_type=MESH)

    for load in small[:3] + loads + small[3:]:
        load.start()

    @pl.when(band == 0)
    def _():
        cells[:, 0:8, :] = jnp.zeros((channels, 8, length), F32)
        north[0:8, :] = jnp.zeros((8, length), F32)

    @pl.when(band == bands - 1)
    def _():
        cells[:, rows_dev + 8 : rows_dev + 16, :] = jnp.zeros((channels, 8, length), F32)

    def sine(k):
        z = jnp.minimum(k, lat_count - k) * (1.0 / lat_count)
        return z * series(SIN, z * z)

    def waves_at(turns):
        part = turns - jnp.floor(turns * (0.5 / total) + 0.5) * (2.0 * total)
        z = part * (1.0 / total)
        square = z * z
        return z * series(SIN, square), series(COS, square)

    for r in range(0, rows_dev, 8):
        row = (band * rows_dev + r + lax.broadcasted_iota(jnp.int32, (8, 128), 0)).astype(F32)
        inverse = 1.0 / sine(row + 0.5)
        facts[0, r : r + 8, :] = jnp.where(row < lat_count - 1, sine(row + 1.0), 0.0) * inverse
        facts[1, r : r + 8, :] = jnp.where(row > 0, sine(row), 0.0) * inverse

    for load in small[:3]:
        load.wait()
    repeat = width // 128

    def wide(value):
        return jnp.concatenate([value] * repeat, axis=1)

    column = lax.broadcasted_iota(jnp.int32, (BLOCK, width), 1)
    place = (me * length + column).astype(F32)
    every = lax.broadcasted_iota(jnp.int32, (BLOCK, lat_count), 1)
    local = lax.broadcasted_iota(jnp.int32, (BLOCK, lat_count), 0)
    slot_row = lax.broadcasted_iota(jnp.int32, (BLOCK, ship.shape[2]), 0)
    for r in range(0, rows_dev, BLOCK):
        here = slice(r, r + BLOCK)
        hit = every == local + (band * rows_dev + r)
        cut = jnp.sum(jnp.where(hit, cutoff[...].astype(F32), 0.0), axis=1, keepdims=True)
        damp = jnp.sum(jnp.where(hit, damping[...], 0.0), axis=1, keepdims=True)
        listed = jnp.zeros((BLOCK, ship.shape[2]), F32)
        for d in range(bands):
            listed = listed + jnp.where(ship[band, d : d + 1, :] == slot_row + r, 1.0, 0.0)
        polar = jnp.sum(listed, axis=1, keepdims=True) > 0.0
        waves = 2.0 * cut + 1.0
        mix[0, here, :] = jnp.broadcast_to(
            jnp.where(polar, damp + (1.0 - damp) * (waves * (1.0 / total)), 1.0), (BLOCK, 128)
        )
        mix[1, here, :] = jnp.broadcast_to(jnp.where(polar, 1.0 - damp, 0.0), (BLOCK, 128))
        mix[2, here, :] = jnp.broadcast_to(waves, (BLOCK, 128))
        sines[0, here, :], sines[1, here, :] = waves_at(waves * place)

    beside = jnp.where(band > 0, 1, 0) + jnp.where(band < bands - 1, 1, 0)
    pl.semaphore_wait(barrier, segments - 1 + beside)

    def halo(source, target, slot, device):
        return pltpu.make_async_remote_copy(
            src_ref=source, dst_ref=target, send_sem=halo_send.at[slot],
            recv_sem=halo_recv.at[slot], device_id=device, device_id_type=MESH,
        )

    up = {"lat": jnp.minimum(band + 1, bands - 1)}
    down = {"lat": jnp.maximum(band - 1, 0)}
    first, last = pl.ds(0, 1), pl.ds(rows_dev - 1, 1)
    northward = [
        halo(fields_hbm.at[:, last], cells.at[:, pl.ds(7, 1)], 0, up),
        halo(north_hbm.at[last], north.at[pl.ds(7, 1)], 1, up),
    ]
    southward = halo(fields_hbm.at[:, first], cells.at[:, pl.ds(rows_dev + 8, 1)], 2, down)

    @pl.when(band < bands - 1)
    def _():
        for copy in northward:
            copy.start()

    @pl.when(band > 0)
    def _():
        southward.start()

    for load in loads:
        load.wait()
    lane = lax.broadcasted_iota(jnp.int32, (BLOCK, 128), 1)
    for r in range(0, rows_dev, BLOCK):
        packed = jnp.zeros((BLOCK, 128), F32)
        for c in range(channels):
            packed = jnp.where(lane == c, cells[c, 8 + r : 8 + r + BLOCK, 0:1], packed)
            packed = jnp.where(lane == 8 + c, cells[c, 8 + r : 8 + r + BLOCK, length - 1 : length], packed)
        edge_pack[r : r + BLOCK, :] = jnp.where(
            lane == 8 + channels, east[r : r + BLOCK, length - 1 : length], packed
        )
    edge_out[...] = edge_pack[...].T[0:16, :]
    sideways = [
        halo(edge_out.at[pl.ds(8, 8)], edge_in.at[pl.ds(8, 8)], 3, {"lon": right}),
        halo(edge_out.at[pl.ds(0, 8)], edge_in.at[pl.ds(0, 8)], 4, {"lon": left}),
    ]
    for copy in sideways:
        copy.start()
    small[3].wait()

    lines = [channels * BLOCK * len(group) for group in groups]

    def advect(k):
        for b, r in enumerate(groups[k]):
            here = slice(r, r + BLOCK)
            ce = jnp.where(column == length - 1, 0.0, pad_lanes(east[here, :], width))
            cw = pltpu.roll(ce, 1, 1)
            cn = pad_lanes(north[8 + r : 8 + r + BLOCK, :], width) * wide(facts[0, here, :])
            cs = pad_lanes(north[7 + r : 7 + r + BLOCK, :], width) * wide(facts[1, here, :])
            at_east, at_west = jnp.minimum(ce, 0.0), jnp.maximum(cw, 0.0)
            at_north, at_south = jnp.minimum(cn, 0.0), jnp.maximum(cs, 0.0)
            at_home = 1.0 - (ce - at_east) + (cw - at_west) - (cn - at_north) + (cs - at_south)
            sin, cos = sines[0, here, :], sines[1, here, :]
            for c in range(channels):
                field = pad_lanes(cells[c, 8 + r : 8 + r + BLOCK, :], width)
                upper = pad_lanes(cells[c, 9 + r : 9 + r + BLOCK, :], width)
                lower = pad_lanes(cells[c, 7 + r : 7 + r + BLOCK, :], width)
                ahead, behind = pltpu.roll(field, width - 1, 1), pltpu.roll(field, 1, 1)
                value = at_home * field - at_east * ahead + at_west * behind - at_north * upper + at_south * lower
                advected[c, here, :] = value
                line = (c * len(groups[k]) + b) * BLOCK
                for q, wave in enumerate((sin, cos)):
                    hi, lo = halves(value * wave)
                    spread[k][q * lines[k] + line : q * lines[k] + line + BLOCK, 0:width] = hi
                    spread[k][q * lines[k] + line : q * lines[k] + line + BLOCK, width : 2 * width] = lo

    def remote(source, target, send, recv, device):
        return pltpu.make_async_remote_copy(
            src_ref=source, dst_ref=target, send_sem=send, recv_sem=recv, device_id=device, device_id_type=MESH
        )

    def matmul(k, columns):
        return jnp.dot(
            spread[k][...], forward[0 : 2 * width, columns], preferred_element_type=F32
        ) + jnp.dot(spread[k][:, 0:width], forward[2 * width : 3 * width, columns], preferred_element_type=F32)

    inner_columns, charge_columns = slice(0, width), slice(width, forward.shape[1])
    to_side, to_chips, passed, around = {}, {}, {}, []

    def charge(k, product):
        sine_part, cosine_part = (product[q * lines[k] : (q + 1) * lines[k], :].T for q in range(2))
        charges[k][0:near, :] = sine_part[0:near, :]
        charges[k][near : 2 * near, :] = cosine_part[0:near, :]
        sine_part, cosine_part = (part[near : 3 * near + far, :] for part in (sine_part, cosine_part))
        charges[k][2 * near :, :] = jnp.where(core == 0, cosine_part, sine_part)
        kept[k][...] = jnp.where(core == 0, sine_part, cosine_part)

    def stay(k):
        near_part[k][...] = matmul(k, inner_columns)

    def both(k):
        product = matmul(k, slice(0, forward.shape[1]))
        charge(k, product[:, width:])
        near_part[k][...] = product[:, 0:width]

    def to_sibling(k):
        to_side[k] = remote(charges[k], partial[k], side_send.at[k], side_recv.at[k], sibling)
        to_side[k].start()

    def spread_out(k):
        to_side[k].wait_recv()
        summed[k][...] = partial[k][2 * near :, :] + kept[k][...]
        to_chips[k] = []
        for p, partner in enumerate(partners):
            away = p + 1
            size = near if away in (1, chips - 1) else far
            at = {1: 0, chips - 1: near}.get(away, 2 * near)
            copy = remote(
                summed[k].at[pl.ds(at, size)], arrived[k].at[core, pl.ds(start[away] - near, size)],
                send_sem.at[k, p], recv_sem.at[k, p], partner,
            )
            copy.start()
            to_chips[k].append(copy)

    def hand_on(k):
        for copy in to_chips[k]:
            copy.wait_recv()
        passed[k] = remote(arrived[k].at[core], arrived[k].at[core], pass_send.at[k], pass_recv.at[k], sibling)
        passed[k].start()

    def meet():
        for copy in sideways:
            copy.wait()
        courant, courant_left = edge_out[8 + channels : 9 + channels, :], edge_in[8 + channels : 9 + channels, :]
        faces[0] = courant * jnp.where(courant > 0, edge_out[8:16, :], edge_in[0:8, :])
        faces[segments] = courant_left * jnp.where(courant_left > 0, edge_in[8:16, :], edge_out[0:8, :])
        for p, peer in enumerate(peers):
            copy = remote(faces.at[0], faces.at[p + 1], face_send.at[p], face_recv.at[p], {"lon": peer})
            copy.start()
            around.append(copy)

    count = len(groups)
    advect(0)
    for k in range(count):
        if k == count - 3:

            @pl.when(band < bands - 1)
            def _():
                for copy in northward:
                    copy.wait_send()
                southward.wait_recv()

            @pl.when(band > 0)
            def _():
                southward.wait_send()
                for copy in northward:
                    copy.wait_recv()

        if k < count - 2:
            both(k)
        else:
            charge(k, matmul(k, charge_columns))
        if k < count - 1:
            advect(k + 1)
        to_sibling(k)
        if k > 0:
            spread_out(k - 1)
        if k == count - 4:
            meet()
    stay(count - 2)
    spread_out(count - 1)
    hand_on(0)
    small[4].wait()
    stay(count - 1)
    for k in range(1, count - 2):
        hand_on(k)
    face_columns[:, 0:16] = jnp.concatenate([faces[segments], faces[0]], axis=0).T

    delta = lax.broadcasted_iota(jnp.int32, (2 * segments, rows_dev), 0)
    owner = me - jnp.where(delta < segments, delta, delta - segments)
    owner = jnp.where(owner < 0, owner + segments, owner) * length + jnp.where(delta < segments, length - 1, 0)
    end_waves = waves_at(mix[2].T[0 : 2 * segments, :] * owner.astype(F32))
    for copy in around:
        copy.wait_recv()
    end_charges = []
    for c in range(channels):
        face = faces[0:segments, c, :]
        face = jnp.concatenate([-face, face[1:segments], face[0:1]], axis=0)
        end_charges.append([face * wave for wave in end_waves])

    def signs(k):
        slot = lax.broadcasted_iota(jnp.int32, (slots, lines[k]), 0)
        bound = jnp.where(slot < ends, 3 * near + (chip - 1) * far, ends + me + 1)
        bound = jnp.where(slot < ends + segments, bound, ends + segments + me + 1)
        bound = jnp.where(slot < 3 * near, jnp.where(chip >= chips - 1, 3 * near, 0), bound)
        bound = jnp.where(slot < 2 * near, jnp.where(chip >= 1, 2 * near, 0), bound)
        return jnp.where((slot < bound) | (slot < near), 1.0, -1.0)

    sign_of = {size: signs(lines.index(size)) for size in lines}

    def finish(k):
        sign, sums = sign_of[lines[k]], []
        spare = jnp.zeros((slots - ends - 2 * segments, lines[k]), F32)
        for q in range(2):
            ended = jnp.concatenate([end[q][:, r : r + BLOCK] for end in end_charges for r in groups[k]], axis=1)
            gathered = jnp.concatenate([partial[k][q * near : (q + 1) * near, :], arrived[k][q], ended, spare], axis=0)
            hi, lo = halves(gathered * sign)
            sums.append(jnp.dot(jnp.concatenate([hi, lo, hi], axis=0).T, inward[...], preferred_element_type=F32))
        for b, r in enumerate(groups[k]):
            here = slice(r, r + BLOCK)
            keep, share = wide(mix[0, here, :]), wide(mix[1, here, :])
            sin, cos = sines[0, here, :] * share, sines[1, here, :] * share
            for c in range(channels):
                line = (c * len(groups[k]) + b) * BLOCK
                u = near_part[k][line : line + BLOCK, :] + sums[0][line : line + BLOCK, :]
                v = near_part[k][lines[k] + line : lines[k] + line + BLOCK, :] + sums[1][line : line + BLOCK, :]
                value = advected[c, here, :]
                value = jnp.where(column == 0, value + face_columns[here, c : c + 1], value)
                value = jnp.where(column == length - 1, value - face_columns[here, 8 + c : 9 + c], value)
                value = keep * value + (sin * v - cos * u)
                result[c, here, :] = value[:, 0:length]

    for k in range(count):
        if k in (1, 3):
            hand_on(count - 2 + k // 2)
        passed[k].wait_recv()
        finish(k)
    for k in range(len(groups)):
        for copy in [to_side[k], *to_chips[k], passed[k]]:
            copy.wait_send()
    for copy in around:
        copy.wait_send()


def per_device(fields, east_courant, north_courant, cutoff, damping, ship_rows):
    channels, rows_dev, length = fields.shape
    segments, bands = lax.axis_size("lon"), lax.axis_size("lat")
    width = ceil_to(length, 128)
    blocks = rows_dev // BLOCK
    outer = blocks // 5
    rows = [BLOCK * b for b in range(blocks)]
    inner = [rows[at : min(at + outer, blocks - outer)] for at in range(outer, blocks - outer, outer)]
    groups = inner + [rows[:outer], rows[-outer:]]
    lines = [channels * BLOCK * len(group) for group in groups]
    forward, inward, near, far = tables(segments, length, width)
    assert channels < 8 and outer > 0 and rows_dev % BLOCK == 0 and segments % 2 == 0
    _, ends, _ = layout(segments, near, far)
    semaphores = pltpu.SemaphoreType.DMA((len(groups), segments // 2 - 1))
    semaphore = pltpu.SemaphoreType.DMA((len(groups),))
    whole = pl.BlockSpec(memory_space=pl.ANY)
    return pl.pallas_call(
        functools.partial(step_kernel, segments, bands, groups, near, far),
        out_shape=pltpu.VMEM(fields.shape, F32),
        in_specs=[whole] * 8,
        out_specs=pl.BlockSpec(memory_space=pltpu.VMEM),
        scratch_shapes=[
            pltpu.VMEM((channels, rows_dev + 16, length), F32),
            pltpu.VMEM((rows_dev, length), F32),
            pltpu.VMEM((rows_dev + 16, length), F32),
            pltpu.VMEM((1, cutoff.shape[0]), jnp.int32),
            pltpu.VMEM((1, damping.shape[0]), F32),
            pltpu.VMEM(ship_rows.shape, jnp.int32),
            pltpu.VMEM(forward.shape[1:], BF16),
            pltpu.VMEM(inward.shape[1:], BF16),
            pltpu.VMEM((2, rows_dev, 128), F32),
            pltpu.VMEM((3, rows_dev, 128), F32),
            pltpu.VMEM((2, rows_dev, width), F32),
            pltpu.VMEM((rows_dev, 128), F32),
            pltpu.VMEM((16, rows_dev), F32),
            pltpu.VMEM((16, rows_dev), F32),
            pltpu.VMEM((segments + 1, 8, rows_dev), F32),
            pltpu.VMEM((rows_dev, 128), F32),
            pltpu.VMEM((channels, rows_dev, width), F32),
            [pltpu.VMEM((2 * count, 2 * width), BF16) for count in lines],
            [pltpu.VMEM((2 * count, width), F32) for count in lines],
            [pltpu.VMEM((4 * near + far, count), F32) for count in lines],
            [pltpu.VMEM((2 * near + far, count), F32) for count in lines],
            [pltpu.VMEM((4 * near + far, count), F32) for count in lines],
            [pltpu.VMEM((2 * near + far, count), F32) for count in lines],
            [pltpu.VMEM((2, ends - near, count), F32) for count in lines],
            pltpu.SemaphoreType.DMA((3,)),
            pltpu.SemaphoreType.DMA((5,)),
            pltpu.SemaphoreType.DMA((5,)),
            pltpu.SemaphoreType.DMA((5,)),
            pltpu.SemaphoreType.DMA((segments - 1,)),
            pltpu.SemaphoreType.DMA((segments - 1,)),
            semaphore, semaphore, semaphores, semaphores, semaphore, semaphore,
        ],
        compiler_params=pltpu.CompilerParams(
            collective_id=0, has_side_effects=True, vmem_limit_bytes=36 * 1024 * 1024
        ),
    )(
        *(
            pltpu.with_memory_space_constraint(value, pltpu.HBM)
            for value in (
                fields, east_courant, north_courant, cutoff[None, :], damping[None, :], ship_rows,
                jnp.asarray(forward), jnp.asarray(inward),
            )
        )
    )


def solution(mesh):
    placed = (P(None, "lat", "lon"), P("lat", "lon"), P("lat", "lon"), P(), P(), P())
    return jax.shard_map(
        per_device, mesh=mesh, in_specs=placed, out_specs=P(None, "lat", "lon"), check_vma=False
    )
```

```python
import functools
import math

import jax
import jax.numpy as jnp
import numpy as np
from jax import lax
from jax.experimental import pallas as pl
from jax.experimental.pallas import tpu as pltpu
from jax.sharding import PartitionSpec as P

MESH = pl.DeviceIdType.MESH
BF16 = jnp.bfloat16
F32 = jnp.float32
BLOCK = 16
SIN = (3.14159265357, -5.1677127773, 2.55016398193, -0.59926406421, 0.0821440508123,
       -0.00736648693826, 0.000461586773619, -1.89446619668e-05)
COS = (0.999999999886, -4.93480218586, 4.05871181724, -1.33526028616, 0.235320825531,
       -0.0257858087643, 0.00190432895602, -8.86909350679e-05)


def ceil_to(value, unit):
    return -(-value // unit) * unit


def elliptic_dn(fraction, complement):
    a, b = [1.0], [math.sqrt(complement)]
    c = [math.sqrt(1.0 - complement)]
    for _ in range(12):
        x, y = a[-1], b[-1]
        a.append((x + y) / 2)
        b.append(math.sqrt(x * y))
        c.append((x - y) / 2)
    phi = 2.0 ** 12 * fraction * math.pi / 2
    for i in range(12, 0, -1):
        phi = (phi + math.asin(max(-1.0, min(1.0, c[i] * math.sin(phi) / a[i])))) / 2
    return math.sqrt(1.0 - (1.0 - complement) * math.sin(phi) ** 2)


def zolotarev(a, b, c, d, count):
    gamma = (c - a) * (d - b) / ((c - b) * (d - a))
    alpha = 2 * gamma - 1 + 2 * math.sqrt(gamma * gamma - gamma)

    def moebius(z):
        q = (z + alpha) * -2.0 / ((z - 1.0) * (alpha - 1.0)) * (b - a) / (b - c)
        return (a - q * c) / (1.0 - q)

    values = [alpha * elliptic_dn((i + 0.5) / count, 1.0 / alpha ** 2) for i in range(count)]
    return [moebius(-v) for v in values], [moebius(v) for v in values]


def cosecant(total, target, source):
    away = target[None, :] - source[:, None]
    with np.errstate(divide="ignore"):
        return np.where(away == 0, 0.0, 1.0 / (total * np.sin(np.pi / total * away)))


def factor(total, length, low, high, pole):
    step = math.pi / total
    ref = pole - total / 2

    def turn(n):
        return (n - ref + total / 2) % total - total / 2

    def tangent(n):
        return math.tan(step * turn(n))

    here, there = (tangent(0), tangent(length - 1)), (tangent(low), tangent(high))
    cell = np.array([tangent(m) for m in range(length)])
    cosine = np.array([math.cos(step * turn(m)) for m in range(length)])
    source, target = np.arange(length, dtype=np.float64), np.arange(low, high + 1, dtype=np.float64)
    exact = cosecant(total, target, source)
    for count in range(8, 64, 8):
        if here[0] < there[0]:
            y, x = zolotarev(*here, *there, count)
        else:
            x, y = zolotarev(*there, *here, count)
        rows, nodes = [], []
        for k in range(count):
            angle = math.atan(y[k])
            value = math.cos(angle) / cosine
            for j in range(count):
                if j != k:
                    value = value * ((cell - y[j]) / (y[k] - y[j]))
                value = value * ((x[j] - y[k]) / (x[j] - cell))
            rows.append(value)
            nodes.append(angle / step - turn(0))
        charge, nodes = np.stack(rows, axis=1), np.array(nodes)
        if np.abs(charge @ cosecant(total, target, nodes) / exact - 1.0).max() < 2.0 ** -23:
            break
    return charge, nodes


def split3(matrix):
    hi = matrix.astype(np.float32).astype(BF16)
    lo = (matrix - hi.astype(np.float64)).astype(np.float32).astype(BF16)
    return np.concatenate([hi, hi, lo], axis=0)


def layout(segments, near, far):
    chips = segments // 2
    start = {1: near, chips - 1: 2 * near}
    for away in range(2, chips - 1):
        start[away] = 3 * near + (away - 2) * far
    ends = 3 * near + (chips - 3) * far
    return start, ends, ceil_to(ends + 2 * segments, 16)


def tables(segments, length, width):
    total, chip, chips = segments * length, 2 * length, segments // 2
    cells = np.arange(length, dtype=np.float64)
    beside = [
        factor(total, length, length, chip - 1, total / 2 + length),
        factor(total, length, total - length, total - 1, total / 2),
    ]
    right, right_nodes = factor(total, chip, chip, 2 * chip - 1, total / 2 + chip)
    left, left_nodes = factor(total, chip, total - chip, total - 1, total / 2)
    others, far_nodes = factor(total, chip, 2 * chip, total - chip - 1, 1.5 * chip - 0.5)
    near, far = right.shape[1], others.shape[1]
    assert left.shape[1] == near and beside[0][0].shape[1] == near and beside[1][0].shape[1] == near
    start, ends, rows = layout(segments, near, far)
    own = np.zeros((width, width))
    own[:length, :length] = cosecant(total, cells, cells)
    forward = np.zeros((2, width, width + ceil_to(3 * near + far, 128)))
    inward = np.zeros((2, rows, width))
    for core in range(2):
        mine = slice(core * length, (core + 1) * length)
        blocks = [beside[core][0], right[mine], left[mine], others[mine]]
        forward[core, :width, :width] = own
        forward[core, :length, width : width + 3 * near + far] = np.concatenate(blocks, axis=1)
        inward[core, :near, :length] = cosecant(total, cells + (2 * core - 1) * length, beside[1 - core][1])
        for away, at in start.items():
            nodes = {1: right_nodes, chips - 1: left_nodes}.get(away, far_nodes)
            target = cells + core * length + away * chip
            inward[core, at : at + nodes.size, :length] = cosecant(total, target, nodes)
        for delta in range(segments):
            target = cells + delta * length
            inward[core, ends + delta, :length] = cosecant(total, target, np.array([length - 1.0]))[0]
            inward[core, ends + segments + delta, :length] = cosecant(total, target, np.array([0.0]))[0]
    pairs = [np.stack([split3(table[core]) for core in range(2)]) for table in (forward, inward)]
    return *pairs, near, far


def series(terms, square):
    value = jnp.full_like(square, terms[-1])
    for term in terms[-2::-1]:
        value = value * square + term
    return value


def pad_lanes(value, width):
    rows, length = value.shape
    if width == length:
        return value
    return jnp.concatenate([value, jnp.zeros((rows, width - length), value.dtype)], axis=1)


def halves(value):
    hi = value.astype(BF16)
    return hi, (value - hi.astype(F32)).astype(BF16)


def step_kernel(
    segments, bands, groups, near, far,
    fields_hbm, east_hbm, north_hbm, cutoff_hbm, damping_hbm, ship_hbm, forward_hbm, inward_hbm, result,
    cells, east, north, cutoff, damping, ship, forward, inward, facts, mix, sines, edge_pack, edge_out, edge_in,
    faces, face_columns, advected, spread, near_part, charges, kept, partial, summed, arrived,
    load_sem, small_sem, halo_send, halo_recv, face_send, face_recv, side_send, side_recv,
    send_sem, recv_sem, pass_send, pass_recv,
):
    channels, rows_dev, length = fields_hbm.shape
    width = advected.shape[2]
    total = segments * length
    lat_count = rows_dev * bands
    start, ends, slots = layout(segments, near, far)
    me, band = lax.axis_index("lon"), lax.axis_index("lat")
    right, left = lax.rem(me + 1, segments), lax.rem(me + segments - 1, segments)
    peers = [lax.rem(me + p, segments) for p in range(1, segments)]
    chips, chip, core = segments // 2, me // 2, lax.rem(me, 2)
    sibling = {"lon": me + 1 - 2 * core}
    partners = [{"lon": 2 * lax.rem(chip + p, chips) + core} for p in range(1, chips)]
    small = [
        pltpu.make_async_copy(cutoff_hbm, cutoff, small_sem.at[0]),
        pltpu.make_async_copy(damping_hbm, damping, small_sem.at[1]),
        pltpu.make_async_copy(ship_hbm, ship, small_sem.at[2]),
        pltpu.make_async_copy(forward_hbm.at[core], forward, small_sem.at[3]),
        pltpu.make_async_copy(inward_hbm.at[core], inward, small_sem.at[4]),
    ]
    body = pl.ds(8, rows_dev)
    loads = [
        pltpu.make_async_copy(fields_hbm, cells.at[:, body], load_sem.at[0]),
        pltpu.make_async_copy(east_hbm, east, load_sem.at[1]),
        pltpu.make_async_copy(north_hbm, north.at[body], load_sem.at[2]),
    ]
    barrier = pltpu.get_barrier_semaphore()
    for peer in peers:
        pl.semaphore_signal(barrier, inc=1, device_id={"lon": peer}, device_id_type=MESH)

    @pl.when(band > 0)
    def _():
        pl.semaphore_signal(barrier, inc=1, device_id={"lat": band - 1}, device_id_type=MESH)

    @pl.when(band < bands - 1)
    def _():
        pl.semaphore_signal(barrier, inc=1, device_id={"lat": band + 1}, device_id_type=MESH)

    for load in small[:3] + loads + small[3:]:
        load.start()

    @pl.when(band == 0)
    def _():
        cells[:, 0:8, :] = jnp.zeros((channels, 8, length), F32)
        north[0:8, :] = jnp.zeros((8, length), F32)

    @pl.when(band == bands - 1)
    def _():
        cells[:, rows_dev + 8 : rows_dev + 16, :] = jnp.zeros((channels, 8, length), F32)

    def sine(k):
        z = jnp.minimum(k, lat_count - k) * (1.0 / lat_count)
        return z * series(SIN, z * z)

    def waves_at(turns):
        part = turns - jnp.floor(turns * (0.5 / total) + 0.5) * (2.0 * total)
        z = part * (1.0 / total)
        square = z * z
        return z * series(SIN, square), series(COS, square)

    for r in range(0, rows_dev, 8):
        row = (band * rows_dev + r + lax.broadcasted_iota(jnp.int32, (8, 128), 0)).astype(F32)
        inverse = 1.0 / sine(row + 0.5)
        facts[0, r : r + 8, :] = jnp.where(row < lat_count - 1, sine(row + 1.0), 0.0) * inverse
        facts[1, r : r + 8, :] = jnp.where(row > 0, sine(row), 0.0) * inverse

    for load in small[:3]:
        load.wait()
    repeat = width // 128

    def wide(value):
        return jnp.concatenate([value] * repeat, axis=1)

    column = lax.broadcasted_iota(jnp.int32, (BLOCK, width), 1)
    place = (me * length + column).astype(F32)
    every = lax.broadcasted_iota(jnp.int32, (BLOCK, lat_count), 1)
    local = lax.broadcasted_iota(jnp.int32, (BLOCK, lat_count), 0)
    slot_row = lax.broadcasted_iota(jnp.int32, (BLOCK, ship.shape[2]), 0)
    for r in range(0, rows_dev, BLOCK):
        here = slice(r, r + BLOCK)
        hit = every == local + (band * rows_dev + r)
        cut = jnp.sum(jnp.where(hit, cutoff[...].astype(F32), 0.0), axis=1, keepdims=True)
        damp = jnp.sum(jnp.where(hit, damping[...], 0.0), axis=1, keepdims=True)
        listed = jnp.zeros((BLOCK, ship.shape[2]), F32)
        for d in range(bands):
            listed = listed + jnp.where(ship[band, d : d + 1, :] == slot_row + r, 1.0, 0.0)
        polar = jnp.sum(listed, axis=1, keepdims=True) > 0.0
        waves = 2.0 * cut + 1.0
        mix[0, here, :] = jnp.broadcast_to(
            jnp.where(polar, damp + (1.0 - damp) * (waves * (1.0 / total)), 1.0), (BLOCK, 128)
        )
        mix[1, here, :] = jnp.broadcast_to(jnp.where(polar, 1.0 - damp, 0.0), (BLOCK, 128))
        mix[2, here, :] = jnp.broadcast_to(waves, (BLOCK, 128))
        sines[0, here, :], sines[1, here, :] = waves_at(waves * place)

    beside = jnp.where(band > 0, 1, 0) + jnp.where(band < bands - 1, 1, 0)
    pl.semaphore_wait(barrier, segments - 1 + beside)

    def halo(source, target, slot, device):
        return pltpu.make_async_remote_copy(
            src_ref=source, dst_ref=target, send_sem=halo_send.at[slot],
            recv_sem=halo_recv.at[slot], device_id=device, device_id_type=MESH,
        )

    up = {"lat": jnp.minimum(band + 1, bands - 1)}
    down = {"lat": jnp.maximum(band - 1, 0)}
    first, last = pl.ds(0, 1), pl.ds(rows_dev - 1, 1)
    northward = [
        halo(fields_hbm.at[:, last], cells.at[:, pl.ds(7, 1)], 0, up),
        halo(north_hbm.at[last], north.at[pl.ds(7, 1)], 1, up),
    ]
    southward = halo(fields_hbm.at[:, first], cells.at[:, pl.ds(rows_dev + 8, 1)], 2, down)

    @pl.when(band < bands - 1)
    def _():
        for copy in northward:
            copy.start()

    @pl.when(band > 0)
    def _():
        southward.start()

    for load in loads:
        load.wait()
    lane = lax.broadcasted_iota(jnp.int32, (BLOCK, 128), 1)
    for r in range(0, rows_dev, BLOCK):
        packed = jnp.zeros((BLOCK, 128), F32)
        for c in range(channels):
            packed = jnp.where(lane == c, cells[c, 8 + r : 8 + r + BLOCK, 0:1], packed)
            packed = jnp.where(lane == 8 + c, cells[c, 8 + r : 8 + r + BLOCK, length - 1 : length], packed)
        edge_pack[r : r + BLOCK, :] = jnp.where(
            lane == 8 + channels, east[r : r + BLOCK, length - 1 : length], packed
        )
    edge_out[...] = edge_pack[...].T[0:16, :]
    sideways = [
        halo(edge_out.at[pl.ds(8, 8)], edge_in.at[pl.ds(8, 8)], 3, {"lon": right}),
        halo(edge_out.at[pl.ds(0, 8)], edge_in.at[pl.ds(0, 8)], 4, {"lon": left}),
    ]
    for copy in sideways:
        copy.start()
    small[3].wait()

    lines = [channels * BLOCK * len(group) for group in groups]

    def advect(k):
        for b, r in enumerate(groups[k]):
            here = slice(r, r + BLOCK)
            ce = jnp.where(column == length - 1, 0.0, pad_lanes(east[here, :], width))
            cw = pltpu.roll(ce, 1, 1)
            cn = pad_lanes(north[8 + r : 8 + r + BLOCK, :], width) * wide(facts[0, here, :])
            cs = pad_lanes(north[7 + r : 7 + r + BLOCK, :], width) * wide(facts[1, here, :])
            at_east, at_west = jnp.minimum(ce, 0.0), jnp.maximum(cw, 0.0)
            at_north, at_south = jnp.minimum(cn, 0.0), jnp.maximum(cs, 0.0)
            at_home = 1.0 - (ce - at_east) + (cw - at_west) - (cn - at_north) + (cs - at_south)
            sin, cos = sines[0, here, :], sines[1, here, :]
            for c in range(channels):
                field = pad_lanes(cells[c, 8 + r : 8 + r + BLOCK, :], width)
                upper = pad_lanes(cells[c, 9 + r : 9 + r + BLOCK, :], width)
                lower = pad_lanes(cells[c, 7 + r : 7 + r + BLOCK, :], width)
                ahead, behind = pltpu.roll(field, width - 1, 1), pltpu.roll(field, 1, 1)
                value = at_home * field - at_east * ahead + at_west * behind - at_north * upper + at_south * lower
                advected[c, here, :] = value
                line = (c * len(groups[k]) + b) * BLOCK
                for q, wave in enumerate((sin, cos)):
                    hi, lo = halves(value * wave)
                    spread[k][q * lines[k] + line : q * lines[k] + line + BLOCK, 0:width] = hi
                    spread[k][q * lines[k] + line : q * lines[k] + line + BLOCK, width : 2 * width] = lo

    def remote(source, target, send, recv, device):
        return pltpu.make_async_remote_copy(
            src_ref=source, dst_ref=target, send_sem=send, recv_sem=recv, device_id=device, device_id_type=MESH
        )

    def matmul(k, columns):
        return jnp.dot(
            spread[k][...], forward[0 : 2 * width, columns], preferred_element_type=F32
        ) + jnp.dot(spread[k][:, 0:width], forward[2 * width : 3 * width, columns], preferred_element_type=F32)

    inner_columns, charge_columns = slice(0, width), slice(width, forward.shape[1])
    to_side, to_chips, passed, around = {}, {}, {}, []

    def charge(k, product):
        sine_part, cosine_part = (product[q * lines[k] : (q + 1) * lines[k], :].T for q in range(2))
        charges[k][0:near, :] = sine_part[0:near, :]
        charges[k][near : 2 * near, :] = cosine_part[0:near, :]
        sine_part, cosine_part = (part[near : 3 * near + far, :] for part in (sine_part, cosine_part))
        charges[k][2 * near :, :] = jnp.where(core == 0, cosine_part, sine_part)
        kept[k][...] = jnp.where(core == 0, sine_part, cosine_part)

    def stay(k):
        near_part[k][...] = matmul(k, inner_columns)

    def both(k):
        product = matmul(k, slice(0, forward.shape[1]))
        charge(k, product[:, width:])
        near_part[k][...] = product[:, 0:width]

    def to_sibling(k):
        to_side[k] = remote(charges[k], partial[k], side_send.at[k], side_recv.at[k], sibling)
        to_side[k].start()

    def spread_out(k):
        to_side[k].wait_recv()
        summed[k][...] = partial[k][2 * near :, :] + kept[k][...]
        to_chips[k] = []
        for p, partner in enumerate(partners):
            away = p + 1
            size = near if away in (1, chips - 1) else far
            at = {1: 0, chips - 1: near}.get(away, 2 * near)
            copy = remote(
                summed[k].at[pl.ds(at, size)], arrived[k].at[core, pl.ds(start[away] - near, size)],
                send_sem.at[k, p], recv_sem.at[k, p], partner,
            )
            copy.start()
            to_chips[k].append(copy)

    def hand_on(k):
        for copy in to_chips[k]:
            copy.wait_recv()
        passed[k] = remote(arrived[k].at[core], arrived[k].at[core], pass_send.at[k], pass_recv.at[k], sibling)
        passed[k].start()

    def meet():
        for copy in sideways:
            copy.wait()
        courant, courant_left = edge_out[8 + channels : 9 + channels, :], edge_in[8 + channels : 9 + channels, :]
        faces[0] = courant * jnp.where(courant > 0, edge_out[8:16, :], edge_in[0:8, :])
        faces[segments] = courant_left * jnp.where(courant_left > 0, edge_in[8:16, :], edge_out[0:8, :])
        for p, peer in reversed(list(enumerate(peers))):
            copy = remote(faces.at[0], faces.at[p + 1], face_send.at[p], face_recv.at[p], {"lon": peer})
            copy.start()
            around.append(copy)

    count = len(groups)
    advect(0)
    for k in range(count):
        if k == count - 3:

            @pl.when(band < bands - 1)
            def _():
                for copy in northward:
                    copy.wait_send()
                southward.wait_recv()

            @pl.when(band > 0)
            def _():
                southward.wait_send()
                for copy in northward:
                    copy.wait_recv()

        if k < count - 2:
            both(k)
        else:
            charge(k, matmul(k, charge_columns))
        if k < count - 1:
            advect(k + 1)
        to_sibling(k)
        if k > 0:
            spread_out(k - 1)
        if k == count - 4:
            meet()
    stay(count - 2)
    spread_out(count - 1)
    hand_on(0)
    small[4].wait()
    stay(count - 1)
    for k in range(1, count - 2):
        hand_on(k)
    face_columns[:, 0:16] = jnp.concatenate([faces[segments], faces[0]], axis=0).T

    delta = lax.broadcasted_iota(jnp.int32, (2 * segments, rows_dev), 0)
    owner = me - jnp.where(delta < segments, delta, delta - segments)
    owner = jnp.where(owner < 0, owner + segments, owner) * length + jnp.where(delta < segments, length - 1, 0)
    end_waves = waves_at(mix[2].T[0 : 2 * segments, :] * owner.astype(F32))
    for copy in around:
        copy.wait_recv()
    end_charges = []
    for c in range(channels):
        face = faces[0:segments, c, :]
        face = jnp.concatenate([-face, face[1:segments], face[0:1]], axis=0)
        end_charges.append([face * wave for wave in end_waves])

    def signs(k):
        slot = lax.broadcasted_iota(jnp.int32, (slots, lines[k]), 0)
        bound = jnp.where(slot < ends, 3 * near + (chip - 1) * far, ends + me + 1)
        bound = jnp.where(slot < ends + segments, bound, ends + segments + me + 1)
        bound = jnp.where(slot < 3 * near, jnp.where(chip >= chips - 1, 3 * near, 0), bound)
        bound = jnp.where(slot < 2 * near, jnp.where(chip >= 1, 2 * near, 0), bound)
        return jnp.where((slot < bound) | (slot < near), 1.0, -1.0)

    def finish(k):
        sign, sums = signs(k), []
        spare = jnp.zeros((slots - ends - 2 * segments, lines[k]), F32)
        for q in range(2):
            ended = jnp.concatenate([end[q][:, r : r + BLOCK] for end in end_charges for r in groups[k]], axis=1)
            gathered = jnp.concatenate([partial[k][q * near : (q + 1) * near, :], arrived[k][q], ended, spare], axis=0)
            hi, lo = halves(gathered * sign)
            sums.append(jnp.dot(jnp.concatenate([hi, lo, hi], axis=0).T, inward[...], preferred_element_type=F32))
        for b, r in enumerate(groups[k]):
            here = slice(r, r + BLOCK)
            keep, share = wide(mix[0, here, :]), wide(mix[1, here, :])
            sin, cos = sines[0, here, :] * share, sines[1, here, :] * share
            for c in range(channels):
                line = (c * len(groups[k]) + b) * BLOCK
                u = near_part[k][line : line + BLOCK, :] + sums[0][line : line + BLOCK, :]
                v = near_part[k][lines[k] + line : lines[k] + line + BLOCK, :] + sums[1][line : line + BLOCK, :]
                value = advected[c, here, :]
                value = jnp.where(column == 0, value + face_columns[here, c : c + 1], value)
                value = jnp.where(column == length - 1, value - face_columns[here, 8 + c : 9 + c], value)
                value = keep * value + (sin * v - cos * u)
                result[c, here, :] = value[:, 0:length]

    for k in range(count):
        if k in (1, 3):
            hand_on(count - 2 + k // 2)
        passed[k].wait_recv()
        finish(k)
    for k in range(len(groups)):
        for copy in [to_side[k], *to_chips[k], passed[k]]:
            copy.wait_send()
    for copy in around:
        copy.wait_send()


def per_device(fields, east_courant, north_courant, cutoff, damping, ship_rows):
    channels, rows_dev, length = fields.shape
    segments, bands = lax.axis_size("lon"), lax.axis_size("lat")
    width = ceil_to(length, 128)
    blocks = rows_dev // BLOCK
    outer = blocks // 5
    rows = [BLOCK * b for b in range(blocks)]
    inner = [rows[at : min(at + outer, blocks - outer)] for at in range(outer, blocks - outer, outer)]
    groups = inner + [rows[:outer], rows[-outer:]]
    lines = [channels * BLOCK * len(group) for group in groups]
    forward, inward, near, far = tables(segments, length, width)
    assert channels < 8 and outer > 0 and rows_dev % BLOCK == 0 and segments % 2 == 0
    _, ends, _ = layout(segments, near, far)
    semaphores = pltpu.SemaphoreType.DMA((len(groups), segments // 2 - 1))
    semaphore = pltpu.SemaphoreType.DMA((len(groups),))
    whole = pl.BlockSpec(memory_space=pl.ANY)
    return pl.pallas_call(
        functools.partial(step_kernel, segments, bands, groups, near, far),
        out_shape=pltpu.VMEM(fields.shape, F32),
        in_specs=[whole] * 8,
        out_specs=pl.BlockSpec(memory_space=pltpu.VMEM),
        scratch_shapes=[
            pltpu.VMEM((channels, rows_dev + 16, length), F32),
            pltpu.VMEM((rows_dev, length), F32),
            pltpu.VMEM((rows_dev + 16, length), F32),
            pltpu.VMEM((1, cutoff.shape[0]), jnp.int32),
            pltpu.VMEM((1, damping.shape[0]), F32),
            pltpu.VMEM(ship_rows.shape, jnp.int32),
            pltpu.VMEM(forward.shape[1:], BF16),
            pltpu.VMEM(inward.shape[1:], BF16),
            pltpu.VMEM((2, rows_dev, 128), F32),
            pltpu.VMEM((3, rows_dev, 128), F32),
            pltpu.VMEM((2, rows_dev, width), F32),
            pltpu.VMEM((rows_dev, 128), F32),
            pltpu.VMEM((16, rows_dev), F32),
            pltpu.VMEM((16, rows_dev), F32),
            pltpu.VMEM((segments + 1, 8, rows_dev), F32),
            pltpu.VMEM((rows_dev, 128), F32),
            pltpu.VMEM((channels, rows_dev, width), F32),
            [pltpu.VMEM((2 * count, 2 * width), BF16) for count in lines],
            [pltpu.VMEM((2 * count, width), F32) for count in lines],
            [pltpu.VMEM((4 * near + far, count), F32) for count in lines],
            [pltpu.VMEM((2 * near + far, count), F32) for count in lines],
            [pltpu.VMEM((4 * near + far, count), F32) for count in lines],
            [pltpu.VMEM((2 * near + far, count), F32) for count in lines],
            [pltpu.VMEM((2, ends - near, count), F32) for count in lines],
            pltpu.SemaphoreType.DMA((3,)),
            pltpu.SemaphoreType.DMA((5,)),
            pltpu.SemaphoreType.DMA((5,)),
            pltpu.SemaphoreType.DMA((5,)),
            pltpu.SemaphoreType.DMA((segments - 1,)),
            pltpu.SemaphoreType.DMA((segments - 1,)),
            semaphore, semaphore, semaphores, semaphores, semaphore, semaphore,
        ],
        compiler_params=pltpu.CompilerParams(
            collective_id=0, has_side_effects=True, vmem_limit_bytes=36 * 1024 * 1024
        ),
    )(
        *(
            pltpu.with_memory_space_constraint(value, pltpu.HBM)
            for value in (
                fields, east_courant, north_courant, cutoff[None, :], damping[None, :], ship_rows,
                jnp.asarray(forward), jnp.asarray(inward),
            )
        )
    )


def solution(mesh):
    placed = (P(None, "lat", "lon"), P("lat", "lon"), P("lat", "lon"), P(), P(), P())
    return jax.shard_map(
        per_device, mesh=mesh, in_specs=placed, out_specs=P(None, "lat", "lon"), check_vma=False
    )
```
